32 devices in a mesh: lon: 8 (over z, x), lat: 4 (over y, core).
Axes of the slice: x: 2, y: 2, z: 4, core: 2. Of those that a mesh axis runs over, the one named last changes fastest.
Arguments:
- kappa_east: float32 [64, 1024], P('lat', 'lon'), may hold values from 0.02 to 0.2
- kappa_north: float32 [64, 1024], P('lat', 'lon'), may hold values from 0.02 to 0.2
- depth: int32 [64, 1024], P('lat', 'lon'), may hold values from 0 to 75
- sigma: float32 [151], replicated, may hold values from 0.3 to 3
- obs_precision: float32 [151], replicated, may hold values from 0.5 to 4
- obs_tile: int32 [4096, 1], P(('lon', 'lat')), may hold values from 0 to 7; in each aligned block of 128 rows (0 to 127, 128 to 255, ...) at most 32 rows name the same one
- obs_col: int32 [4096], P(('lon', 'lat')), may hold values from 0 to 127
- obs_lat: int32 [4096], P(('lon', 'lat')), may hold values from 0 to 15
- innovation: float32 [151, 4096], P(None, ('lon', 'lat')), may hold values from -6 to 6
Outputs:
- increment: float32 [151, 64, 1024], P(None, 'lat', 'lon')
- residual: float32 [151, 64, 1024], P(None, 'lat', 'lon')
The draws below stay inside these ranges and needn't reach their ends.
Inputs may be any that keep to these rules, and one draw needn't show every extreme that they name: `obs_tile`: among the 128 profiles listed on one device, no longitude tile is named by more than 32, a bound that some block reaches.
All inputs are finite; a program needn't handle non-finite values.
Results may differ from the reference program's by a relative error of at most 0.00013.
Values sent between devices are 32-bit elements; how exact they have to be, the bound alone decides.
A program may use at most 128 MiB of HBM per device.

```python
import math
import jax
import jax.numpy as jnp
import numpy as np

NZ = 75
CX = 128
CY = 16
OBS_DEV = 128
ITERS = 2
CH = 151
NX = 1024
NY = 64
NOBS = 4096
CAP = 32
N_LON = 8
N_LAT = 4


def set_ends(values, own_key, least, largest):
    longest = values.shape.index(max(values.shape))
    spots = []
    for shift in (0, 1):
        where = [jax.random.randint(jax.random.fold_in(own_key, axis), (), 0, length) for axis, length in enumerate(values.shape)]
        where[longest] = (where[longest] + shift) % values.shape[longest]
        spots.append(tuple(where))
    return values.at[spots[0]].set(least).at[spots[1]].set(largest)


def shard_levels(key, shape, shards, smallest, top_value):
    level, own = 1.0, jax.random.fold_in(key, 6)
    for dim, shards_of in shards:
        draws = jnp.exp(jax.random.uniform(jax.random.fold_in(own, dim), (shards_of,), jnp.float32, smallest / len(shards), top_value / len(shards)))
        level = level * jnp.repeat(draws, shape[dim] // shards_of).reshape([-1 if axis == dim else 1 for axis in range(len(shape))])
    return level


def routed_block(key, own, number, rows, amount, top, limit, skew):
    ranking = jax.random.permutation(key, amount)
    heavy_load, common = load_shares(amount, rows * top, limit, skew, True), load_shares(amount, rows * top, limit, skew, False)
    places = jnp.arange(amount)

    def named(lengths, offset_by):
        used = int((lengths > 0).sum())
        fixed = max(1, used // 4)
        shifted = fixed + (places - fixed + offset_by * (used - fixed)) % max(1, amount - fixed)
        return jnp.zeros((amount,), jnp.int32).at[ranking[jnp.where(places < fixed, places, shifted)]].set(jnp.asarray(lengths, jnp.int32))

    lengths = jnp.where(number % 4 == 0, named(heavy_load, number // 4), named(common, number - number // 4 - 1))
    mixed = jax.random.permutation(jax.random.fold_in(own, 3), amount)
    donor, receiver = mixed[0:amount // 2 * 2:2], mixed[1:amount // 2 * 2:2]
    room = jnp.minimum(lengths[donor] - 1, limit - lengths[receiver]) // 2
    room = jnp.where((donor == ranking[0]) | (receiver == ranking[0]) | (lengths[receiver] == 0), 0, jnp.maximum(room, 0))
    shifted = jax.random.randint(jax.random.fold_in(own, 4), (amount // 2,), 0, 1 << 20) % (room + 1)
    lengths = lengths.at[donor].add(-shifted).at[receiver].add(shifted)
    labels = jnp.searchsorted(jnp.cumsum(lengths), jnp.arange(rows * top), side="right").astype(jnp.int32)
    listing = labels.reshape(top, rows).T
    listing = listing[jax.random.permutation(jax.random.fold_in(own, 1), rows)]
    offset_by = jax.random.randint(jax.random.fold_in(own, 2), (rows, 1), 0, top)
    return jnp.take_along_axis(listing, (jnp.arange(top)[None, :] + offset_by) % top, axis=1)


def load_shares(count, total, limit, skew, full):
    weights = [(1 << 20) // math.isqrt(standing ** skew) + 1 for standing in range(1, count + 1)]
    largest = limit if full else min(limit, max(-(-total // count), total * weights[0] // sum(weights)))
    least = 1 if total - largest >= count - 1 else 0
    holding, surplus = [largest] + [least] * (count - 1), total - largest - least * (count - 1)
    while surplus > 0:
        movable = [i for i in range(1, count) if holding[i] < largest] or [i for i in range(1, count) if holding[i] < limit]
        whole, budget = sum([weights[i] for i in movable]), surplus
        for i in movable:
            more = min(limit - holding[i], max(1, budget * weights[i] // whole), surplus)
            holding[i] = holding[i] + more
            surplus = surplus - more
    return np.array(holding)


def scatter_about(stream_key, shape, spread, reach, shards=(), kind=jnp.bfloat16):
    array = spread * jax.random.normal(stream_key, shape, jnp.float32)
    if shards:
        array = array * shard_levels(stream_key, shape, shards, -0.22, 0.18)
    return jnp.clip(array, -reach, reach).astype(kind)


def setup_inputs(seed: int = 0) -> dict:
    seeds = jax.random.split(jax.random.key(seed), 10)
    kappa_east = jnp.clip(0.02 + 0.18 * jax.random.uniform(seeds[0], (NY, NX), jnp.float32) ** shard_levels(seeds[0], (NY, NX), ((0, 4), (1, 8)), -0.2, 0.2), 0.02, 0.2)
    kappa_north = jnp.clip(0.02 + 0.18 * jax.random.uniform(seeds[1], (NY, NX), jnp.float32) ** shard_levels(seeds[1], (NY, NX), ((0, 4), (1, 8)), -0.2, 0.2), 0.02, 0.2)
    depth = set_ends(jax.random.randint(seeds[2], (NY, NX), 0, NZ + 1), jax.random.fold_in(seeds[2], 1), 0, NZ).astype(jnp.int32)
    sigma = jnp.clip(jnp.exp(jax.random.uniform(seeds[3], (CH,), jnp.float32, math.log(0.3), math.log(3.0))), 0.3, 3.0)
    obs_precision = jnp.clip(jnp.exp(jax.random.uniform(seeds[4], (CH,), jnp.float32, math.log(0.5), math.log(4.0))), 0.5, 4.0)
    obs_tile_keys = jax.random.split(jax.random.fold_in(seeds[5], 1), NOBS // OBS_DEV)
    obs_tile_turns = jax.random.permutation(jax.random.fold_in(seeds[5], 3), NOBS // OBS_DEV)
    obs_tile = jax.vmap(lambda own, number: routed_block(jax.random.fold_in(seeds[5], 2), own, number, OBS_DEV, N_LON, 1, CAP, 0))(obs_tile_keys, obs_tile_turns).reshape((NOBS, 1))
    obs_col = set_ends(jax.random.randint(seeds[6], (NOBS,), 0, CX), jax.random.fold_in(seeds[6], 1), 0, CX - 1).astype(jnp.int32)
    obs_lat = set_ends(jax.random.randint(seeds[7], (NOBS,), 0, CY), jax.random.fold_in(seeds[7], 1), 0, CY - 1).astype(jnp.int32)
    innovation = scatter_about(seeds[8], (CH, NOBS), 1.0, 6.0, ((1, 32),), jnp.float32)
    return dict(kappa_east=kappa_east, kappa_north=kappa_north, depth=depth, sigma=sigma, obs_precision=obs_precision, obs_tile=obs_tile, obs_col=obs_col, obs_lat=obs_lat, innovation=innovation)


def smooth_once(v, face_east, face_north):
    east = jnp.roll(v, -1, 2)
    west = jnp.roll(v, 1, 2)
    north = jnp.roll(v, -1, 1)
    south = jnp.roll(v, 1, 1)
    out = v + face_east * (east - v) + jnp.roll(face_east, 1, 2) * (west - v)
    return out + face_north * (north - v) + jnp.roll(face_north, 1, 1) * (south - v)


def smooth_five(v, face_east, face_north):
    for step in range(5):
        v = smooth_once(v, face_east, face_north)
    return v


def reference(kappa_east, kappa_north, depth, sigma, obs_precision, obs_tile, obs_col, obs_lat, innovation):
    levels = jnp.arange(CH, dtype=jnp.int32)
    level_of = jnp.where(levels < 2 * NZ, levels % NZ, 0).astype(jnp.int32)
    wet = (depth[None, :, :] > level_of[:, None, None]).astype(jnp.float32)
    keep_row = (jnp.arange(NY, dtype=jnp.int32) < NY - 1).astype(jnp.float32)[:, None]
    face_east = kappa_east[None] * wet * jnp.roll(wet, -1, 2)
    face_north = (kappa_north * keep_row)[None] * wet * jnp.roll(wet, -1, 1)
    order = jnp.arange(NOBS, dtype=jnp.int32)
    obs_row = ((order // OBS_DEV) % N_LAT) * CY + obs_lat
    obs_lon = (obs_tile[:, 0] * CX + obs_col).astype(jnp.int32)
    scale = sigma[:, None, None]
    weight = obs_precision[:, None]

    def forward_obs(u):
        return (u * wet)[:, obs_row, obs_lon]

    def adjoint_obs(w):
        cells = jnp.zeros((CH, NY, NX), jnp.float32).at[:, obs_row, obs_lon].add(w)
        return cells * wet

    def hessian(p):
        u = scale * smooth_five(p, face_east, face_north)
        w = weight * forward_obs(u)
        return p + smooth_five(scale * adjoint_obs(w), face_east, face_north)

    rhs = smooth_five(scale * adjoint_obs(weight * innovation), face_east, face_north)
    increment = jnp.zeros_like(rhs)
    residual = rhs
    direction = rhs
    norm_now = jnp.sum(residual * residual)
    for step in range(ITERS):
        image = hessian(direction)
        alpha = norm_now / jnp.sum(direction * image)
        increment = increment + alpha * direction
        residual = residual - alpha * image
        norm_next = jnp.sum(residual * residual)
        direction = residual + (norm_next / norm_now) * direction
        norm_now = norm_next
    return increment, residual
```

```python
import functools

import jax
import jax.numpy as jnp
from jax import lax
from jax.experimental import pallas as pl
from jax.experimental.pallas import tpu as pltpu
from jax.sharding import PartitionSpec as P

MESH = pl.DeviceIdType.MESH
SUB = 8
PACK = 4
PASSES = 5
STAGES = 5
STRIDE = 32
OWN = 2 * PASSES
EAST = 16


def split3(x):
    high = x.astype(jnp.bfloat16)
    left = x - high.astype(jnp.float32)
    middle = left.astype(jnp.bfloat16)
    low = (left - middle.astype(jnp.float32)).astype(jnp.bfloat16)
    return high, middle, low


def place_of(row, rows):
    starts = [0, PASSES, 2 * PASSES, rows, rows + PASSES]
    a = max(i for i, s in enumerate(starts) if row >= s)
    return a, row - starts[a]


def main_kernel(
    tiles,
    bands,
    cap,
    total,
    data,
    tile_row,
    tile_col,
    maps,
    coef,
    v_out,
    c_out,
    pay,
    rcv,
    parts,
    table,
    near,
    ext,
    strip,
    base,
    f,
    fe,
    fn,
    res,
    gain,
    hs,
    hn,
    pw,
    pe,
    pk,
    mom,
    red,
    red_lat,
    red_lon,
    obs_send,
    obs_recv,
    map_send,
    map_recv,
    own_sem,
    halo_send,
    halo_recv,
    sum_send,
    sum_recv,
):
    lon, lat = lax.axis_index("lon"), lax.axis_index("lat")
    rows, lanes = maps.shape[1], maps.shape[2]
    quads = f.shape[0]
    deep = rows + 2 * PASSES
    last = rows + PASSES
    has_s, has_n = lat > 0, lat < bands - 1

    def at(dl, db):
        return lax.rem(lon + dl + tiles, tiles), lax.rem(lat + db + bands, bands)

    beside = [(lon, lax.rem(lat + k, bands)) for k in range(1, bands)]
    along = [(lax.rem(lon + k, tiles), lat) for k in range(1, tiles)]
    ways = [(0, -1), (0, 1), (-1, 0), (1, 0), (-1, -1), (1, -1), (-1, 1), (1, 1)]
    there = {-1: has_s, 0: None, 1: has_n}

    def only(cond, body):
        if cond is None:
            body()
        else:
            pl.when(cond)(body)

    barrier = pltpu.get_barrier_semaphore()

    def greet(peer):
        pl.semaphore_signal(barrier, inc=1, device_id=peer, device_id_type=MESH)

    for peer in beside + along:
        greet(peer)
    for dl, db in ways[4:]:
        only(there[db], functools.partial(greet, at(dl, db)))

    def remote(src, dst, send, recv, peer):
        return pltpu.make_async_remote_copy(
            src_ref=src,
            dst_ref=dst,
            send_sem=send,
            recv_sem=recv,
            device_id=peer,
            device_id_type=MESH,
        )

    listed = tile_row.shape[1]
    slots = tiles * cap
    same = tile_col[...] == tile_row[...]
    earlier = lax.broadcasted_iota(jnp.int32, (listed, listed), 0) < lax.broadcasted_iota(
        jnp.int32, (listed, listed), 1
    )
    rank = jnp.sum(jnp.where(same & earlier, 1.0, 0.0), 0, keepdims=True)
    slot = tile_row[...] * cap + rank.astype(jnp.int32)
    chosen = lax.broadcasted_iota(jnp.int32, (slots, listed), 0) == slot
    chosen = jnp.where(chosen, 1.0, 0.0).astype(jnp.bfloat16)
    width = data.shape[0]
    packed = jnp.zeros((slots, width), jnp.float32)
    for part in split3(data[...]):
        packed = packed + lax.dot_general(
            chosen, part, (((1,), (1,)), ((), ())), preferred_element_type=jnp.float32
        )
    pay[...] = packed.reshape(tiles, cap, width)

    diagonal = jnp.where(has_s, 2, 0) + jnp.where(has_n, 2, 0)
    pl.semaphore_wait(barrier, len(beside) + len(along) + diagonal)

    def slot_of(dl, db):
        return (dl + 1) * 3 + db + 1

    def map_copy(d):
        dl, db = ways[d]
        return remote(
            maps, near.at[slot_of(-dl, -db)], map_send.at[d], map_recv.at[d], at(dl, db)
        )

    for d in (4, 5, 6, 7, 2, 3, 0, 1):
        only(there[ways[d][1]], lambda d=d: map_copy(d).start())
    obs = []
    for k, peer in enumerate(along):
        copy = remote(pay.at[peer[0]], rcv.at[lon], obs_send.at[k], obs_recv.at[k], peer)
        copy.start()
        obs.append(copy)
    own = pltpu.make_async_copy(pay.at[lon], rcv.at[lon], own_sem)
    own.start()

    zero = jnp.zeros((SUB, lanes), jnp.float32)
    nothing = jnp.zeros(maps.shape, jnp.float32)
    near[slot_of(0, 0)] = maps[...]
    for dl in (-1, 0, 1):

        @pl.when(jnp.logical_not(has_s))
        def _(dl=dl):
            near[slot_of(dl, -1)] = nothing

        @pl.when(jnp.logical_not(has_n))
        def _(dl=dl):
            near[slot_of(dl, 1)] = nothing

    @pl.when(jnp.logical_not(has_s))
    def _():
        hs[...] = jnp.zeros(hs.shape, jnp.float32)
        pw[:, :, 0] = jnp.zeros(pw.shape[:2] + pw.shape[3:], jnp.float32)
        pe[:, :, 0] = jnp.zeros(pe.shape[:2] + pe.shape[3:], jnp.float32)

    @pl.when(jnp.logical_not(has_n))
    def _():
        hn[...] = jnp.zeros(hn.shape, jnp.float32)
        pw[:, :, 4] = jnp.zeros(pw.shape[:2] + pw.shape[3:], jnp.float32)
        pe[:, :, 4] = jnp.zeros(pe.shape[:2] + pe.shape[3:], jnp.float32)

    for i in range(STAGES):
        mom[i] = zero
    red[...] = zero
    ext[...] = jnp.zeros(ext.shape, jnp.float32)
    strip[...] = jnp.zeros(strip.shape, jnp.float32)

    for d in range(8):
        dl, db = ways[d]
        only(there[-db], lambda d=d: map_copy(d).wait_recv())
    for d in range(8):
        only(there[ways[d][1]], lambda d=d: map_copy(d).wait_send())

    for m in range(3):
        for side in range(3):
            ext[m, side, 0:PASSES] = near[3 * side, m, rows - PASSES : rows]
            ext[m, side, PASSES:last] = near[3 * side + 1, m]
            ext[m, side, last:deep] = near[3 * side + 2, m, 0:PASSES]
    padded = -(-deep // SUB) * SUB
    lane = lax.broadcasted_iota(jnp.int32, (padded, lanes), 1)
    part_of, within = lane // STRIDE, lane % STRIDE
    for m in range(3):
        west, mid, east = (ext[m, side, 0:padded] for side in range(3))
        out = jnp.zeros((padded, lanes), jnp.float32)
        for k in range(PACK):
            here, start = part_of == k, STRIDE * k
            pieces = (
                (west, lanes - PASSES, 0, PASSES),
                (mid, 0, PASSES, OWN),
                (mid, lanes - OWN, EAST, OWN),
                (east, 0, EAST + OWN, PASSES),
            )
            for source, column, first, count in pieces:
                moved = pltpu.roll(source, (start + first - column) % lanes, 1)
                inside = here & (within >= first) & (within < first + count)
                out = jnp.where(inside, moved, out)
        strip[m, 0:padded] = out
    for i, (ke, kn, depth, above) in enumerate(
        (
            (ext[0, 1, 0:padded], ext[1, 1, 0:padded], ext[2, 1, 0:padded], ext[2, 1, 1 : padded + 1]),
            (strip[0, 0:padded], strip[1, 0:padded], strip[2, 0:padded], strip[2, 1 : padded + 1]),
        )
    ):
        base[i, 0] = ke
        base[i, 1] = jnp.minimum(depth, pltpu.roll(depth, lanes - 1, 1))
        base[i, 2] = kn
        base[i, 3] = jnp.minimum(depth, above)

    cell = lax.broadcasted_iota(jnp.int32, (SUB, lanes), 1)

    def spread(group, which):
        return jnp.broadcast_to(coef[group, :, which : which + 1], (SUB, lanes))

    def build(n, carry):
        q = n // PACK
        k = n % PACK
        level = spread(n, 0)
        for r in range(deep):
            line = [jnp.broadcast_to(base[0, i, r : r + 1, :], (SUB, lanes)) for i in range(4)]
            fe[q, 1 + k, r] = jnp.where(line[1] > level, line[0], 0.0)
            fn[q, 1 + k, r] = jnp.where(line[3] > level, line[2], 0.0)
        return carry

    lax.fori_loop(0, quads * PACK, build, 0)

    def build_strip(q, carry):
        level = spread(q * PACK, 0)
        for k in range(1, PACK):
            level = jnp.where(cell >= STRIDE * k, spread(q * PACK + k, 0), level)
        for r in range(deep):
            line = [jnp.broadcast_to(base[1, i, r : r + 1, :], (SUB, lanes)) for i in range(4)]
            fe[q, 0, r] = jnp.where(line[1] > level, line[0], 0.0)
            fn[q, 0, r] = jnp.where(line[3] > level, line[2], 0.0)
        return carry

    lax.fori_loop(0, quads, build_strip, 0)

    own.wait()
    for copy in obs:
        copy.wait()
    arrived = rcv[...].reshape(slots, width)
    for i, part in enumerate(split3(arrived.T[: parts.shape[1]])):
        parts[i] = part
    columns = arrived[:, total + 1 : total + 2]
    lines = arrived[:, total + 2 : total + 3]
    places = lax.broadcasted_iota(jnp.int32, (slots, lanes), 1).astype(jnp.float32)
    table[...] = jnp.where(columns == places, 1.0, 0.0)

    def scatter(r, carry):
        at_row = jnp.where(lines == r.astype(jnp.float32), table[...], 0.0).astype(jnp.bfloat16)
        cells = jnp.zeros((parts.shape[1], lanes), jnp.float32)
        for i in range(3):
            cells = cells + jnp.dot(parts[i], at_row, preferred_element_type=jnp.float32)
        count = jnp.broadcast_to(cells[total : total + 1], (SUB, lanes))
        depth = jnp.broadcast_to(maps[2, pl.ds(r, 1), :], (SUB, lanes))
        for n in range(quads * PACK):
            wet = depth > spread(n, 0)
            block = cells[SUB * n : SUB * n + SUB]
            f[n // PACK, 1 + n % PACK, PASSES + r] = jnp.where(wet, spread(n, 1) * block, 0.0)
            gain[n // PACK, n % PACK, r] = jnp.where(wet, spread(n, 2) * count, 0.0)
        return carry

    lax.fori_loop(0, rows, scatter, 0)

    group_of, inside = cell // STRIDE, cell % STRIDE

    def strip_row(q, r):
        z = zero
        for k in range(PACK):
            moved = pltpu.roll(f[q, 1 + k, r], (STRIDE * k + OWN) % lanes, 1)
            z = moved if k == 0 else jnp.where(group_of == k, moved, z)
        x = jnp.where(inside < EAST, pltpu.roll(z, lanes - PASSES, 1), pltpu.roll(z, EAST, 1))
        return z, x

    def halo(par, q, d):
        dl, db = ways[d]
        send, recv = halo_send.at[par, q, d], halo_recv.at[par, q, d]
        to_lat = {-1: rows + PASSES, 1: 0}
        if dl == 0:
            first = PASSES if db < 0 else last - PASSES
            src = f.at[q, pl.ds(1, PACK), pl.ds(first, PASSES)]
            dst = (hn if db < 0 else hs).at[par, q]
        else:
            pack, target = (0, pe) if dl < 0 else (1, pw)
            if db == 0:
                src = pk.at[q, pack]
                dst = target.at[par, q, pl.ds(1, 3)]
            else:
                src = pk.at[q, pack, pl.ds(0 if db < 0 else 2, 1)]
                dst = target.at[par, q, pl.ds(4 if db < 0 else 0, 1)]
        return remote(src, dst, send, recv, at(dl, db))

    def emit(par, q):
        for d in (0, 1):
            only(there[ways[d][1]], lambda d=d: halo(par, q, d).start())
        packs = {}
        for r in range(PASSES, last):
            z, x = strip_row(q, r)
            f[q, 0, r] = x
            a, j = place_of(r, rows)
            for side, first in ((0, OWN), (1, PASSES)):
                moved = pltpu.roll(z, (PASSES * j - first) % lanes, 1)
                if j:
                    moved = jnp.where(inside >= PASSES * j, moved, packs[side])
                packs[side] = moved
                pk[q, side, a - 1] = moved
        for d in (6, 7, 4, 5, 2, 3):
            only(there[ways[d][1]], lambda d=d: halo(par, q, d).start())

    def first_emit(q, carry):
        emit(0, q)
        return carry

    lax.fori_loop(0, quads, first_emit, 0)

    def passes(q, p):
        v = [f[q, p, r] for r in range(deep)]
        for t in range(PASSES):
            new = list(v)
            south = fn[q, p, t] * (v[t + 1] - v[t])
            for r in range(t + 1, deep - 1 - t):
                centre = v[r]
                flux = fe[q, p, r] * (pltpu.roll(centre, lanes - 1, 1) - centre)
                north = fn[q, p, r] * (v[r + 1] - centre)
                change = (flux - pltpu.roll(flux, 1, 1)) + (north - south)
                new[r] = centre + change
                south = north
            v = new
        for r in range(PASSES, last):
            res[p, r - PASSES] = v[r]

    def reduce_lat(k):
        return remote(red, red_lat.at[lat], sum_send.at[k], sum_recv.at[k], beside[k])

    def reduce_lon(k):
        n = len(beside) + k
        return remote(red, red_lon.at[lon], sum_send.at[n], sum_recv.at[n], along[k])

    def stage(e, carry):
        par = lax.rem(e, 2)
        odd = par == 1

        def quad(q, carry):
            for d in range(8):
                only(there[-ways[d][1]], lambda d=d: halo(par, q, d).wait_recv())
            for i in range(PASSES):
                for k in range(PACK):
                    f[q, 1 + k, i] = hs[par, q, k, i]
                    f[q, 1 + k, last + i] = hn[par, q, k, i]
            for r in range(deep):
                if PASSES <= r < last:
                    x = f[q, 0, r]
                else:
                    x = strip_row(q, r)[1]
                a, j = place_of(r, rows)
                west = pltpu.roll(pw[par, q, a], (-PASSES * j) % lanes, 1)
                east = pltpu.roll(pe[par, q, a], (EAST + OWN - PASSES * j) % lanes, 1)
                x = jnp.where(inside < PASSES, west, x)
                x = jnp.where((inside >= EAST + OWN) & (inside < EAST + OWN + PASSES), east, x)
                f[q, 0, r] = x

            def plane(p, carry):
                passes(q, p)
                return carry

            lax.fori_loop(0, 1 + PACK, plane, 0)
            for d in range(8):
                only(there[ways[d][1]], lambda d=d: halo(par, q, d).wait_send())
            sums = mom[e]
            for r in range(rows):
                edge = res[0, r]
                edge = jnp.where(
                    inside < PASSES, pltpu.roll(edge, lanes - EAST - PASSES, 1), edge
                )
                for k in range(PACK):
                    moved = pltpu.roll(edge, lanes - PASSES - STRIDE * k, 1)
                    fixed = jnp.where(
                        (cell < PASSES) | (cell >= lanes - PASSES), moved, res[1 + k, r]
                    )
                    weighed = fixed * jnp.where(odd, gain[q, k, r], 1.0)
                    sums = sums + fixed * weighed
                    f[q, 1 + k, PASSES + r] = weighed
            mom[e] = sums

            @pl.when(jnp.logical_not(odd))
            def _():
                for r in range(rows):
                    for k in range(PACK):
                        first = (q * PACK + k) * (SUB * rows) + r
                        v_out[lax.div(e, 2), pl.ds(first, SUB, stride=rows), :] = f[
                            q, 1 + k, PASSES + r
                        ]

            @pl.when(e < STAGES - 1)
            def _():
                emit(1 - par, q)

            return carry

        lax.fori_loop(0, quads, quad, 0)

        @pl.when(e == STAGES - 2)
        def _():
            for i in range(4):
                red[i : i + 1, :] = jnp.sum(mom[i], 0, keepdims=True)
            red_lat[lat] = red[...]
            for k in range(len(beside)):
                reduce_lat(k).start()

        return carry

    lax.fori_loop(0, STAGES, stage, 0)

    for k in range(len(beside)):
        reduce_lat(k).wait()
    red[...] = jnp.sum(red_lat[...], 0)
    red_lon[lon] = red[...]
    for k in range(len(along)):
        reduce_lon(k).start()
    for k in range(len(along)):
        reduce_lon(k).wait()
    sums = jnp.sum(jnp.sum(red_lon[...], 0), 1, keepdims=True)
    m0 = sums[0:1]
    x, y, z = sums[1:2] / m0, sums[2:3] / m0, sums[3:4] / m0
    alpha = 1.0 / (1.0 + x)
    beta = (y - x * x) * alpha * alpha
    c0, c1 = 1.0 - alpha + beta, -alpha
    curve = c0 * c0 * (1.0 + x) + 2.0 * c0 * c1 * (x + y) + c1 * c1 * (y + z)
    second = beta / curve
    values = (
        alpha + second * c0,
        second * c1,
        (1.0 - second) * (1.0 - alpha) - second * beta,
        -(1.0 - second) * alpha - second * c0,
        alpha * second,
    )
    for i, value in enumerate(values):
        c_out[i : i + 1, :] = jnp.broadcast_to(value, (1, lanes))


def combine_kernel(v, c, increment, residual):
    shape = increment.shape

    def scalar(i):
        return jnp.broadcast_to(c[i : i + 1, :].reshape(1, 1, shape[2]), shape)

    increment[...] = scalar(0) * v[0] + scalar(1) * v[1]
    residual[...] = scalar(2) * v[0] + scalar(3) * v[1] + scalar(4) * v[2]


def local(
    kappa_east, kappa_north, depth, sigma, obs_precision, obs_tile, obs_col, obs_lat, innovation
):
    rows, lanes = kappa_east.shape
    total = sigma.shape[0]
    tiles, bands = lax.axis_size("lon"), lax.axis_size("lat")
    listed = obs_col.shape[0]
    cap = 2 * listed // tiles
    quads = -(-total // (SUB * PACK))
    channels = quads * PACK * SUB
    levels = (total - 1) // 2
    width = -(-(total + 3) // 128) * 128

    data = jnp.concatenate(
        [
            innovation,
            jnp.zeros((width - total, listed), jnp.float32),
        ]
    )
    row = lax.broadcasted_iota(jnp.int32, (width, listed), 0)
    data = jnp.where(row == total, 1.0, data)
    data = jnp.where(row == total + 1, obs_col.astype(jnp.float32)[None], data)
    data = jnp.where(row == total + 2, obs_lat.astype(jnp.float32)[None], data)
    maps = jnp.stack([kappa_east, kappa_north, depth.astype(jnp.float32)])
    ids = jnp.arange(channels, dtype=jnp.int32)
    level = jnp.where(ids < 2 * levels, ids % levels, 0)
    level = jnp.where(ids < total, level, 2 * levels).astype(jnp.float32)
    scale = jnp.pad(sigma, (0, channels - total))
    weight = jnp.pad(obs_precision, (0, channels - total))
    coef = jnp.stack([level, scale * weight, scale * scale * weight, scale], axis=-1)
    coef = coef.reshape(quads * PACK, SUB, 4)

    deep = rows + 2 * PASSES
    padded = -(-deep // SUB) * SUB + SUB
    vmem = pl.BlockSpec(memory_space=pltpu.VMEM)
    f32 = jnp.float32
    dma = pltpu.SemaphoreType.DMA
    planes = (quads, 1 + PACK, deep, SUB, lanes)
    slots = tiles * cap
    v, c = pl.pallas_call(
        functools.partial(main_kernel, tiles, bands, cap, total),
        out_shape=[
            jax.ShapeDtypeStruct((3, channels * rows, lanes), f32),
            jax.ShapeDtypeStruct((SUB, lanes), f32),
        ],
        in_specs=[vmem] * 5,
        out_specs=[vmem] * 2,
        scratch_shapes=[
            pltpu.VMEM((tiles, cap, width), f32),
            pltpu.VMEM((tiles, cap, width), f32),
            pltpu.VMEM((3, channels, slots), jnp.bfloat16),
            pltpu.VMEM((slots, lanes), f32),
            pltpu.VMEM((9, 3, rows, lanes), f32),
            pltpu.VMEM((3, 3, padded, lanes), f32),
            pltpu.VMEM((3, padded, lanes), f32),
            pltpu.VMEM((2, 4, padded - SUB, lanes), f32),
            pltpu.VMEM(planes, f32),
            pltpu.VMEM(planes, f32),
            pltpu.VMEM(planes, f32),
            pltpu.VMEM((1 + PACK, rows, SUB, lanes), f32),
            pltpu.VMEM((quads, PACK, rows, SUB, lanes), f32),
            pltpu.VMEM((2, quads, PACK, PASSES, SUB, lanes), f32),
            pltpu.VMEM((2, quads, PACK, PASSES, SUB, lanes), f32),
            pltpu.VMEM((2, quads, 5, SUB, lanes), f32),
            pltpu.VMEM((2, quads, 5, SUB, lanes), f32),
            pltpu.VMEM((quads, 2, 3, SUB, lanes), f32),
            pltpu.VMEM((STAGES, SUB, lanes), f32),
            pltpu.VMEM((SUB, lanes), f32),
            pltpu.VMEM((bands, SUB, lanes), f32),
            pltpu.VMEM((tiles, SUB, lanes), f32),
            dma((tiles - 1,)),
            dma((tiles - 1,)),
            dma((8,)),
            dma((8,)),
            dma,
            dma((2, quads, 8)),
            dma((2, quads, 8)),
            dma((tiles + bands - 2,)),
            dma((tiles + bands - 2,)),
        ],
        compiler_params=pltpu.CompilerParams(
            collective_id=1, has_side_effects=True, vmem_limit_bytes=40 * 1024 * 1024
        ),
        name="smooth_all",
    )(data, obs_tile.reshape(1, listed), obs_tile, maps, coef)

    v = v.reshape(3, channels, rows, lanes)
    block = SUB * PACK
    out = pl.BlockSpec((block, rows, lanes), lambda i: (i, 0, 0))
    return pl.pallas_call(
        combine_kernel,
        grid=(quads,),
        out_shape=[jax.ShapeDtypeStruct((total, rows, lanes), f32)] * 2,
        in_specs=[
            pl.BlockSpec((3, block, rows, lanes), lambda i: (0, i, 0, 0)),
            pl.BlockSpec((SUB, lanes), lambda i: (0, 0)),
        ],
        out_specs=[out, out],
        name="combine",
    )(v, c)


def solution(mesh):
    return jax.shard_map(
        local,
        mesh=mesh,
        in_specs=(
            P("lat", "lon"),
            P("lat", "lon"),
            P("lat", "lon"),
            P(),
            P(),
            P(("lon", "lat"), None),
            P(("lon", "lat")),
            P(("lon", "lat")),
            P(None, ("lon", "lat")),
        ),
        out_specs=(P(None, "lat", "lon"), P(None, "lat", "lon")),
        check_vma=False,
    )
```

```python
import functools

import jax
import jax.numpy as jnp
from jax import lax
from jax.experimental import pallas as pl
from jax.experimental.pallas import tpu as pltpu
from jax.sharding import PartitionSpec as P

MESH = pl.DeviceIdType.MESH
SUB = 8
GROUPS = 4
PASSES = 5
STAGES = 5
EDGE = 8


def split3(x):
    high = x.astype(jnp.bfloat16)
    left = x - high.astype(jnp.float32)
    middle = left.astype(jnp.bfloat16)
    low = (left - middle.astype(jnp.float32)).astype(jnp.bfloat16)
    return high, middle, low


def chunks(first, end, most=8):
    count = -(-(end - first) // most)
    cuts = [first + (end - first) * i // count for i in range(count + 1)]
    return list(zip(cuts[:-1], cuts[1:]))


def iota(shape, dim):
    return lax.broadcasted_iota(jnp.int32, shape, dim)


def ones_where(mask):
    return jnp.where(mask, 1.0, 0.0).astype(jnp.bfloat16)


def main_kernel(
    tiles,
    bands,
    cap,
    total,
    data,
    tile_row,
    tile_col,
    maps,
    coef,
    v_out,
    c_out,
    pay,
    rcv,
    values,
    near,
    ext,
    base,
    f,
    fe,
    fn,
    tmp,
    gain,
    hs,
    hn,
    pw,
    pe,
    pk,
    mom,
    red,
    red_lat,
    red_lon,
    obs_send,
    obs_recv,
    map_send,
    map_recv,
    own_sem,
    halo_send,
    halo_recv,
    sum_send,
    sum_recv,
):
    lon, lat = lax.axis_index("lon"), lax.axis_index("lat")
    rows, lanes = maps.shape[1], maps.shape[2]
    blocks = f.shape[0]
    deep = rows + 2 * PASSES
    last = rows + PASSES
    wide = lanes // GROUPS
    span = wide + 2 * EDGE
    regs = span // SUB
    has_s, has_n = lat > 0, lat < bands - 1

    def at(dl, db):
        return lax.rem(lon + dl + tiles, tiles), lax.rem(lat + db + bands, bands)

    beside = [(lon, lax.rem(lat + k, bands)) for k in range(1, bands)]
    along = [(lax.rem(lon + k, tiles), lat) for k in range(1, tiles)]
    ways = [(0, -1), (0, 1), (-1, 0), (1, 0), (-1, -1), (1, -1), (-1, 1), (1, 1)]
    there = {-1: has_s, 0: None, 1: has_n}

    def only(cond, body):
        if cond is None:
            body()
        else:
            pl.when(cond)(body)

    barrier = pltpu.get_barrier_semaphore()

    def greet(peer):
        pl.semaphore_signal(barrier, inc=1, device_id=peer, device_id_type=MESH)

    for peer in beside + along:
        greet(peer)
    for dl, db in ways[4:]:
        only(there[db], functools.partial(greet, at(dl, db)))

    def remote(src, dst, send, recv, peer):
        return pltpu.make_async_remote_copy(
            src_ref=src,
            dst_ref=dst,
            send_sem=send,
            recv_sem=recv,
            device_id=peer,
            device_id_type=MESH,
        )

    listed = tile_row.shape[1]
    slots = tiles * cap
    same = tile_col[...] == tile_row[...]
    earlier = iota((listed, listed), 0) < iota((listed, listed), 1)
    rank = jnp.sum(jnp.where(same & earlier, 1.0, 0.0), 0, keepdims=True)
    slot = tile_row[...] * cap + rank.astype(jnp.int32)
    chosen = ones_where(iota((slots, listed), 0) == slot)
    width = data.shape[0]
    packed = jnp.zeros((slots, width), jnp.float32)
    for part in split3(data[...]):
        packed = packed + lax.dot_general(
            chosen, part, (((1,), (1,)), ((), ())), preferred_element_type=jnp.float32
        )
    pay[...] = packed.reshape(tiles, cap, width)

    diagonal = jnp.where(has_s, 2, 0) + jnp.where(has_n, 2, 0)
    pl.semaphore_wait(barrier, len(beside) + len(along) + diagonal)

    def slot_of(dl, db):
        return (dl + 1) * 3 + db + 1

    def map_copy(d):
        dl, db = ways[d]
        return remote(
            maps, near.at[slot_of(-dl, -db)], map_send.at[d], map_recv.at[d], at(dl, db)
        )

    for d in (4, 5, 6, 7, 2, 3, 0, 1):
        only(there[ways[d][1]], lambda d=d: map_copy(d).start())
    obs = []
    for k, peer in enumerate(along):
        copy = remote(pay.at[peer[0]], rcv.at[lon], obs_send.at[k], obs_recv.at[k], peer)
        copy.start()
        obs.append(copy)
    own = pltpu.make_async_copy(pay.at[lon], rcv.at[lon], own_sem)
    own.start()

    nothing = jnp.zeros(maps.shape, jnp.float32)
    near[slot_of(0, 0)] = maps[...]
    corner = jnp.zeros(pw.shape[:2] + pw.shape[3:], jnp.float32)

    @pl.when(jnp.logical_not(has_s))
    def _():
        for dl in (-1, 0, 1):
            near[slot_of(dl, -1)] = nothing
        hs[...] = jnp.zeros(hs.shape, jnp.float32)
        pw[:, :, 0] = corner
        pe[:, :, 0] = corner

    @pl.when(jnp.logical_not(has_n))
    def _():
        for dl in (-1, 0, 1):
            near[slot_of(dl, 1)] = nothing
        hn[...] = jnp.zeros(hn.shape, jnp.float32)
        pw[:, :, pw.shape[2] - 1] = corner
        pe[:, :, pe.shape[2] - 1] = corner

    mom[...] = jnp.zeros(mom.shape, jnp.float32)
    red[...] = jnp.zeros(red.shape, jnp.float32)
    ext[...] = jnp.zeros(ext.shape, jnp.float32)

    def clear(b, carry):
        for r in (0, deep - 1):
            f[b, r] = jnp.zeros((span, lanes), jnp.float32)
        for c in (0, span - EDGE):
            f[b, :, c : c + EDGE] = jnp.zeros((deep, EDGE, lanes), jnp.float32)
            gain[b, :, c : c + EDGE] = jnp.zeros((rows, EDGE, lanes), jnp.float32)
        return carry

    lax.fori_loop(0, blocks, clear, 0)

    for d in range(8):
        dl, db = ways[d]
        only(there[-db], lambda d=d: map_copy(d).wait_recv())
    for d in range(8):
        only(there[ways[d][1]], lambda d=d: map_copy(d).wait_send())

    for m in range(3):
        for side in range(3):
            ext[m, side, 0:PASSES] = near[3 * side, m, rows - PASSES : rows]
            ext[m, side, PASSES:last] = near[3 * side + 1, m]
            ext[m, side, last:deep] = near[3 * side + 2, m, 0:PASSES]
    edge = iota((deep, lanes), 1) == lanes - 1
    east, north, depth = [], [], [ext[2, side, 0:deep] for side in range(3)]
    ahead = [pltpu.roll(ext[2, side], lanes - 1, 1)[0:deep] for side in range(3)]
    for side in range(3):
        moved = ahead[side]
        if side < 2:
            moved = jnp.where(edge, ahead[side + 1], moved)
        east.append(jnp.minimum(depth[side], moved))
        north.append(jnp.minimum(depth[side], ext[2, side, 1 : deep + 1]))
    reach = 3 * lanes
    column = iota((reach, regs * lanes), 0) - lanes + EDGE
    target = iota((reach, regs * lanes), 1)
    start = target % lanes // wide * wide + target // lanes * SUB
    to_lane = ones_where((column >= start) & (column < start + SUB))
    sub_mask = iota((1, SUB, reach), 2) % SUB == iota((1, SUB, reach), 1)
    kinds = (
        [ext[0, side, 0:deep] for side in range(3)],
        east,
        [ext[1, side, 0:deep] for side in range(3)],
        north,
        depth,
    )
    for m, kind in enumerate(kinds):
        line = jnp.concatenate(kind, 1)
        parts = [line] if m in (1, 3, 4) else [x.astype(jnp.float32) for x in split3(line)]
        out = jnp.zeros((deep * SUB, regs * lanes), jnp.float32)
        for part in parts:
            picked = jnp.where(sub_mask, part[:, None, :], 0.0).reshape(deep * SUB, reach)
            out = out + jnp.dot(
                picked.astype(jnp.bfloat16), to_lane, preferred_element_type=jnp.float32
            )
        for i in range(regs):
            base[m, :, SUB * i : SUB * i + SUB] = out[:, lanes * i : lanes * i + lanes].reshape(
                deep, SUB, lanes
            )

    def build(b, carry):
        level = coef[b, 0:1][None]
        for j in range(regs):
            pick = pl.ds(j, SUB, stride=regs)
            for r in range(deep):
                fe[b, j, r] = jnp.where(base[1, r, pick, :] > level[0], base[0, r, pick, :], 0.0)
                fn[b, j, r] = jnp.where(base[3, r, pick, :] > level[0], base[2, r, pick, :], 0.0)
        return carry

    lax.fori_loop(0, blocks, build, 0)

    own.wait()
    for copy in obs:
        copy.wait()
    arrived = rcv[...].reshape(slots, width)
    columns = arrived[:, total + 1 : total + 2]
    flat = (blocks + 1) * lanes
    source, goal = iota((width, flat), 0), iota((width, flat), 1)
    channel = jnp.where(goal < blocks * lanes, goal // lanes * wide + goal % wide, total)
    to_flat = ones_where(source == channel)
    group = (iota((slots, flat), 1) % lanes // wide * wide).astype(jnp.float32)
    mine = (columns >= group) & (columns < group + wide)
    for i, part in enumerate(split3(arrived)):
        wide_part = jnp.dot(part, to_flat, preferred_element_type=jnp.float32)
        values[i] = jnp.where(mine, wide_part, 0.0).astype(jnp.bfloat16)
    picker = ones_where(iota((SUB, width), 1) == iota((SUB, width), 0) + total + 1)
    turned = lax.dot_general(
        picker,
        arrived.astype(jnp.bfloat16),
        (((1,), (1,)), ((), ())),
        preferred_element_type=jnp.float32,
    )
    place = turned[1:2] * wide + turned[0:1] - jnp.floor(turned[0:1] / wide) * wide
    spots = iota((rows * wide, slots), 0).astype(jnp.float32)
    to_cell = ones_where(spots == place)
    own_cols = slice(EDGE, EDGE + wide)
    depths = base[4, PASSES:last, own_cols]

    def cells_of(b):
        out = jnp.zeros((rows * wide, lanes), jnp.float32)
        for i in range(3):
            out = out + jnp.dot(
                to_cell,
                values[i, :, b * lanes : (b + 1) * lanes],
                preferred_element_type=jnp.float32,
            )
        return out.reshape(rows, wide, lanes)

    counts = cells_of(blocks)
    for b in range(blocks):
        wet = depths > coef[b, 0:1][None]
        f[b, PASSES:last, own_cols] = jnp.where(wet, coef[b, 1:2][None] * cells_of(b), 0.0)
        gain[b, :, own_cols] = jnp.where(wet, coef[b, 2:3][None] * counts, 0.0)

    lane = iota((SUB, lanes), 1)
    subs = iota((SUB, lanes), 0)
    packs = rows // GROUPS
    inner = pl.ds(EDGE, wide)

    def halo(par, b, d):
        dl, db = ways[d]
        send, recv = halo_send.at[par, b, d], halo_recv.at[par, b, d]
        if dl == 0:
            first = PASSES if db < 0 else last - PASSES
            src = f.at[b, pl.ds(first, PASSES), inner]
            dst = (hn if db < 0 else hs).at[par, b]
        else:
            pack, to = (0, pe) if dl < 0 else (1, pw)
            if db == 0:
                src = pk.at[b, pack]
                dst = to.at[par, b, pl.ds(1, packs)]
            else:
                src = pk.at[b, pack, pl.ds(0 if db < 0 else packs - 1, 1)]
                dst = to.at[par, b, pl.ds(packs + 1 if db < 0 else 0, 1)]
        return remote(src, dst, send, recv, at(dl, db))

    def emit(par, b):
        for d in (0, 1):
            only(there[ways[d][1]], lambda d=d: halo(par, b, d).start())
        for a in range(packs):
            for side, first, from_lane in ((0, EDGE, 0), (1, wide, lanes - wide)):
                out = None
                for i in range(GROUPS):
                    piece = f[b, PASSES + GROUPS * a + i, first : first + EDGE]
                    move = (wide * i - from_lane) % lanes
                    piece = pltpu.roll(piece, move, 1) if move else piece
                    out = piece if out is None else jnp.where(lane >= wide * i, piece, out)
                pk[b, side, a] = out
        for d in (6, 7, 4, 5, 2, 3):
            only(there[ways[d][1]], lambda d=d: halo(par, b, d).start())

    def first_emit(b, carry):
        emit(0, b)
        return carry

    lax.fori_loop(0, blocks, first_emit, 0)

    def reduce_lat(k):
        return remote(red, red_lat.at[lat], sum_send.at[k], sum_recv.at[k], beside[k])

    def reduce_lon(k):
        n = len(beside) + k
        return remote(red, red_lon.at[lon], sum_send.at[n], sum_recv.at[n], along[k])

    def one_pass(b, t, finish):
        def old(j, lo, hi):
            if t == 0:
                return jnp.stack(
                    [f[b, r, pl.ds(j, SUB, stride=regs), :] for r in range(lo, hi)]
                )
            return tmp[(t + 1) % 2, j, lo:hi]

        for lo, hi in chunks(t + 1, deep - 1 - t):
            v = old(0, lo - 1, hi + 1)
            wrap = pltpu.roll(v[1:-1], SUB - 1, 1)
            end = old(regs - 1, lo, hi)
            end = fe[b, regs - 1, lo:hi] * (wrap - end)
            west = pltpu.roll(end, 1, 1)
            for j in range(regs):
                centre = v[1:-1]
                if j < regs - 1:
                    following = old(j + 1, lo - 1, hi + 1)
                    flux = fe[b, j, lo:hi] * (following[1:-1] - centre)
                else:
                    following, flux = None, end
                up = fn[b, j, lo - 1 : hi] * (v[1:] - v[:-1])
                new = centre + ((flux - west) + (up[1:] - up[:-1]))
                if finish is None:
                    tmp[t % 2, j, lo:hi] = new
                else:
                    finish(j, lo, new)
                v, west = following, flux

    def stage(e, carry):
        par = lax.rem(e, 2)
        odd = par == 1

        def block(b, carry):
            for d in range(8):
                only(there[-ways[d][1]], lambda d=d: halo(par, b, d).wait_recv())
            f[b, 0:PASSES, own_cols] = hs[par, b]
            f[b, last:deep, own_cols] = hn[par, b]
            for r in range(1, deep - 1):
                a, i = (r - 1) // GROUPS, (r - 1) % GROUPS
                west = pltpu.roll(f[b, r, wide : wide + EDGE], wide, 1)
                far = pw[par, b, a]
                far = pltpu.roll(far, lanes - wide * i, 1) if i else far
                f[b, r, 0:EDGE] = jnp.where(lane < wide, far, west)
                east = pltpu.roll(f[b, r, EDGE : 2 * EDGE], lanes - wide, 1)
                far = pe[par, b, a]
                move = (lanes - wide - wide * i) % lanes
                far = pltpu.roll(far, move, 1) if move else far
                f[b, r, wide + EDGE : span] = jnp.where(lane >= lanes - wide, far, east)
            for t in range(PASSES - 1):
                one_pass(b, t, None)
            for d in range(8):
                only(there[ways[d][1]], lambda d=d: halo(par, b, d).wait_send())

            def finish(j, lo, new):
                pick = pl.ds(j, SUB, stride=regs)
                at_col = subs * regs + j
                own_here = jnp.where((at_col >= EDGE) & (at_col < EDGE + wide), 1.0, 0.0)
                sums = mom[e]
                for i in range(new.shape[0]):
                    r = lo + i
                    weight = jnp.where(odd, gain[b, r - PASSES, pick, :], own_here)
                    weighed = new[i] * weight
                    sums = sums + new[i] * weighed
                    f[b, r, pick, :] = weighed
                mom[e] = sums

            one_pass(b, PASSES - 1, finish)

            @pl.when(e < STAGES - 1)
            def _():
                emit(1 - par, b)

            @pl.when(jnp.logical_not(odd))
            def _():
                for a in range(packs):
                    first = PASSES + GROUPS * a
                    square = f[b, first : first + GROUPS, own_cols].reshape(lanes, lanes).T
                    for i in range(GROUPS):
                        out = None
                        for g in range(GROUPS):
                            piece = square[wide * g : wide * g + wide]
                            move = wide * (g - i) % lanes
                            piece = pltpu.roll(piece, move, 1) if move else piece
                            lane_all = iota((wide, lanes), 1)
                            out = piece if g == 0 else jnp.where(lane_all >= wide * g, piece, out)
                        begin = b * (wide * rows) + GROUPS * a + i
                        v_out[lax.div(e, 2), pl.ds(begin, wide, stride=rows), :] = out

            @pl.when((e == STAGES - 1) & (b == blocks // 2))
            def _():
                for k in range(len(beside)):
                    reduce_lat(k).wait()
                red[...] = jnp.sum(red_lat[...], 0)
                red_lon[lon] = red[...]
                for k in range(len(along)):
                    reduce_lon(k).start()

            return carry

        lax.fori_loop(0, blocks, block, 0)

        @pl.when(e == STAGES - 2)
        def _():
            for i in range(4):
                red[i : i + 1, :] = jnp.sum(mom[i], 0, keepdims=True)
            red_lat[lat] = red[...]
            for k in range(len(beside)):
                reduce_lat(k).start()

        return carry

    lax.fori_loop(0, STAGES, stage, 0)

    for k in range(len(along)):
        reduce_lon(k).wait()
    sums = jnp.sum(jnp.sum(red_lon[...], 0), 1, keepdims=True)
    m0 = sums[0:1]
    x, y, z = sums[1:2] / m0, sums[2:3] / m0, sums[3:4] / m0
    alpha = 1.0 / (1.0 + x)
    beta = (y - x * x) * alpha * alpha
    c0, c1 = 1.0 - alpha + beta, -alpha
    curve = c0 * c0 * (1.0 + x) + 2.0 * c0 * c1 * (x + y) + c1 * c1 * (y + z)
    second = beta / curve
    values = (
        alpha + second * c0,
        second * c1,
        (1.0 - second) * (1.0 - alpha) - second * beta,
        -(1.0 - second) * alpha - second * c0,
        alpha * second,
    )
    for i, value in enumerate(values):
        c_out[i : i + 1, :] = jnp.broadcast_to(value, (1, lanes))


def combine_kernel(v, c, increment, residual):
    shape = increment.shape

    def scalar(i):
        return jnp.broadcast_to(c[i : i + 1, :].reshape(1, 1, shape[2]), shape)

    increment[...] = scalar(0) * v[0] + scalar(1) * v[1]
    residual[...] = scalar(2) * v[0] + scalar(3) * v[1] + scalar(4) * v[2]


def local(
    kappa_east, kappa_north, depth, sigma, obs_precision, obs_tile, obs_col, obs_lat, innovation
):
    rows, lanes = kappa_east.shape
    total = sigma.shape[0]
    tiles, bands = lax.axis_size("lon"), lax.axis_size("lat")
    listed = obs_col.shape[0]
    cap = 2 * listed // tiles
    wide = lanes // GROUPS
    blocks = -(-total // wide)
    channels = blocks * wide
    levels = (total - 1) // 2
    width = -(-(total + 3) // 128) * 128

    data = jnp.concatenate(
        [
            innovation,
            jnp.zeros((width - total, listed), jnp.float32),
        ]
    )
    row = lax.broadcasted_iota(jnp.int32, (width, listed), 0)
    data = jnp.where(row == total, 1.0, data)
    data = jnp.where(row == total + 1, obs_col.astype(jnp.float32)[None], data)
    data = jnp.where(row == total + 2, obs_lat.astype(jnp.float32)[None], data)
    maps = jnp.stack([kappa_east, kappa_north, depth.astype(jnp.float32)])
    ids = jnp.arange(channels, dtype=jnp.int32)
    level = jnp.where(ids < 2 * levels, ids % levels, 0)
    level = jnp.where(ids < total, level, 2 * levels).astype(jnp.float32)
    scale = jnp.pad(sigma, (0, channels - total))
    weight = jnp.pad(obs_precision, (0, channels - total))
    coef = jnp.stack([level, scale * weight, scale * scale * weight])
    coef = jnp.tile(coef.reshape(3, blocks, wide), (1, 1, GROUPS)).transpose(1, 0, 2)
    coef = jnp.pad(coef, ((0, 0), (0, SUB - 3), (0, 0)))

    deep = rows + 2 * PASSES
    span = wide + 2 * EDGE
    regs = span // SUB
    packs = rows // GROUPS
    vmem = pl.BlockSpec(memory_space=pltpu.VMEM)
    f32 = jnp.float32
    dma = pltpu.SemaphoreType.DMA
    slots = tiles * cap
    v, c = pl.pallas_call(
        functools.partial(main_kernel, tiles, bands, cap, total),
        out_shape=[
            jax.ShapeDtypeStruct((3, channels * rows, lanes), f32),
            jax.ShapeDtypeStruct((SUB, lanes), f32),
        ],
        in_specs=[vmem] * 5,
        out_specs=[vmem] * 2,
        scratch_shapes=[
            pltpu.VMEM((tiles, cap, width), f32),
            pltpu.VMEM((tiles, cap, width), f32),
            pltpu.VMEM((3, slots, (blocks + 1) * lanes), jnp.bfloat16),
            pltpu.VMEM((9, 3, rows, lanes), f32),
            pltpu.VMEM((3, 3, -(-(deep + 1) // SUB) * SUB, lanes), f32),
            pltpu.VMEM((5, deep, span, lanes), f32),
            pltpu.VMEM((blocks, deep, span, lanes), f32),
            pltpu.VMEM((blocks, regs, deep, SUB, lanes), f32),
            pltpu.VMEM((blocks, regs, deep, SUB, lanes), f32),
            pltpu.VMEM((2, regs, deep, SUB, lanes), f32),
            pltpu.VMEM((blocks, rows, span, lanes), f32),
            pltpu.VMEM((2, blocks, PASSES, wide, lanes), f32),
            pltpu.VMEM((2, blocks, PASSES, wide, lanes), f32),
            pltpu.VMEM((2, blocks, packs + 2, SUB, lanes), f32),
            pltpu.VMEM((2, blocks, packs + 2, SUB, lanes), f32),
            pltpu.VMEM((blocks, 2, packs, SUB, lanes), f32),
            pltpu.VMEM((STAGES, SUB, lanes), f32),
            pltpu.VMEM((SUB, lanes), f32),
            pltpu.VMEM((bands, SUB, lanes), f32),
            pltpu.VMEM((tiles, SUB, lanes), f32),
            dma((tiles - 1,)),
            dma((tiles - 1,)),
            dma((8,)),
            dma((8,)),
            dma,
            dma((2, blocks, 8)),
            dma((2, blocks, 8)),
            dma((tiles + bands - 2,)),
            dma((tiles + bands - 2,)),
        ],
        compiler_params=pltpu.CompilerParams(
            collective_id=1, has_side_effects=True, vmem_limit_bytes=48 * 1024 * 1024
        ),
        name="smooth_all",
    )(data, obs_tile.reshape(1, listed), obs_tile, maps, coef)

    v = v.reshape(3, channels, rows, lanes)
    block = wide
    out = pl.BlockSpec((block, rows, lanes), lambda i: (i, 0, 0))
    return pl.pallas_call(
        combine_kernel,
        grid=(blocks,),
        out_shape=[jax.ShapeDtypeStruct((total, rows, lanes), f32)] * 2,
        in_specs=[
            pl.BlockSpec((3, block, rows, lanes), lambda i: (0, i, 0, 0)),
            pl.BlockSpec((SUB, lanes), lambda i: (0, 0)),
        ],
        out_specs=[out, out],
        name="combine",
    )(v, c)


def solution(mesh):
    return jax.shard_map(
        local,
        mesh=mesh,
        in_specs=(
            P("lat", "lon"),
            P("lat", "lon"),
            P("lat", "lon"),
            P(),
            P(),
            P(("lon", "lat"), None),
            P(("lon", "lat")),
            P(("lon", "lat")),
            P(None, ("lon", "lat")),
        ),
        out_specs=(P(None, "lat", "lon"), P(None, "lat", "lon")),
        check_vma=False,
    )
```

```python
import functools

import jax
import jax.numpy as jnp
from jax import lax
from jax.experimental import pallas as pl
from jax.experimental.pallas import tpu as pltpu
from jax.sharding import PartitionSpec as P

MESH = pl.DeviceIdType.MESH
SUB = 8
GROUPS = 4
PASSES = 5
STAGES = 5
EDGE = 8


def split3(x):
    high = x.astype(jnp.bfloat16)
    left = x - high.astype(jnp.float32)
    middle = left.astype(jnp.bfloat16)
    low = (left - middle.astype(jnp.float32)).astype(jnp.bfloat16)
    return high, middle, low


def chunks(first, end, most=8):
    count = -(-(end - first) // most)
    cuts = [first + (end - first) * i // count for i in range(count + 1)]
    return list(zip(cuts[:-1], cuts[1:]))


def iota(shape, dim):
    return lax.broadcasted_iota(jnp.int32, shape, dim)


def ones_where(mask):
    return jnp.where(mask, 1.0, 0.0).astype(jnp.bfloat16)


def main_kernel(
    tiles,
    bands,
    cap,
    total,
    ke_in,
    kn_in,
    depth_in,
    sigma_in,
    precision_in,
    tile_in,
    col_in,
    lat_in,
    innovation_in,
    v_out,
    c_out,
    depth_own,
    sigma,
    precision,
    index,
    innovation,
    maps,
    data,
    rates,
    coef,
    pay,
    rcv,
    values,
    near,
    ext,
    base,
    f,
    fe,
    fn,
    tmp,
    gain,
    hs,
    hn,
    pw,
    pe,
    pk,
    mom,
    red,
    red_lat,
    red_lon,
    obs_send,
    obs_recv,
    map_send,
    map_recv,
    own_sem,
    load_sem,
    halo_send,
    halo_recv,
    sum_send,
    sum_recv,
):
    lon, lat = lax.axis_index("lon"), lax.axis_index("lat")
    rows, lanes = maps.shape[1], maps.shape[2]
    blocks = f.shape[0]
    deep = rows + 2 * PASSES
    last = rows + PASSES
    wide = lanes // GROUPS
    span = wide + 2 * EDGE
    regs = span // SUB
    has_s, has_n = lat > 0, lat < bands - 1

    def at(dl, db):
        return lax.rem(lon + dl + tiles, tiles), lax.rem(lat + db + bands, bands)

    beside = [(lon, lax.rem(lat + k, bands)) for k in range(1, bands)]
    along = [(lax.rem(lon + k, tiles), lat) for k in range(1, tiles)]
    ways = [(0, -1), (0, 1), (-1, 0), (1, 0), (-1, -1), (1, -1), (-1, 1), (1, 1)]
    there = {-1: has_s, 0: None, 1: has_n}

    def only(cond, body):
        if cond is None:
            body()
        else:
            pl.when(cond)(body)

    loads = [
        pltpu.make_async_copy(src, dst, load_sem.at[i])
        for i, (src, dst) in enumerate(
            (
                (ke_in, maps.at[0]),
                (kn_in, maps.at[1]),
                (depth_in, depth_own),
                (tile_in, index.at[0]),
                (col_in, index.at[1]),
                (lat_in, index.at[2]),
                (innovation_in, innovation),
                (sigma_in, sigma),
                (precision_in, precision),
            )
        )
    ]
    for load in loads:
        load.start()

    barrier = pltpu.get_barrier_semaphore()

    def greet(peer):
        pl.semaphore_signal(barrier, inc=1, device_id=peer, device_id_type=MESH)

    for peer in beside + along:
        greet(peer)
    for dl, db in ways[4:]:
        only(there[db], functools.partial(greet, at(dl, db)))

    def remote(src, dst, send, recv, peer):
        return pltpu.make_async_remote_copy(
            src_ref=src,
            dst_ref=dst,
            send_sem=send,
            recv_sem=recv,
            device_id=peer,
            device_id_type=MESH,
        )

    def slot_of(dl, db):
        return (dl + 1) * 3 + db + 1

    def map_copy(d):
        dl, db = ways[d]
        return remote(
            maps, near.at[slot_of(-dl, -db)], map_send.at[d], map_recv.at[d], at(dl, db)
        )

    for load in loads[:3]:
        load.wait()
    maps[2] = depth_own[...].astype(jnp.float32)
    diagonal = jnp.where(has_s, 2, 0) + jnp.where(has_n, 2, 0)
    pl.semaphore_wait(barrier, len(beside) + len(along) + diagonal)
    for d in (4, 5, 6, 7, 2, 3, 0, 1):
        only(there[ways[d][1]], lambda d=d: map_copy(d).start())

    for load in loads[3:7]:
        load.wait()
    listed = index.shape[2]
    slots = tiles * cap
    width = data.shape[0]
    kinds_at = -(-total // SUB) * SUB
    data[kinds_at - SUB :] = jnp.zeros((width - kinds_at + SUB, listed), jnp.float32)
    data[0:total] = innovation[...]
    data[kinds_at : kinds_at + 1] = jnp.ones((1, listed), jnp.float32)
    data[kinds_at + 1 : kinds_at + 2] = index[1].astype(jnp.float32)
    data[kinds_at + 2 : kinds_at + 3] = index[2].astype(jnp.float32)
    tile_row = jnp.broadcast_to(index[0].astype(jnp.float32), (listed, listed))
    earlier = iota((listed, listed), 0) < iota((listed, listed), 1)
    same = (tile_row == tile_row.T) & earlier
    rank = jnp.sum(jnp.where(same, 1.0, 0.0), 0, keepdims=True)
    slot = index[0] * cap + rank.astype(jnp.int32)
    chosen = ones_where(iota((slots, listed), 0) == slot)
    packed = jnp.zeros((slots, width), jnp.float32)
    for part in split3(data[...]):
        packed = packed + lax.dot_general(
            chosen, part, (((1,), (1,)), ((), ())), preferred_element_type=jnp.float32
        )
    pay[...] = packed.reshape(tiles, cap, width)
    obs = []
    for k, peer in enumerate(along):
        copy = remote(pay.at[peer[0]], rcv.at[lon], obs_send.at[k], obs_recv.at[k], peer)
        copy.start()
        obs.append(copy)
    own = pltpu.make_async_copy(pay.at[lon], rcv.at[lon], own_sem)
    own.start()

    nothing = jnp.zeros(maps.shape, jnp.float32)
    near[slot_of(0, 0)] = maps[...]
    corner = jnp.zeros(pw.shape[:2] + pw.shape[3:], jnp.float32)

    @pl.when(jnp.logical_not(has_s))
    def _():
        for dl in (-1, 0, 1):
            near[slot_of(dl, -1)] = nothing
        hs[...] = jnp.zeros(hs.shape, jnp.float32)
        pw[:, :, 0] = corner
        pe[:, :, 0] = corner

    @pl.when(jnp.logical_not(has_n))
    def _():
        for dl in (-1, 0, 1):
            near[slot_of(dl, 1)] = nothing
        hn[...] = jnp.zeros(hn.shape, jnp.float32)
        pw[:, :, pw.shape[2] - 1] = corner
        pe[:, :, pe.shape[2] - 1] = corner

    mom[...] = jnp.zeros(mom.shape, jnp.float32)
    red[...] = jnp.zeros(red.shape, jnp.float32)
    ext[...] = jnp.zeros(ext.shape, jnp.float32)

    def clear(b, carry):
        for r in (0, deep - 1):
            f[b, r] = jnp.zeros((span, lanes), jnp.float32)
        for c in (0, span - EDGE):
            f[b, :, c : c + EDGE] = jnp.zeros((deep, EDGE, lanes), jnp.float32)
            gain[b, :, c : c + EDGE] = jnp.zeros((rows, EDGE, lanes), jnp.float32)
        return carry

    lax.fori_loop(0, blocks, clear, 0)

    for load in loads[7:]:
        load.wait()
    levels = (total - 1) // 2
    rates[...] = jnp.zeros(rates.shape, jnp.float32)
    rates[0:1, 0:total] = sigma[...] * precision[...]
    rates[1:2, 0:total] = sigma[...] * sigma[...] * precision[...]
    coef_lane = iota((SUB, lanes), 1)
    for b in range(blocks):
        tile, first = b * wide // lanes, b * wide % lanes
        piece = rates[:, tile * lanes : tile * lanes + lanes]
        out = None
        for g in range(GROUPS):
            move = (wide * g - first) % lanes
            moved = pltpu.roll(piece, move, 1) if move else piece
            out = moved if g == 0 else jnp.where(coef_lane >= wide * g, moved, out)
        coef[b, 1:3] = out[0:2]
        channel = coef_lane[0:1] % wide + b * wide
        level = jnp.where(channel < 2 * levels, channel % levels, 0)
        level = jnp.where(channel < total, level, 2 * levels)
        coef[b, 0:1] = level.astype(jnp.float32)

    for d in range(8):
        dl, db = ways[d]
        only(there[-db], lambda d=d: map_copy(d).wait_recv())
    for d in range(8):
        only(there[ways[d][1]], lambda d=d: map_copy(d).wait_send())

    for m in range(3):
        for side in range(3):
            ext[m, side, 0:PASSES] = near[3 * side, m, rows - PASSES : rows]
            ext[m, side, PASSES:last] = near[3 * side + 1, m]
            ext[m, side, last:deep] = near[3 * side + 2, m, 0:PASSES]
    edge = iota((deep, lanes), 1) == lanes - 1
    east, north, depth = [], [], [ext[2, side, 0:deep] for side in range(3)]
    ahead = [pltpu.roll(ext[2, side], lanes - 1, 1)[0:deep] for side in range(3)]
    for side in range(3):
        moved = ahead[side]
        if side < 2:
            moved = jnp.where(edge, ahead[side + 1], moved)
        east.append(jnp.minimum(depth[side], moved))
        north.append(jnp.minimum(depth[side], ext[2, side, 1 : deep + 1]))
    reach = 3 * lanes
    column = iota((reach, regs * lanes), 0) - lanes + EDGE
    target = iota((reach, regs * lanes), 1)
    start = target % lanes // wide * wide + target // lanes * SUB
    to_lane = ones_where((column >= start) & (column < start + SUB))
    sub_mask = iota((1, SUB, reach), 2) % SUB == iota((1, SUB, reach), 1)
    kinds = (
        [ext[0, side, 0:deep] for side in range(3)],
        east,
        [ext[1, side, 0:deep] for side in range(3)],
        north,
        depth,
    )
    for m, kind in enumerate(kinds):
        line = jnp.concatenate(kind, 1)
        parts = [line] if m in (1, 3, 4) else [x.astype(jnp.float32) for x in split3(line)]
        out = jnp.zeros((deep * SUB, regs * lanes), jnp.float32)
        for part in parts:
            picked = jnp.where(sub_mask, part[:, None, :], 0.0).reshape(deep * SUB, reach)
            out = out + jnp.dot(
                picked.astype(jnp.bfloat16), to_lane, preferred_element_type=jnp.float32
            )
        for i in range(regs):
            base[m, :, SUB * i : SUB * i + SUB] = out[:, lanes * i : lanes * i + lanes].reshape(
                deep, SUB, lanes
            )

    def build(b, carry):
        level = coef[b, 0:1][None]
        for j in range(regs):
            pick = pl.ds(j, SUB, stride=regs)
            for r in range(deep):
                fe[b, j, r] = jnp.where(base[1, r, pick, :] > level[0], base[0, r, pick, :], 0.0)
                fn[b, j, r] = jnp.where(base[3, r, pick, :] > level[0], base[2, r, pick, :], 0.0)
        return carry

    lax.fori_loop(0, blocks, build, 0)

    own.wait()
    for copy in obs:
        copy.wait()
    arrived = rcv[...].reshape(slots, width)
    columns = arrived[:, kinds_at + 1 : kinds_at + 2]
    flat = (blocks + 1) * lanes
    source, goal = iota((width, flat), 0), iota((width, flat), 1)
    channel = jnp.where(goal < blocks * lanes, goal // lanes * wide + goal % wide, kinds_at)
    to_flat = ones_where(source == channel)
    group = (iota((slots, flat), 1) % lanes // wide * wide).astype(jnp.float32)
    mine = (columns >= group) & (columns < group + wide)
    for i, part in enumerate(split3(arrived)):
        wide_part = jnp.dot(part, to_flat, preferred_element_type=jnp.float32)
        values[i] = jnp.where(mine, wide_part, 0.0).astype(jnp.bfloat16)
    picker = ones_where(iota((SUB, width), 1) == iota((SUB, width), 0) + kinds_at + 1)
    turned = lax.dot_general(
        picker,
        arrived.astype(jnp.bfloat16),
        (((1,), (1,)), ((), ())),
        preferred_element_type=jnp.float32,
    )
    place = turned[1:2] * wide + turned[0:1] - jnp.floor(turned[0:1] / wide) * wide
    spots = iota((rows * wide, slots), 0).astype(jnp.float32)
    to_cell = ones_where(spots == place)
    own_cols = slice(EDGE, EDGE + wide)
    depths = base[4, PASSES:last, own_cols]

    def cells_of(b):
        out = jnp.zeros((rows * wide, lanes), jnp.float32)
        for i in range(3):
            out = out + jnp.dot(
                to_cell,
                values[i, :, b * lanes : (b + 1) * lanes],
                preferred_element_type=jnp.float32,
            )
        return out.reshape(rows, wide, lanes)

    counts = cells_of(blocks)
    for b in range(blocks):
        wet = depths > coef[b, 0:1][None]
        f[b, PASSES:last, own_cols] = jnp.where(wet, coef[b, 1:2][None] * cells_of(b), 0.0)
        gain[b, :, own_cols] = jnp.where(wet, coef[b, 2:3][None] * counts, 0.0)

    lane = iota((SUB, lanes), 1)
    subs = iota((SUB, lanes), 0)
    packs = rows // GROUPS
    inner = pl.ds(EDGE, wide)

    def halo(par, b, d):
        dl, db = ways[d]
        send, recv = halo_send.at[par, b, d], halo_recv.at[par, b, d]
        if dl == 0:
            first = PASSES if db < 0 else last - PASSES
            src = f.at[b, pl.ds(first, PASSES), inner]
            dst = (hn if db < 0 else hs).at[par, b]
        else:
            pack, to = (0, pe) if dl < 0 else (1, pw)
            if db == 0:
                src = pk.at[b, pack]
                dst = to.at[par, b, pl.ds(1, packs)]
            else:
                src = pk.at[b, pack, pl.ds(0 if db < 0 else packs - 1, 1)]
                dst = to.at[par, b, pl.ds(packs + 1 if db < 0 else 0, 1)]
        return remote(src, dst, send, recv, at(dl, db))

    def emit(par, b):
        for d in (0, 1):
            only(there[ways[d][1]], lambda d=d: halo(par, b, d).start())
        for a in range(packs):
            for side, first, from_lane in ((0, EDGE, 0), (1, wide, lanes - wide)):
                out = None
                for i in range(GROUPS):
                    piece = f[b, PASSES + GROUPS * a + i, first : first + EDGE]
                    move = (wide * i - from_lane) % lanes
                    piece = pltpu.roll(piece, move, 1) if move else piece
                    out = piece if out is None else jnp.where(lane >= wide * i, piece, out)
                pk[b, side, a] = out
        for d in (6, 7, 4, 5, 2, 3):
            only(there[ways[d][1]], lambda d=d: halo(par, b, d).start())

    def first_emit(b, carry):
        emit(0, b)
        return carry

    lax.fori_loop(0, blocks, first_emit, 0)

    def reduce_lat(k):
        return remote(red, red_lat.at[lat], sum_send.at[k], sum_recv.at[k], beside[k])

    def reduce_lon(k):
        n = len(beside) + k
        return remote(red, red_lon.at[lon], sum_send.at[n], sum_recv.at[n], along[k])

    def one_pass(b, t, finish):
        def old(j, lo, hi):
            if t == 0:
                return jnp.stack(
                    [f[b, r, pl.ds(j, SUB, stride=regs), :] for r in range(lo, hi)]
                )
            return tmp[(t + 1) % 2, j, lo:hi]

        for lo, hi in chunks(t + 1, deep - 1 - t):
            v = old(0, lo - 1, hi + 1)
            wrap = pltpu.roll(v[1:-1], SUB - 1, 1)
            end = old(regs - 1, lo, hi)
            end = fe[b, regs - 1, lo:hi] * (wrap - end)
            west = pltpu.roll(end, 1, 1)
            for j in range(regs):
                centre = v[1:-1]
                if j < regs - 1:
                    following = old(j + 1, lo - 1, hi + 1)
                    flux = fe[b, j, lo:hi] * (following[1:-1] - centre)
                else:
                    following, flux = None, end
                up = fn[b, j, lo - 1 : hi] * (v[1:] - v[:-1])
                new = centre + ((flux - west) + (up[1:] - up[:-1]))
                if finish is None:
                    tmp[t % 2, j, lo:hi] = new
                else:
                    finish(j, lo, new)
                v, west = following, flux

    def stage(e, carry):
        par = lax.rem(e, 2)
        odd = par == 1

        def block(b, carry):
            for d in range(8):
                only(there[-ways[d][1]], lambda d=d: halo(par, b, d).wait_recv())
            f[b, 0:PASSES, own_cols] = hs[par, b]
            f[b, last:deep, own_cols] = hn[par, b]
            for r in range(1, deep - 1):
                a, i = (r - 1) // GROUPS, (r - 1) % GROUPS
                west = pltpu.roll(f[b, r, wide : wide + EDGE], wide, 1)
                far = pw[par, b, a]
                far = pltpu.roll(far, lanes - wide * i, 1) if i else far
                f[b, r, 0:EDGE] = jnp.where(lane < wide, far, west)
                east = pltpu.roll(f[b, r, EDGE : 2 * EDGE], lanes - wide, 1)
                far = pe[par, b, a]
                move = (lanes - wide - wide * i) % lanes
                far = pltpu.roll(far, move, 1) if move else far
                f[b, r, wide + EDGE : span] = jnp.where(lane >= lanes - wide, far, east)
            for t in range(PASSES - 1):
                one_pass(b, t, None)
            for d in range(8):
                only(there[ways[d][1]], lambda d=d: halo(par, b, d).wait_send())

            def finish(j, lo, new):
                pick = pl.ds(j, SUB, stride=regs)
                at_col = subs * regs + j
                own_here = jnp.where((at_col >= EDGE) & (at_col < EDGE + wide), 1.0, 0.0)
                sums = mom[e]
                for i in range(new.shape[0]):
                    r = lo + i
                    weight = jnp.where(odd, gain[b, r - PASSES, pick, :], own_here)
                    weighed = new[i] * weight
                    sums = sums + new[i] * weighed
                    f[b, r, pick, :] = weighed
                mom[e] = sums

            one_pass(b, PASSES - 1, finish)

            @pl.when(e < STAGES - 1)
            def _():
                emit(1 - par, b)

            @pl.when(jnp.logical_not(odd))
            def _():
                for a in range(packs):
                    first = PASSES + GROUPS * a
                    square = f[b, first : first + GROUPS, own_cols].reshape(lanes, lanes).T
                    pieces = [square[wide * g : wide * g + wide] for g in range(GROUPS)]
                    lane_all = iota((wide, lanes), 1)
                    step = GROUPS // 2
                    while step:
                        move = step * wide
                        low = lane_all // move % 2 == 0
                        for g in range(GROUPS):
                            if g // step % 2 == 0:
                                one, two = pieces[g], pieces[g + step]
                                pieces[g] = jnp.where(low, one, pltpu.roll(two, move, 1))
                                pieces[g + step] = jnp.where(
                                    low, pltpu.roll(one, lanes - move, 1), two
                                )
                        step //= 2
                    for i in range(GROUPS):
                        begin = b * (wide * rows) + GROUPS * a + i
                        v_out[lax.div(e, 2), pl.ds(begin, wide, stride=rows), :] = pieces[i]

            @pl.when((e == STAGES - 1) & (b == blocks // 2))
            def _():
                for k in range(len(beside)):
                    reduce_lat(k).wait()
                red[...] = jnp.sum(red_lat[...], 0)
                red_lon[lon] = red[...]
                for k in range(len(along)):
                    reduce_lon(k).start()

            return carry

        lax.fori_loop(0, blocks, block, 0)

        @pl.when(e == STAGES - 2)
        def _():
            for i in range(4):
                red[i : i + 1, :] = jnp.sum(mom[i], 0, keepdims=True)
            red_lat[lat] = red[...]
            for k in range(len(beside)):
                reduce_lat(k).start()

        return carry

    lax.fori_loop(0, STAGES, stage, 0)

    for k in range(len(along)):
        reduce_lon(k).wait()
    sums = jnp.sum(jnp.sum(red_lon[...], 0), 1, keepdims=True)
    m0 = sums[0:1]
    x, y, z = sums[1:2] / m0, sums[2:3] / m0, sums[3:4] / m0
    alpha = 1.0 / (1.0 + x)
    beta = (y - x * x) * alpha * alpha
    c0, c1 = 1.0 - alpha + beta, -alpha
    curve = c0 * c0 * (1.0 + x) + 2.0 * c0 * c1 * (x + y) + c1 * c1 * (y + z)
    second = beta / curve
    values = (
        alpha + second * c0,
        second * c1,
        (1.0 - second) * (1.0 - alpha) - second * beta,
        -(1.0 - second) * alpha - second * c0,
        alpha * second,
    )
    for i, value in enumerate(values):
        c_out[i : i + 1, :] = jnp.broadcast_to(value, (1, lanes))


def combine_kernel(block, v, c, increment, residual, held, sems):
    size, lanes = increment.shape
    copies = []
    for n, first in enumerate(range(0, size, block)):
        count = min(block, size - first)
        part = pl.ds(first, count)
        zero, one, two = v[0, part], v[1, part], v[2, part]
        held[0, part] = c[0:1] * zero + c[1:2] * one
        held[1, part] = c[2:3] * zero + c[3:4] * one + c[4:5] * two
        for i, target in enumerate((increment, residual)):
            copy = pltpu.make_async_copy(held.at[i, part], target.at[part], sems.at[i, n])
            copy.start()
            copies.append(copy)
    for copy in copies:
        copy.wait()


def local(
    kappa_east, kappa_north, depth, sigma, obs_precision, obs_tile, obs_col, obs_lat, innovation
):
    rows, lanes = kappa_east.shape
    total = sigma.shape[0]
    tiles, bands = lax.axis_size("lon"), lax.axis_size("lat")
    listed = obs_col.shape[0]
    cap = 2 * listed // tiles
    wide = lanes // GROUPS
    blocks = -(-total // wide)
    channels = blocks * wide
    width = -(-(-(-total // SUB) * SUB + SUB) // 128) * 128

    deep = rows + 2 * PASSES
    span = wide + 2 * EDGE
    regs = span // SUB
    packs = rows // GROUPS
    vmem = pl.BlockSpec(memory_space=pltpu.VMEM)
    f32 = jnp.float32
    dma = pltpu.SemaphoreType.DMA
    slots = tiles * cap
    v, c = pl.pallas_call(
        functools.partial(main_kernel, tiles, bands, cap, total),
        out_shape=[
            jax.ShapeDtypeStruct((3, channels * rows, lanes), f32),
            jax.ShapeDtypeStruct((SUB, lanes), f32),
        ],
        in_specs=[pl.BlockSpec(memory_space=pltpu.HBM)] * 9,
        out_specs=[vmem] * 2,
        scratch_shapes=[
            pltpu.VMEM((rows, lanes), jnp.int32),
            pltpu.VMEM((1, total), f32),
            pltpu.VMEM((1, total), f32),
            pltpu.VMEM((3, 1, listed), jnp.int32),
            pltpu.VMEM((total, listed), f32),
            pltpu.VMEM((3, rows, lanes), f32),
            pltpu.VMEM((width, listed), f32),
            pltpu.VMEM((SUB, -(-channels // lanes) * lanes), f32),
            pltpu.VMEM((blocks, SUB, lanes), f32),
            pltpu.VMEM((tiles, cap, width), f32),
            pltpu.VMEM((tiles, cap, width), f32),
            pltpu.VMEM((3, slots, (blocks + 1) * lanes), jnp.bfloat16),
            pltpu.VMEM((9, 3, rows, lanes), f32),
            pltpu.VMEM((3, 3, -(-(deep + 1) // SUB) * SUB, lanes), f32),
            pltpu.VMEM((5, deep, span, lanes), f32),
            pltpu.VMEM((blocks, deep, span, lanes), f32),
            pltpu.VMEM((blocks, regs, deep, SUB, lanes), f32),
            pltpu.VMEM((blocks, regs, deep, SUB, lanes), f32),
            pltpu.VMEM((2, regs, deep, SUB, lanes), f32),
            pltpu.VMEM((blocks, rows, span, lanes), f32),
            pltpu.VMEM((2, blocks, PASSES, wide, lanes), f32),
            pltpu.VMEM((2, blocks, PASSES, wide, lanes), f32),
            pltpu.VMEM((2, blocks, packs + 2, SUB, lanes), f32),
            pltpu.VMEM((2, blocks, packs + 2, SUB, lanes), f32),
            pltpu.VMEM((blocks, 2, packs, SUB, lanes), f32),
            pltpu.VMEM((STAGES, SUB, lanes), f32),
            pltpu.VMEM((SUB, lanes), f32),
            pltpu.VMEM((bands, SUB, lanes), f32),
            pltpu.VMEM((tiles, SUB, lanes), f32),
            dma((tiles - 1,)),
            dma((tiles - 1,)),
            dma((8,)),
            dma((8,)),
            dma,
            dma((9,)),
            dma((2, blocks, 8)),
            dma((2, blocks, 8)),
            dma((tiles + bands - 2,)),
            dma((tiles + bands - 2,)),
        ],
        compiler_params=pltpu.CompilerParams(
            collective_id=1, has_side_effects=True, vmem_limit_bytes=48 * 1024 * 1024
        ),
        name="smooth_all",
    )(
        *[
            pltpu.with_memory_space_constraint(x, pltpu.HBM)
            for x in (
                kappa_east,
                kappa_north,
                depth,
                sigma.reshape(1, total),
                obs_precision.reshape(1, total),
                obs_tile.reshape(1, listed),
                obs_col.reshape(1, listed),
                obs_lat.reshape(1, listed),
                innovation,
            )
        ]
    )

    block = wide * rows
    increment, residual = pl.pallas_call(
        functools.partial(combine_kernel, block),
        out_shape=[jax.ShapeDtypeStruct((total * rows, lanes), f32)] * 2,
        in_specs=[vmem] * 2,
        out_specs=[pl.BlockSpec(memory_space=pl.ANY)] * 2,
        scratch_shapes=[pltpu.VMEM((2, total * rows, lanes), f32), dma((2, blocks))],
        compiler_params=pltpu.CompilerParams(vmem_limit_bytes=10 * 1024 * 1024),
        name="combine",
    )(v, c)
    shape = (total, rows, lanes)
    return increment.reshape(shape), residual.reshape(shape)


def solution(mesh):
    return jax.shard_map(
        local,
        mesh=mesh,
        in_specs=(
            P("lat", "lon"),
            P("lat", "lon"),
            P("lat", "lon"),
            P(),
            P(),
            P(("lon", "lat"), None),
            P(("lon", "lat")),
            P(("lon", "lat")),
            P(None, ("lon", "lat")),
        ),
        out_specs=(P(None, "lat", "lon"), P(None, "lat", "lon")),
        check_vma=False,
    )
```

```python
import functools

import jax
import jax.numpy as jnp
from jax import lax
from jax.experimental import pallas as pl
from jax.experimental.pallas import tpu as pltpu
from jax.sharding import PartitionSpec as P

MESH = pl.DeviceIdType.MESH
SUB = 8
PASSES = 5
STAGES = 5
EDGE = 8


SCRATCH = ("base", "values", "coef", "f", "fe", "fn", "tmp", "gain")
SCRATCH += ("hs", "hn", "pw", "pe", "pk", "send", "recv")


class Layout:
    def __init__(self, first, blocks, groups, rows, lanes):
        self.first, self.blocks, self.groups = first, blocks, groups
        self.wide = lanes // groups
        self.span = self.wide + 2 * EDGE
        self.regs = self.span // SUB
        self.packs = rows // groups
        self.corner = (PASSES - 1) // groups
        self.rows, self.lanes = rows, lanes

    def bind(self, refs):
        for name, ref in zip(SCRATCH, refs):
            setattr(self, name, ref)

    def shapes(self, slots):
        f32, dma = jnp.float32, pltpu.SemaphoreType.DMA
        rows, lanes, blocks = self.rows, self.lanes, self.blocks
        deep = rows + 2 * PASSES
        faces = pltpu.VMEM((blocks, self.regs, deep, SUB, lanes), f32)
        beside = pltpu.VMEM((2, blocks, PASSES, self.wide, lanes), f32)
        edge = pltpu.VMEM((2, blocks, self.packs + 2 * self.corner, SUB, lanes), f32)
        return [
            pltpu.VMEM((5, deep, self.span, lanes), f32),
            pltpu.VMEM((3, slots, (blocks + 1) * lanes), jnp.bfloat16),
            pltpu.VMEM((blocks, SUB, lanes), f32),
            pltpu.VMEM((blocks, deep, self.span, lanes), f32),
            faces,
            faces,
            pltpu.VMEM((2, self.regs, deep, SUB, lanes), f32),
            pltpu.VMEM((blocks, rows, self.span, lanes), f32),
            beside,
            beside,
            edge,
            edge,
            pltpu.VMEM((blocks, 2, self.packs, SUB, lanes), f32),
            dma((2, blocks, 8)),
            dma((2, blocks, 8)),
        ]


def layouts_of(total, rows, lanes):
    pairs = total // (lanes // 2)
    left = total - pairs * (lanes // 2)
    out = [Layout(0, pairs, 2, rows, lanes)]
    if left:
        out.append(Layout(pairs * (lanes // 2), -(-left // (lanes // 4)), 4, rows, lanes))
    return out


def split3(x):
    high = x.astype(jnp.bfloat16)
    left = x - high.astype(jnp.float32)
    middle = left.astype(jnp.bfloat16)
    low = (left - middle.astype(jnp.float32)).astype(jnp.bfloat16)
    return high, middle, low


def chunks(first, end, most=8):
    count = -(-(end - first) // most)
    cuts = [first + (end - first) * i // count for i in range(count + 1)]
    return list(zip(cuts[:-1], cuts[1:]))


def iota(shape, dim):
    return lax.broadcasted_iota(jnp.int32, shape, dim)


def ones_where(mask):
    return jnp.where(mask, 1.0, 0.0).astype(jnp.bfloat16)


def main_kernel(
    tiles,
    bands,
    cap,
    total,
    ke_in,
    kn_in,
    depth_in,
    sigma_in,
    precision_in,
    tile_in,
    col_in,
    lat_in,
    innovation_in,
    v_out,
    c_out,
    depth_own,
    sigma,
    precision,
    index,
    innovation,
    maps,
    data,
    rates,
    pay,
    rcv,
    near,
    ext,
    mom,
    red,
    red_all,
    obs_send,
    obs_recv,
    map_send,
    map_recv,
    own_sem,
    load_sem,
    sum_send,
    sum_recv,
    *rest,
):
    lon, lat = lax.axis_index("lon"), lax.axis_index("lat")
    rows, lanes = maps.shape[1], maps.shape[2]
    deep = rows + 2 * PASSES
    last = rows + PASSES
    layouts = layouts_of(total, rows, lanes)
    for n, lay in enumerate(layouts):
        lay.bind(rest[n * len(SCRATCH) : (n + 1) * len(SCRATCH)])
    has_s, has_n = lat > 0, lat < bands - 1

    def at(dl, db):
        return lax.rem(lon + dl + tiles, tiles), lax.rem(lat + db + bands, bands)

    along = [(lax.rem(lon + k, tiles), lat) for k in range(1, tiles)]
    ways = [(0, -1), (0, 1), (-1, 0), (1, 0), (-1, -1), (1, -1), (-1, 1), (1, 1)]
    there = {-1: has_s, 0: None, 1: has_n}

    def only(cond, body):
        if cond is None:
            body()
        else:
            pl.when(cond)(body)

    loads = [
        pltpu.make_async_copy(src, dst, load_sem.at[i])
        for i, (src, dst) in enumerate(
            (
                (ke_in, maps.at[0]),
                (kn_in, maps.at[1]),
                (depth_in, depth_own),
                (tile_in, index.at[0]),
                (col_in, index.at[1]),
                (lat_in, index.at[2]),
                (innovation_in, innovation),
                (sigma_in, sigma),
                (precision_in, precision),
            )
        )
    ]
    for load in loads:
        load.start()

    barrier = pltpu.get_barrier_semaphore()

    def greet(peer):
        pl.semaphore_signal(barrier, inc=1, device_id=peer, device_id_type=MESH)

    def greet_all(k, carry):
        peer = lax.rem(lon * bands + lat + k, tiles * bands)
        greet((lax.div(peer, bands), lax.rem(peer, bands)))
        return carry

    lax.fori_loop(1, tiles * bands, greet_all, 0)

    def remote(src, dst, send, recv, peer):
        return pltpu.make_async_remote_copy(
            src_ref=src,
            dst_ref=dst,
            send_sem=send,
            recv_sem=recv,
            device_id=peer,
            device_id_type=MESH,
        )

    def slot_of(dl, db):
        return (dl + 1) * 3 + db + 1

    def map_copy(d):
        dl, db = ways[d]
        return remote(
            maps, near.at[slot_of(-dl, -db)], map_send.at[d], map_recv.at[d], at(dl, db)
        )

    for load in loads[:3]:
        load.wait()
    maps[2] = depth_own[...].astype(jnp.float32)
    for load in loads[3:7]:
        load.wait()
    listed = index.shape[2]
    slots = tiles * cap
    width = data.shape[0]
    kinds_at = -(-total // SUB) * SUB
    data[kinds_at - SUB :] = jnp.zeros((width - kinds_at + SUB, listed), jnp.float32)
    data[0:total] = innovation[...]
    data[kinds_at : kinds_at + 1] = jnp.ones((1, listed), jnp.float32)
    data[kinds_at + 1 : kinds_at + 2] = index[1].astype(jnp.float32)
    data[kinds_at + 2 : kinds_at + 3] = index[2].astype(jnp.float32)
    tile_row = jnp.broadcast_to(index[0].astype(jnp.float32), (listed, listed))
    earlier = iota((listed, listed), 0) < iota((listed, listed), 1)
    same = (tile_row == tile_row.T) & earlier
    rank = jnp.sum(jnp.where(same, 1.0, 0.0), 0, keepdims=True)
    slot = index[0] * cap + rank.astype(jnp.int32)
    chosen = ones_where(iota((slots, listed), 0) == slot)
    packed = jnp.zeros((slots, width), jnp.float32)
    for part in split3(data[...]):
        packed = packed + lax.dot_general(
            chosen, part, (((1,), (1,)), ((), ())), preferred_element_type=jnp.float32
        )
    share = lanes * SUB // cap
    packed = packed.reshape(tiles, cap, width)
    pay[:, 0:cap] = packed[:, :, 0:lanes]
    low = iota((SUB, lanes), 1)
    for n in range(tiles):
        out = packed[n, 0:SUB, lanes:]
        for i in range(1, cap // SUB):
            piece = pltpu.roll(packed[n, SUB * i : SUB * i + SUB, lanes:], share * i, 1)
            out = jnp.where(low >= share * i, piece, out)
        pay[n, cap:] = out
    pl.semaphore_wait(barrier, tiles * bands - 1)
    obs = []
    for k, peer in enumerate(along):
        copy = remote(pay.at[peer[0]], rcv.at[lon], obs_send.at[k], obs_recv.at[k], peer)
        copy.start()
        obs.append(copy)
    for d in (4, 5, 6, 7, 2, 3, 0, 1):
        only(there[ways[d][1]], lambda d=d: map_copy(d).start())
    own = pltpu.make_async_copy(pay.at[lon], rcv.at[lon], own_sem)
    own.start()

    nothing = jnp.zeros(maps.shape, jnp.float32)
    near[slot_of(0, 0)] = maps[...]

    @pl.when(jnp.logical_not(has_s))
    def _():
        for dl in (-1, 0, 1):
            near[slot_of(dl, -1)] = nothing
        for lay in layouts:
            lay.hs[...] = jnp.zeros(lay.hs.shape, jnp.float32)
            for ref in (lay.pw, lay.pe):
                none = jnp.zeros(ref.shape[:2] + (lay.corner,) + ref.shape[3:], jnp.float32)
                ref[:, :, 0 : lay.corner] = none

    @pl.when(jnp.logical_not(has_n))
    def _():
        for dl in (-1, 0, 1):
            near[slot_of(dl, 1)] = nothing
        for lay in layouts:
            lay.hn[...] = jnp.zeros(lay.hn.shape, jnp.float32)
            for ref in (lay.pw, lay.pe):
                none = jnp.zeros(ref.shape[:2] + (lay.corner,) + ref.shape[3:], jnp.float32)
                ref[:, :, lay.packs + lay.corner :] = none

    mom[...] = jnp.zeros(mom.shape, jnp.float32)
    red[...] = jnp.zeros(red.shape, jnp.float32)
    ext[...] = jnp.zeros(ext.shape, jnp.float32)

    for lay in layouts:
        for b in range(lay.blocks):
            for r in (0, deep - 1):
                lay.f[b, r] = jnp.zeros((lay.span, lanes), jnp.float32)
            for c in (0, lay.span - EDGE):
                lay.f[b, :, c : c + EDGE] = jnp.zeros((deep, EDGE, lanes), jnp.float32)
                lay.gain[b, :, c : c + EDGE] = jnp.zeros((rows, EDGE, lanes), jnp.float32)

    for load in loads[7:]:
        load.wait()
    levels = (total - 1) // 2
    rates[...] = jnp.zeros(rates.shape, jnp.float32)
    rates[0:1, 0:total] = sigma[...] * precision[...]
    rates[1:2, 0:total] = sigma[...] * sigma[...] * precision[...]
    coef_lane = iota((SUB, lanes), 1)
    for lay in layouts:
        for b in range(lay.blocks):
            start = lay.first + b * lay.wide
            tile, first = start // lanes, start % lanes
            piece = rates[:, tile * lanes : tile * lanes + lanes]
            out = None
            for g in range(lay.groups):
                move = (lay.wide * g - first) % lanes
                moved = pltpu.roll(piece, move, 1) if move else piece
                out = moved if g == 0 else jnp.where(coef_lane >= lay.wide * g, moved, out)
            lay.coef[b, 1:3] = out[0:2]
            channel = coef_lane[0:1] % lay.wide + start
            level = jnp.where(channel < 2 * levels, channel % levels, 0)
            level = jnp.where(channel < total, level, 2 * levels)
            lay.coef[b, 0:1] = level.astype(jnp.float32)

    own_mask = iota((1, SUB, lanes), 2) % SUB == iota((1, SUB, lanes), 1)
    picked = jnp.where(own_mask, maps[2][:, None, :], 0.0)
    picked = picked.reshape(rows * SUB, lanes).astype(jnp.bfloat16)
    for lay in layouts:
        tiles_of = lay.wide // SUB
        column = iota((lanes, tiles_of * lanes), 0)
        target = iota((lanes, tiles_of * lanes), 1)
        start = target % lanes // lay.wide * lay.wide + target // lanes * SUB
        to_lane = ones_where((column >= start) & (column < start + SUB))
        out = jnp.dot(picked, to_lane, preferred_element_type=jnp.float32)
        for i in range(tiles_of):
            piece = out[:, lanes * i : lanes * i + lanes].reshape(rows, SUB, lanes)
            lay.base[4, PASSES:last, EDGE + SUB * i : EDGE + SUB * i + SUB] = piece

    own.wait()
    for copy in obs:
        copy.wait()
    first_half = rcv[:, 0:cap].reshape(slots, lanes)
    second = []
    for n in range(tiles):
        for i in range(cap // SUB):
            piece = rcv[n, cap:]
            second.append(pltpu.roll(piece, lanes - share * i, 1) if i else piece)
    arrived = jnp.concatenate([first_half, jnp.concatenate(second, 0)], 1)
    arrived = jnp.where(iota((slots, width), 1) < lanes + share, arrived, 0.0)
    columns = arrived[:, kinds_at + 1 : kinds_at + 2]
    picker = ones_where(iota((SUB, width), 1) == iota((SUB, width), 0) + kinds_at + 1)
    turned = lax.dot_general(
        picker,
        arrived.astype(jnp.bfloat16),
        (((1,), (1,)), ((), ())),
        preferred_element_type=jnp.float32,
    )
    pieces = split3(arrived)
    for lay in layouts:
        wide, blocks = lay.wide, lay.blocks
        flat = (blocks + 1) * lanes
        source, goal = iota((width, flat), 0), iota((width, flat), 1)
        channel = goal // lanes * wide + goal % wide + lay.first
        to_flat = ones_where(source == jnp.where(goal < blocks * lanes, channel, kinds_at))
        group = (iota((slots, flat), 1) % lanes // wide * wide).astype(jnp.float32)
        mine = (columns >= group) & (columns < group + wide)
        for i, piece in enumerate(pieces):
            wide_part = jnp.dot(piece, to_flat, preferred_element_type=jnp.float32)
            lay.values[i] = jnp.where(mine, wide_part, 0.0).astype(jnp.bfloat16)
        place = turned[1:2] * wide + turned[0:1] - jnp.floor(turned[0:1] / wide) * wide
        spots = iota((rows * wide, slots), 0).astype(jnp.float32)
        to_cell = ones_where(spots == place)
        own_cols = slice(EDGE, EDGE + wide)
        depths = lay.base[4, PASSES:last, own_cols]

        def cells_of(b, count):
            out = jnp.zeros((rows * wide, lanes), jnp.float32)
            for i in range(count):
                out = out + jnp.dot(
                    to_cell,
                    lay.values[i, :, b * lanes : (b + 1) * lanes],
                    preferred_element_type=jnp.float32,
                )
            return out.reshape(rows, wide, lanes)

        counts = cells_of(blocks, 1)
        for b in range(blocks):
            wet = depths > lay.coef[b, 0:1][None]
            cells = lay.coef[b, 1:2][None] * cells_of(b, 3)
            lay.f[b, PASSES:last, own_cols] = jnp.where(wet, cells, 0.0)
            lay.gain[b, :, own_cols] = jnp.where(wet, lay.coef[b, 2:3][None] * counts, 0.0)

    lane = iota((SUB, lanes), 1)
    subs = iota((SUB, lanes), 0)

    def halo(lay, par, b, d):
        dl, db = ways[d]
        send, recv = lay.send.at[par, b, d], lay.recv.at[par, b, d]
        if dl == 0:
            first = PASSES if db < 0 else last - PASSES
            src = lay.f.at[b, pl.ds(first, PASSES), pl.ds(EDGE, lay.wide)]
            dst = (lay.hn if db < 0 else lay.hs).at[par, b]
        else:
            pack, to = (0, lay.pe) if dl < 0 else (1, lay.pw)
            packs, corner = lay.packs, lay.corner
            if db == 0:
                src = lay.pk.at[b, pack]
                dst = to.at[par, b, pl.ds(corner, packs)]
            else:
                src = lay.pk.at[b, pack, pl.ds(0 if db < 0 else packs - corner, corner)]
                dst = to.at[par, b, pl.ds(packs + corner if db < 0 else 0, corner)]
        return remote(src, dst, send, recv, at(dl, db))

    def emit(lay, par, b):
        wide, groups = lay.wide, lay.groups
        for a in range(lay.packs):
            for side, first, from_lane in ((0, EDGE, 0), (1, wide, lanes - wide)):
                out = None
                for i in range(groups):
                    piece = lay.f[b, PASSES + groups * a + i, first : first + EDGE]
                    move = (wide * i - from_lane) % lanes
                    piece = pltpu.roll(piece, move, 1) if move else piece
                    out = piece if out is None else jnp.where(lane >= wide * i, piece, out)
                lay.pk[b, side, a] = out
        for d in (2, 3, 4, 5, 6, 7, 0, 1):
            only(there[ways[d][1]], lambda d=d: halo(lay, par, b, d).start())

    for lay in layouts:
        for b in range(lay.blocks):
            emit(lay, 0, b)

    for d in range(8):
        dl, db = ways[d]
        only(there[-db], lambda d=d: map_copy(d).wait_recv())
    for d in range(8):
        only(there[ways[d][1]], lambda d=d: map_copy(d).wait_send())

    for m in range(3):
        for side in range(3):
            ext[m, side, 0:PASSES] = near[3 * side, m, rows - PASSES : rows]
            ext[m, side, PASSES:last] = near[3 * side + 1, m]
            ext[m, side, last:deep] = near[3 * side + 2, m, 0:PASSES]
    edge = iota((deep, lanes), 1) == lanes - 1
    east, north, depth = [], [], [ext[2, side, 0:deep] for side in range(3)]
    ahead = [pltpu.roll(ext[2, side], lanes - 1, 1)[0:deep] for side in range(3)]
    for side in range(3):
        moved = ahead[side]
        if side < 2:
            moved = jnp.where(edge, ahead[side + 1], moved)
        east.append(jnp.minimum(depth[side], moved))
        north.append(jnp.minimum(depth[side], ext[2, side, 1 : deep + 1]))
    reach = 3 * lanes
    for lay in layouts:
        column = iota((reach, lay.regs * lanes), 0) - lanes + EDGE
        target = iota((reach, lay.regs * lanes), 1)
        start = target % lanes // lay.wide * lay.wide + target // lanes * SUB
        lay.to_lane = ones_where((column >= start) & (column < start + SUB))
    sub_mask = iota((1, SUB, reach), 2) % SUB == iota((1, SUB, reach), 1)
    kinds = (
        [ext[0, side, 0:deep] for side in range(3)],
        east,
        [ext[1, side, 0:deep] for side in range(3)],
        north,
    )
    for m, kind in enumerate(kinds):
        line = jnp.concatenate(kind, 1)
        parts = [line] if m in (1, 3) else [x.astype(jnp.float32) for x in split3(line)]
        picked = [
            jnp.where(sub_mask, part[:, None, :], 0.0)
            .reshape(deep * SUB, reach)
            .astype(jnp.bfloat16)
            for part in parts
        ]
        for lay in layouts:
            out = jnp.zeros((deep * SUB, lay.regs * lanes), jnp.float32)
            for part in picked:
                out = out + jnp.dot(part, lay.to_lane, preferred_element_type=jnp.float32)
            for i in range(lay.regs):
                piece = out[:, lanes * i : lanes * i + lanes].reshape(deep, SUB, lanes)
                lay.base[m, :, SUB * i : SUB * i + SUB] = piece

    def build(lay, b, carry):
        level = lay.coef[b, 0:1]
        base, regs = lay.base, lay.regs
        for j in range(regs):
            pick = pl.ds(j, SUB, stride=regs)
            for r in range(deep):
                east_wet = base[1, r, pick, :] > level
                north_wet = base[3, r, pick, :] > level
                lay.fe[b, j, r] = jnp.where(east_wet, base[0, r, pick, :], 0.0)
                lay.fn[b, j, r] = jnp.where(north_wet, base[2, r, pick, :], 0.0)
        return carry

    for lay in layouts:
        lax.fori_loop(0, lay.blocks, functools.partial(build, lay), 0)

    everyone = tiles * bands
    me = lon * bands + lat

    def sum_copy(k):
        peer = lax.rem(me + k, everyone)
        return remote(
            red, red_all.at[k - 1], sum_send, sum_recv, (lax.div(peer, bands), lax.rem(peer, bands))
        )

    def one_pass(lay, b, t, finish):
        f, fe, fn, tmp, regs = lay.f, lay.fe, lay.fn, lay.tmp, lay.regs

        def old(j, lo, hi):
            if t == 0:
                return jnp.stack(
                    [f[b, r, pl.ds(j, SUB, stride=regs), :] for r in range(lo, hi)]
                )
            return tmp[(t + 1) % 2, j, lo:hi]

        for lo, hi in chunks(t + 1, deep - 1 - t):
            v = old(0, lo - 1, hi + 1)
            wrap = pltpu.roll(v[1:-1], SUB - 1, 1)
            end = old(regs - 1, lo, hi)
            end = fe[b, regs - 1, lo:hi] * (wrap - end)
            west = pltpu.roll(end, 1, 1)
            for j in range(regs):
                centre = v[1:-1]
                if j < regs - 1:
                    following = old(j + 1, lo - 1, hi + 1)
                    flux = fe[b, j, lo:hi] * (following[1:-1] - centre)
                else:
                    following, flux = None, end
                up = fn[b, j, lo - 1 : hi] * (v[1:] - v[:-1])
                new = centre + ((flux - west) + (up[1:] - up[:-1]))
                if finish is None:
                    tmp[t % 2, j, lo:hi] = new
                else:
                    finish(j, lo, new)
                v, west = following, flux

    def step(lay, e, b):
        par = lax.rem(e, 2)
        odd = par == 1
        f, wide, span, groups = lay.f, lay.wide, lay.span, lay.groups
        own_cols = slice(EDGE, EDGE + wide)
        for d in range(8):
            only(there[-ways[d][1]], lambda d=d: halo(lay, par, b, d).wait_recv())
        f[b, 0:PASSES, own_cols] = lay.hs[par, b]
        f[b, last:deep, own_cols] = lay.hn[par, b]
        for r in range(1, deep - 1):
            a, i = (r - 1) // groups, (r - 1) % groups
            west = pltpu.roll(f[b, r, wide : wide + EDGE], wide, 1)
            far = lay.pw[par, b, a]
            far = pltpu.roll(far, lanes - wide * i, 1) if i else far
            f[b, r, 0:EDGE] = jnp.where(lane < wide, far, west)
            east = pltpu.roll(f[b, r, EDGE : 2 * EDGE], lanes - wide, 1)
            far = lay.pe[par, b, a]
            move = (lanes - wide - wide * i) % lanes
            far = pltpu.roll(far, move, 1) if move else far
            f[b, r, wide + EDGE : span] = jnp.where(lane >= lanes - wide, far, east)
        for t in range(PASSES - 1):
            one_pass(lay, b, t, None)
        for d in range(8):
            only(there[ways[d][1]], lambda d=d: halo(lay, par, b, d).wait_send())

        def finish(j, lo, new):
            pick = pl.ds(j, SUB, stride=lay.regs)
            at_col = subs * lay.regs + j
            own_here = jnp.where((at_col >= EDGE) & (at_col < EDGE + wide), 1.0, 0.0)
            sums = None
            for i in range(new.shape[0]):
                r = lo + i
                weight = jnp.where(odd, lay.gain[b, r - PASSES, pick, :], own_here)
                weighed = new[i] * weight
                square = new[i] * weighed
                sums = square if sums is None else sums + square
                f[b, r, pick, :] = weighed
            mom[e] = mom[e] + sums

        one_pass(lay, b, PASSES - 1, finish)

        @pl.when(e < STAGES - 1)
        def _():
            emit(lay, 1 - par, b)

        @pl.when(jnp.logical_not(odd))
        def _():
            lane_all = iota((wide, lanes), 1)
            for a in range(lay.packs):
                first = PASSES + groups * a
                square = f[b, first : first + groups, own_cols].reshape(lanes, lanes).T
                pieces = [square[wide * g : wide * g + wide] for g in range(groups)]
                half = groups // 2
                while half:
                    move = half * wide
                    low = lane_all // move % 2 == 0
                    for g in range(groups):
                        if g // half % 2 == 0:
                            one, two = pieces[g], pieces[g + half]
                            pieces[g] = jnp.where(low, one, pltpu.roll(two, move, 1))
                            pieces[g + half] = jnp.where(
                                low, pltpu.roll(one, lanes - move, 1), two
                            )
                    half //= 2
                for i in range(groups):
                    begin = (lay.first + b * wide) * rows + groups * a + i
                    v_out[lax.div(e, 2), pl.ds(begin, wide, stride=rows), :] = pieces[i]

    def send_sum(k, carry):
        sum_copy(k).start()
        return carry

    def stage(e, carry):
        for lay in layouts:

            def block(b, carry, lay=lay):
                step(lay, e, b)
                return carry

            lax.fori_loop(0, lay.blocks, block, 0)
        @pl.when(e == STAGES - 2)
        def _():
            for i in range(4):
                red[i : i + 1, :] = jnp.sum(mom[i], 0, keepdims=True)
            lax.fori_loop(1, everyone, send_sum, 0)

        return carry

    lax.fori_loop(0, STAGES, stage, 0)

    total_copy = remote(red_all, red_all, sum_send, sum_recv, at(1, 0))
    total_copy.wait_recv()
    total_copy.wait_send()
    sums = jnp.sum(red[...] + jnp.sum(red_all[...], 0), 1, keepdims=True)
    m0 = sums[0:1]
    x, y, z = sums[1:2] / m0, sums[2:3] / m0, sums[3:4] / m0
    alpha = 1.0 / (1.0 + x)
    beta = (y - x * x) * alpha * alpha
    c0, c1 = 1.0 - alpha + beta, -alpha
    curve = c0 * c0 * (1.0 + x) + 2.0 * c0 * c1 * (x + y) + c1 * c1 * (y + z)
    second = beta / curve
    values = (
        alpha + second * c0,
        second * c1,
        (1.0 - second) * (1.0 - alpha) - second * beta,
        -(1.0 - second) * alpha - second * c0,
        alpha * second,
    )
    for i, value in enumerate(values):
        c_out[i : i + 1, :] = jnp.broadcast_to(value, (1, lanes))


def combine_kernel(block, v, c, increment, residual, held, sems):
    size, lanes = increment.shape
    copies = []
    for n, first in enumerate(range(0, size, block)):
        count = min(block, size - first)
        part = pl.ds(first, count)
        zero, one, two = v[0, part], v[1, part], v[2, part]
        held[0, part] = c[0:1] * zero + c[1:2] * one
        held[1, part] = c[2:3] * zero + c[3:4] * one + c[4:5] * two
        for i, target in enumerate((increment, residual)):
            copy = pltpu.make_async_copy(held.at[i, part], target.at[part], sems.at[i, n])
            copy.start()
            copies.append(copy)
    for copy in copies:
        copy.wait()


def local(
    kappa_east, kappa_north, depth, sigma, obs_precision, obs_tile, obs_col, obs_lat, innovation
):
    rows, lanes = kappa_east.shape
    total = sigma.shape[0]
    tiles, bands = lax.axis_size("lon"), lax.axis_size("lat")
    listed = obs_col.shape[0]
    cap = 2 * listed // tiles
    layouts = layouts_of(total, rows, lanes)
    channels = layouts[-1].first + layouts[-1].blocks * layouts[-1].wide
    width = -(-(-(-total // SUB) * SUB + SUB) // 128) * 128

    deep = rows + 2 * PASSES
    vmem = pl.BlockSpec(memory_space=pltpu.VMEM)
    f32 = jnp.float32
    dma = pltpu.SemaphoreType.DMA
    slots = tiles * cap
    v, c = pl.pallas_call(
        functools.partial(main_kernel, tiles, bands, cap, total),
        out_shape=[
            jax.ShapeDtypeStruct((3, channels * rows, lanes), f32),
            jax.ShapeDtypeStruct((SUB, lanes), f32),
        ],
        in_specs=[pl.BlockSpec(memory_space=pltpu.HBM)] * 9,
        out_specs=[vmem] * 2,
        scratch_shapes=[
            pltpu.VMEM((rows, lanes), jnp.int32),
            pltpu.VMEM((1, total), f32),
            pltpu.VMEM((1, total), f32),
            pltpu.VMEM((3, 1, listed), jnp.int32),
            pltpu.VMEM((total, listed), f32),
            pltpu.VMEM((3, rows, lanes), f32),
            pltpu.VMEM((width, listed), f32),
            pltpu.VMEM((SUB, -(-channels // lanes) * lanes), f32),
            pltpu.VMEM((tiles, cap + SUB, lanes), f32),
            pltpu.VMEM((tiles, cap + SUB, lanes), f32),
            pltpu.VMEM((9, 3, rows, lanes), f32),
            pltpu.VMEM((3, 3, -(-(deep + 1) // SUB) * SUB, lanes), f32),
            pltpu.VMEM((STAGES, SUB, lanes), f32),
            pltpu.VMEM((SUB, lanes), f32),
            pltpu.VMEM((tiles * bands - 1, SUB, lanes), f32),
            dma((tiles - 1,)),
            dma((tiles - 1,)),
            dma((8,)),
            dma((8,)),
            dma,
            dma((9,)),
            dma,
            dma,
        ]
        + [shape for lay in layouts for shape in lay.shapes(slots)],
        compiler_params=pltpu.CompilerParams(
            collective_id=1, has_side_effects=True, vmem_limit_bytes=48 * 1024 * 1024
        ),
        name="smooth_all",
    )(
        *[
            pltpu.with_memory_space_constraint(x, pltpu.HBM)
            for x in (
                kappa_east,
                kappa_north,
                depth,
                sigma.reshape(1, total),
                obs_precision.reshape(1, total),
                obs_tile.reshape(1, listed),
                obs_col.reshape(1, listed),
                obs_lat.reshape(1, listed),
                innovation,
            )
        ]
    )

    block = 4 * SUB * rows
    pieces = -(-total * rows // block)
    increment, residual = pl.pallas_call(
        functools.partial(combine_kernel, block),
        out_shape=[jax.ShapeDtypeStruct((total * rows, lanes), f32)] * 2,
        in_specs=[vmem] * 2,
        out_specs=[pl.BlockSpec(memory_space=pl.ANY)] * 2,
        scratch_shapes=[pltpu.VMEM((2, total * rows, lanes), f32), dma((2, pieces))],
        compiler_params=pltpu.CompilerParams(vmem_limit_bytes=10 * 1024 * 1024),
        name="combine",
    )(v, c)
    shape = (total, rows, lanes)
    return increment.reshape(shape), residual.reshape(shape)


def solution(mesh):
    return jax.shard_map(
        local,
        mesh=mesh,
        in_specs=(
            P("lat", "lon"),
            P("lat", "lon"),
            P("lat", "lon"),
            P(),
            P(),
            P(("lon", "lat"), None),
            P(("lon", "lat")),
            P(("lon", "lat")),
            P(None, ("lon", "lat")),
        ),
        out_specs=(P(None, "lat", "lon"), P(None, "lat", "lon")),
        check_vma=False,
    )
```

```python
import functools

import jax
import jax.numpy as jnp
from jax import lax
from jax.experimental import pallas as pl
from jax.experimental.pallas import tpu as pltpu
from jax.sharding import PartitionSpec as P

MESH = pl.DeviceIdType.MESH
SUB = 8
PASSES = 5
STAGES = 5
EDGE = 8


SCRATCH = ("base", "values", "cell", "coef", "f", "fe", "fn", "tmp", "gain")
SCRATCH += ("hs", "hn", "pw", "pe", "pk", "send", "recv")


class Layout:
    def __init__(self, first, blocks, groups, rows, lanes):
        self.first, self.blocks, self.groups = first, blocks, groups
        self.wide = lanes // groups
        self.span = self.wide + 2 * EDGE
        self.regs = self.span // SUB
        self.packs = rows // groups
        self.corner = (PASSES - 1) // groups
        self.rows, self.lanes = rows, lanes

    def bind(self, refs):
        for name, ref in zip(SCRATCH, refs):
            setattr(self, name, ref)

    def shapes(self, slots):
        f32, dma = jnp.float32, pltpu.SemaphoreType.DMA
        rows, lanes, blocks = self.rows, self.lanes, self.blocks
        deep = rows + 2 * PASSES
        faces = pltpu.VMEM((blocks, self.regs, deep, SUB, lanes), f32)
        beside = pltpu.VMEM((2, blocks, PASSES, self.wide, lanes), f32)
        edge = pltpu.VMEM((2, blocks, self.packs + 2 * self.corner, SUB, lanes), f32)
        return [
            pltpu.VMEM((5, deep, self.span, lanes), f32),
            pltpu.VMEM((3, slots, (blocks + 1) * lanes), jnp.bfloat16),
            pltpu.VMEM((rows * self.wide, slots), jnp.bfloat16),
            pltpu.VMEM((blocks, SUB, lanes), f32),
            pltpu.VMEM((blocks, deep, self.span, lanes), f32),
            faces,
            faces,
            pltpu.VMEM((2, self.regs, deep, SUB, lanes), f32),
            pltpu.VMEM((blocks, rows, self.span, lanes), f32),
            beside,
            beside,
            edge,
            edge,
            pltpu.VMEM((blocks, 2, self.packs, SUB, lanes), f32),
            dma((2, blocks, 8)),
            dma((2, blocks, 8)),
        ]


def layouts_of(total, rows, lanes):
    pairs = total // (lanes // 2)
    left = total - pairs * (lanes // 2)
    out = [Layout(0, pairs, 2, rows, lanes)]
    if left:
        out.append(Layout(pairs * (lanes // 2), -(-left // (lanes // 4)), 4, rows, lanes))
    return out


def split3(x):
    high = x.astype(jnp.bfloat16)
    left = x - high.astype(jnp.float32)
    middle = left.astype(jnp.bfloat16)
    low = (left - middle.astype(jnp.float32)).astype(jnp.bfloat16)
    return high, middle, low


def chunks(first, end, most=8):
    count = -(-(end - first) // most)
    cuts = [first + (end - first) * i // count for i in range(count + 1)]
    return list(zip(cuts[:-1], cuts[1:]))


def iota(shape, dim):
    return lax.broadcasted_iota(jnp.int32, shape, dim)


def ones_where(mask):
    return jnp.where(mask, 1.0, 0.0).astype(jnp.bfloat16)


def main_kernel(
    tiles,
    bands,
    cap,
    total,
    ke_in,
    kn_in,
    depth_in,
    sigma_in,
    precision_in,
    tile_in,
    col_in,
    lat_in,
    innovation_in,
    v_out,
    c_out,
    depth_own,
    sigma,
    precision,
    index,
    innovation,
    maps,
    data,
    rates,
    pay,
    rcv,
    near,
    ext,
    mom,
    red,
    red_pair,
    red_all,
    obs_send,
    obs_recv,
    map_send,
    map_recv,
    own_sem,
    load_sem,
    sum_send,
    sum_recv,
    *rest,
):
    lon, lat = lax.axis_index("lon"), lax.axis_index("lat")
    rows, lanes = maps.shape[1], maps.shape[2]
    deep = rows + 2 * PASSES
    last = rows + PASSES
    layouts = layouts_of(total, rows, lanes)
    for n, lay in enumerate(layouts):
        lay.bind(rest[n * len(SCRATCH) : (n + 1) * len(SCRATCH)])
    has_s, has_n = lat > 0, lat < bands - 1

    def at(dl, db):
        return lax.rem(lon + dl + tiles, tiles), lax.rem(lat + db + bands, bands)

    along = [(lax.rem(lon + k, tiles), lat) for k in range(1, tiles)]
    ways = [(0, -1), (0, 1), (-1, 0), (1, 0), (-1, -1), (1, -1), (-1, 1), (1, 1)]
    there = {-1: has_s, 0: None, 1: has_n}

    def only(cond, body):
        if cond is None:
            body()
        else:
            pl.when(cond)(body)

    loads = [
        pltpu.make_async_copy(src, dst, load_sem.at[i])
        for i, (src, dst) in enumerate(
            (
                (ke_in, maps.at[0]),
                (kn_in, maps.at[1]),
                (depth_in, depth_own),
                (tile_in, index.at[0]),
                (col_in, index.at[1]),
                (lat_in, index.at[2]),
                (innovation_in, innovation),
                (sigma_in, sigma),
                (precision_in, precision),
            )
        )
    ]
    for load in loads:
        load.start()

    barrier = pltpu.get_barrier_semaphore()

    def greet(peer):
        pl.semaphore_signal(barrier, inc=1, device_id=peer, device_id_type=MESH)

    half = bands // 2
    kin = tiles * half
    me = lon * half + lax.div(lat, 2)

    def kin_of(k):
        peer = lax.rem(me + k, kin)
        return lax.div(peer, half), 2 * lax.rem(peer, half) + lax.rem(lat, 2)

    def greet_kin(k, carry):
        greet(kin_of(k))
        return carry

    lax.fori_loop(1, kin, greet_kin, 0)
    for dl, db in ways:
        if db:
            only(there[db], functools.partial(greet, at(dl, db)))

    def remote(src, dst, send, recv, peer):
        return pltpu.make_async_remote_copy(
            src_ref=src,
            dst_ref=dst,
            send_sem=send,
            recv_sem=recv,
            device_id=peer,
            device_id_type=MESH,
        )

    def slot_of(dl, db):
        return (dl + 1) * 3 + db + 1

    def map_copy(d):
        dl, db = ways[d]
        return remote(
            maps, near.at[slot_of(-dl, -db)], map_send.at[d], map_recv.at[d], at(dl, db)
        )

    for load in loads[:3]:
        load.wait()
    maps[2] = depth_own[...].astype(jnp.float32)
    for load in loads[3:7]:
        load.wait()
    listed = index.shape[2]
    slots = tiles * cap
    width = data.shape[0]
    kinds_at = -(-total // SUB) * SUB
    data[kinds_at - SUB :] = jnp.zeros((width - kinds_at + SUB, listed), jnp.float32)
    data[0:total] = innovation[...]
    data[kinds_at : kinds_at + 1] = jnp.ones((1, listed), jnp.float32)
    data[kinds_at + 1 : kinds_at + 2] = index[1].astype(jnp.float32)
    data[kinds_at + 2 : kinds_at + 3] = index[2].astype(jnp.float32)
    tile_row = jnp.broadcast_to(index[0].astype(jnp.float32), (listed, listed))
    earlier = iota((listed, listed), 0) < iota((listed, listed), 1)
    same = (tile_row == tile_row.T) & earlier
    rank = jnp.sum(jnp.where(same, 1.0, 0.0), 0, keepdims=True)
    slot = index[0] * cap + rank.astype(jnp.int32)
    chosen = ones_where(iota((slots, listed), 0) == slot)
    packed = jnp.zeros((slots, width), jnp.float32)
    for part in split3(data[...]):
        packed = packed + lax.dot_general(
            chosen, part, (((1,), (1,)), ((), ())), preferred_element_type=jnp.float32
        )
    share = lanes * SUB // cap
    packed = packed.reshape(tiles, cap, width)
    pay[:, 0:cap] = packed[:, :, 0:lanes]
    low = iota((SUB, lanes), 1)
    for n in range(tiles):
        out = packed[n, 0:SUB, lanes:]
        for i in range(1, cap // SUB):
            piece = pltpu.roll(packed[n, SUB * i : SUB * i + SUB, lanes:], share * i, 1)
            out = jnp.where(low >= share * i, piece, out)
        pay[n, cap:] = out
    greeted = jnp.where(has_s, 3, 0) + jnp.where(has_n, 3, 0)
    pl.semaphore_wait(barrier, kin - 1 + greeted)
    obs = []
    for k, peer in enumerate(along):
        copy = remote(pay.at[peer[0]], rcv.at[lon], obs_send.at[k], obs_recv.at[k], peer)
        copy.start()
        obs.append(copy)
    for d in (4, 5, 6, 7, 2, 3, 0, 1):
        only(there[ways[d][1]], lambda d=d: map_copy(d).start())
    own = pltpu.make_async_copy(pay.at[lon], rcv.at[lon], own_sem)
    own.start()

    nothing = jnp.zeros(maps.shape, jnp.float32)
    near[slot_of(0, 0)] = maps[...]

    @pl.when(jnp.logical_not(has_s))
    def _():
        for dl in (-1, 0, 1):
            near[slot_of(dl, -1)] = nothing
        for lay in layouts:
            lay.hs[...] = jnp.zeros(lay.hs.shape, jnp.float32)
            for ref in (lay.pw, lay.pe):
                none = jnp.zeros(ref.shape[:2] + (lay.corner,) + ref.shape[3:], jnp.float32)
                ref[:, :, 0 : lay.corner] = none

    @pl.when(jnp.logical_not(has_n))
    def _():
        for dl in (-1, 0, 1):
            near[slot_of(dl, 1)] = nothing
        for lay in layouts:
            lay.hn[...] = jnp.zeros(lay.hn.shape, jnp.float32)
            for ref in (lay.pw, lay.pe):
                none = jnp.zeros(ref.shape[:2] + (lay.corner,) + ref.shape[3:], jnp.float32)
                ref[:, :, lay.packs + lay.corner :] = none

    mom[...] = jnp.zeros(mom.shape, jnp.float32)
    red[...] = jnp.zeros(red.shape, jnp.float32)
    ext[...] = jnp.zeros(ext.shape, jnp.float32)

    for lay in layouts:
        for b in range(lay.blocks):
            for r in (0, deep - 1):
                lay.f[b, r] = jnp.zeros((lay.span, lanes), jnp.float32)
            for c in (0, lay.span - EDGE):
                lay.f[b, :, c : c + EDGE] = jnp.zeros((deep, EDGE, lanes), jnp.float32)
                lay.gain[b, :, c : c + EDGE] = jnp.zeros((rows, EDGE, lanes), jnp.float32)

    for load in loads[7:]:
        load.wait()
    levels = (total - 1) // 2
    rates[...] = jnp.zeros(rates.shape, jnp.float32)
    rates[0:1, 0:total] = sigma[...] * precision[...]
    rates[1:2, 0:total] = sigma[...] * sigma[...] * precision[...]
    coef_lane = iota((SUB, lanes), 1)
    for lay in layouts:
        for b in range(lay.blocks):
            start = lay.first + b * lay.wide
            tile, first = start // lanes, start % lanes
            piece = rates[:, tile * lanes : tile * lanes + lanes]
            out = None
            for g in range(lay.groups):
                move = (lay.wide * g - first) % lanes
                moved = pltpu.roll(piece, move, 1) if move else piece
                out = moved if g == 0 else jnp.where(coef_lane >= lay.wide * g, moved, out)
            lay.coef[b, 1:3] = out[0:2]
            channel = coef_lane[0:1] % lay.wide + start
            level = jnp.where(channel < 2 * levels, channel % levels, 0)
            level = jnp.where(channel < total, level, 2 * levels)
            lay.coef[b, 0:1] = level.astype(jnp.float32)

    own_mask = iota((1, SUB, lanes), 2) % SUB == iota((1, SUB, lanes), 1)
    picked = jnp.where(own_mask, maps[2][:, None, :], 0.0)
    picked = picked.reshape(rows * SUB, lanes).astype(jnp.bfloat16)
    for lay in layouts:
        tiles_of = lay.wide // SUB
        column = iota((lanes, tiles_of * lanes), 0)
        target = iota((lanes, tiles_of * lanes), 1)
        start = target % lanes // lay.wide * lay.wide + target // lanes * SUB
        to_lane = ones_where((column >= start) & (column < start + SUB))
        out = jnp.dot(picked, to_lane, preferred_element_type=jnp.float32)
        for i in range(tiles_of):
            piece = out[:, lanes * i : lanes * i + lanes].reshape(rows, SUB, lanes)
            lay.base[4, PASSES:last, EDGE + SUB * i : EDGE + SUB * i + SUB] = piece

    for lay in layouts:
        flat = (lay.blocks + 1) * lanes
        source, goal = iota((width, flat), 0), iota((width, flat), 1)
        channel = goal // lanes * lay.wide + goal % lay.wide + lay.first
        channel = jnp.where(goal < lay.blocks * lanes, channel, kinds_at)
        lay.to_flat = ones_where(source == channel)

    own.wait()
    for copy in obs:
        copy.wait()
    def cells_of(lay, first, end, count):
        out = None
        for i in range(count):
            part = jnp.dot(
                lay.cell[...],
                lay.values[i, :, first * lanes : end * lanes],
                preferred_element_type=jnp.float32,
            )
            out = part if i == 0 else out + part
        return [
            out[:, n * lanes : (n + 1) * lanes].reshape(rows, lay.wide, lanes)
            for n in range(end - first)
        ]

    first_half = rcv[:, 0:cap].reshape(slots, lanes)
    second = []
    for n in range(tiles):
        for i in range(cap // SUB):
            piece = rcv[n, cap:]
            second.append(pltpu.roll(piece, lanes - share * i, 1) if i else piece)
    arrived = jnp.concatenate([first_half, jnp.concatenate(second, 0)], 1)
    arrived = jnp.where(iota((slots, width), 1) < lanes + share, arrived, 0.0)
    columns = arrived[:, kinds_at + 1 : kinds_at + 2]
    picker = ones_where(iota((SUB, width), 1) == iota((SUB, width), 0) + kinds_at + 1)
    turned = lax.dot_general(
        picker,
        arrived.astype(jnp.bfloat16),
        (((1,), (1,)), ((), ())),
        preferred_element_type=jnp.float32,
    )
    pieces = split3(arrived)
    for lay in layouts:
        wide, blocks = lay.wide, lay.blocks
        flat = (blocks + 1) * lanes
        group = (iota((slots, flat), 1) % lanes // wide * wide).astype(jnp.float32)
        mine = (columns >= group) & (columns < group + wide)
        for i, piece in enumerate(pieces):
            wide_part = jnp.dot(piece, lay.to_flat, preferred_element_type=jnp.float32)
            lay.values[i] = jnp.where(mine, wide_part, 0.0).astype(jnp.bfloat16)
        place = turned[1:2] * wide + turned[0:1] - jnp.floor(turned[0:1] / wide) * wide
        spots = iota((rows * wide, slots), 0).astype(jnp.float32)
        lay.cell[...] = ones_where(spots == place)
        own_cols = slice(EDGE, EDGE + wide)
        depths = lay.base[4, PASSES:last, own_cols]
        for b, cells in enumerate(cells_of(lay, 0, blocks, 3)):
            wet = depths > lay.coef[b, 0:1][None]
            cells = lay.coef[b, 1:2][None] * cells
            lay.f[b, PASSES:last, own_cols] = jnp.where(wet, cells, 0.0)

    lane = iota((SUB, lanes), 1)
    subs = iota((SUB, lanes), 0)

    def halo(lay, par, b, d):
        dl, db = ways[d]
        send, recv = lay.send.at[par, b, d], lay.recv.at[par, b, d]
        if dl == 0:
            first = PASSES if db < 0 else last - PASSES
            src = lay.f.at[b, pl.ds(first, PASSES), pl.ds(EDGE, lay.wide)]
            dst = (lay.hn if db < 0 else lay.hs).at[par, b]
        else:
            pack, to = (0, lay.pe) if dl < 0 else (1, lay.pw)
            packs, corner = lay.packs, lay.corner
            if db == 0:
                src = lay.pk.at[b, pack]
                dst = to.at[par, b, pl.ds(corner, packs)]
            else:
                src = lay.pk.at[b, pack, pl.ds(0 if db < 0 else packs - corner, corner)]
                dst = to.at[par, b, pl.ds(packs + corner if db < 0 else 0, corner)]
        return remote(src, dst, send, recv, at(dl, db))

    def emit(lay, par, b):
        wide, groups = lay.wide, lay.groups
        for a in range(lay.packs):
            for side, first, from_lane in ((0, EDGE, 0), (1, wide, lanes - wide)):
                out = None
                for i in range(groups):
                    piece = lay.f[b, PASSES + groups * a + i, first : first + EDGE]
                    move = (wide * i - from_lane) % lanes
                    piece = pltpu.roll(piece, move, 1) if move else piece
                    out = piece if out is None else jnp.where(lane >= wide * i, piece, out)
                lay.pk[b, side, a] = out
        for d in (2, 3, 4, 5, 6, 7, 0, 1):
            only(there[ways[d][1]], lambda d=d: halo(lay, par, b, d).start())

    for lay in layouts:
        for b in range(lay.blocks):
            emit(lay, 0, b)

    for lay in layouts:
        own_cols = slice(EDGE, EDGE + lay.wide)
        depths = lay.base[4, PASSES:last, own_cols]
        counts = cells_of(lay, lay.blocks, lay.blocks + 1, 1)[0]
        for b in range(lay.blocks):
            wet = depths > lay.coef[b, 0:1][None]
            lay.gain[b, :, own_cols] = jnp.where(wet, lay.coef[b, 2:3][None] * counts, 0.0)

    for d in range(8):
        dl, db = ways[d]
        only(there[-db], lambda d=d: map_copy(d).wait_recv())
    for d in range(8):
        only(there[ways[d][1]], lambda d=d: map_copy(d).wait_send())

    for m in range(3):
        for side in range(3):
            ext[m, side, 0:PASSES] = near[3 * side, m, rows - PASSES : rows]
            ext[m, side, PASSES:last] = near[3 * side + 1, m]
            ext[m, side, last:deep] = near[3 * side + 2, m, 0:PASSES]
    edge = iota((deep, lanes), 1) == lanes - 1
    east, north, depth = [], [], [ext[2, side, 0:deep] for side in range(3)]
    ahead = [pltpu.roll(ext[2, side], lanes - 1, 1)[0:deep] for side in range(3)]
    for side in range(3):
        moved = ahead[side]
        if side < 2:
            moved = jnp.where(edge, ahead[side + 1], moved)
        east.append(jnp.minimum(depth[side], moved))
        north.append(jnp.minimum(depth[side], ext[2, side, 1 : deep + 1]))
    reach = 3 * lanes
    for lay in layouts:
        column = iota((reach, lay.regs * lanes), 0) - lanes + EDGE
        target = iota((reach, lay.regs * lanes), 1)
        start = target % lanes // lay.wide * lay.wide + target // lanes * SUB
        lay.to_lane = ones_where((column >= start) & (column < start + SUB))
    sub_mask = iota((1, SUB, reach), 2) % SUB == iota((1, SUB, reach), 1)
    kinds = (
        [ext[0, side, 0:deep] for side in range(3)],
        east,
        [ext[1, side, 0:deep] for side in range(3)],
        north,
    )
    for m, kind in enumerate(kinds):
        line = jnp.concatenate(kind, 1)
        parts = [line] if m in (1, 3) else [x.astype(jnp.float32) for x in split3(line)]
        picked = [
            jnp.where(sub_mask, part[:, None, :], 0.0)
            .reshape(deep * SUB, reach)
            .astype(jnp.bfloat16)
            for part in parts
        ]
        for lay in layouts:
            out = jnp.zeros((deep * SUB, lay.regs * lanes), jnp.float32)
            for part in picked:
                out = out + jnp.dot(part, lay.to_lane, preferred_element_type=jnp.float32)
            for i in range(lay.regs):
                piece = out[:, lanes * i : lanes * i + lanes].reshape(deep, SUB, lanes)
                lay.base[m, :, SUB * i : SUB * i + SUB] = piece

    def build(lay, b, carry):
        level = lay.coef[b, 0:1]
        base, regs = lay.base, lay.regs
        for j in range(regs):
            pick = pl.ds(j, SUB, stride=regs)
            for r in range(deep):
                east_wet = base[1, r, pick, :] > level
                north_wet = base[3, r, pick, :] > level
                lay.fe[b, j, r] = jnp.where(east_wet, base[0, r, pick, :], 0.0)
                lay.fn[b, j, r] = jnp.where(north_wet, base[2, r, pick, :], 0.0)
        return carry

    for lay in layouts:
        lax.fori_loop(0, lay.blocks, functools.partial(build, lay), 0)

    def pair_copy():
        partner = lat + 1 - 2 * lax.rem(lat, 2)
        return remote(red, red_pair, sum_send.at[0], sum_recv.at[0], (lon, partner))

    def sum_copy(k):
        return remote(red, red_all.at[k - 1], sum_send.at[1], sum_recv.at[1], kin_of(k))

    def one_pass(lay, b, t, finish):
        f, fe, fn, tmp, regs = lay.f, lay.fe, lay.fn, lay.tmp, lay.regs

        def old(j, lo, hi):
            if t == 0:
                return jnp.stack(
                    [f[b, r, pl.ds(j, SUB, stride=regs), :] for r in range(lo, hi)]
                )
            return tmp[(t + 1) % 2, j, lo:hi]

        for lo, hi in chunks(t + 1, deep - 1 - t):
            v = old(0, lo - 1, hi + 1)
            wrap = pltpu.roll(v[1:-1], SUB - 1, 1)
            end = old(regs - 1, lo, hi)
            end = fe[b, regs - 1, lo:hi] * (wrap - end)
            west = pltpu.roll(end, 1, 1)
            for j in range(regs):
                centre = v[1:-1]
                if j < regs - 1:
                    following = old(j + 1, lo - 1, hi + 1)
                    flux = fe[b, j, lo:hi] * (following[1:-1] - centre)
                else:
                    following, flux = None, end
                up = fn[b, j, lo - 1 : hi] * (v[1:] - v[:-1])
                new = centre + ((flux - west) + (up[1:] - up[:-1]))
                if finish is None:
                    tmp[t % 2, j, lo:hi] = new
                else:
                    finish(j, lo, new)
                v, west = following, flux

    def step(lay, e, b):
        par = lax.rem(e, 2)
        odd = par == 1
        f, wide, span, groups = lay.f, lay.wide, lay.span, lay.groups
        own_cols = slice(EDGE, EDGE + wide)
        for d in range(8):
            only(there[-ways[d][1]], lambda d=d: halo(lay, par, b, d).wait_recv())
        f[b, 0:PASSES, own_cols] = lay.hs[par, b]
        f[b, last:deep, own_cols] = lay.hn[par, b]
        for r in range(1, deep - 1):
            a, i = (r - 1) // groups, (r - 1) % groups
            west = pltpu.roll(f[b, r, wide : wide + EDGE], wide, 1)
            far = lay.pw[par, b, a]
            far = pltpu.roll(far, lanes - wide * i, 1) if i else far
            f[b, r, 0:EDGE] = jnp.where(lane < wide, far, west)
            east = pltpu.roll(f[b, r, EDGE : 2 * EDGE], lanes - wide, 1)
            far = lay.pe[par, b, a]
            move = (lanes - wide - wide * i) % lanes
            far = pltpu.roll(far, move, 1) if move else far
            f[b, r, wide + EDGE : span] = jnp.where(lane >= lanes - wide, far, east)
        for t in range(PASSES - 1):
            one_pass(lay, b, t, None)
        for d in range(8):
            only(there[ways[d][1]], lambda d=d: halo(lay, par, b, d).wait_send())

        def finish(j, lo, new):
            pick = pl.ds(j, SUB, stride=lay.regs)
            at_col = subs * lay.regs + j
            own_here = jnp.where((at_col >= EDGE) & (at_col < EDGE + wide), 1.0, 0.0)
            sums = None
            for i in range(new.shape[0]):
                r = lo + i
                weight = jnp.where(odd, lay.gain[b, r - PASSES, pick, :], own_here)
                weighed = new[i] * weight
                square = new[i] * weighed
                sums = square if sums is None else sums + square
                f[b, r, pick, :] = weighed
            mom[e] = mom[e] + sums

        one_pass(lay, b, PASSES - 1, finish)

        @pl.when(e < STAGES - 1)
        def _():
            emit(lay, 1 - par, b)

        @pl.when(jnp.logical_not(odd))
        def _():
            lane_all = iota((wide, lanes), 1)
            for a in range(lay.packs):
                first = PASSES + groups * a
                square = f[b, first : first + groups, own_cols].reshape(lanes, lanes).T
                pieces = [square[wide * g : wide * g + wide] for g in range(groups)]
                half = groups // 2
                while half:
                    move = half * wide
                    low = lane_all // move % 2 == 0
                    for g in range(groups):
                        if g // half % 2 == 0:
                            one, two = pieces[g], pieces[g + half]
                            pieces[g] = jnp.where(low, one, pltpu.roll(two, move, 1))
                            pieces[g + half] = jnp.where(
                                low, pltpu.roll(one, lanes - move, 1), two
                            )
                    half //= 2
                for i in range(groups):
                    begin = (lay.first + b * wide) * rows + groups * a + i
                    v_out[lax.div(e, 2), pl.ds(begin, wide, stride=rows), :] = pieces[i]

    def send_sum(k, carry):
        sum_copy(k).start()
        return carry

    def stage(e, carry):
        for lay in layouts:

            def block(b, carry, lay=lay):
                step(lay, e, b)
                if lay is layouts[0]:

                    @pl.when((e == STAGES - 1) & (b == 0))
                    def _():
                        pair_copy().wait()
                        red[...] = red[...] + red_pair[...]
                        lax.fori_loop(1, kin, send_sum, 0)

                return carry

            lax.fori_loop(0, lay.blocks, block, 0)
        @pl.when(e == STAGES - 2)
        def _():
            for i in range(4):
                red[i : i + 1, :] = jnp.sum(mom[i], 0, keepdims=True)
            pair_copy().start()

        return carry

    lax.fori_loop(0, STAGES, stage, 0)

    total_copy = remote(red_all, red_all, sum_send.at[1], sum_recv.at[1], at(1, 0))
    total_copy.wait_recv()
    total_copy.wait_send()
    sums = jnp.sum(red[...] + jnp.sum(red_all[...], 0), 1, keepdims=True)
    m0 = sums[0:1]
    x, y, z = sums[1:2] / m0, sums[2:3] / m0, sums[3:4] / m0
    alpha = 1.0 / (1.0 + x)
    beta = (y - x * x) * alpha * alpha
    c0, c1 = 1.0 - alpha + beta, -alpha
    curve = c0 * c0 * (1.0 + x) + 2.0 * c0 * c1 * (x + y) + c1 * c1 * (y + z)
    second = beta / curve
    values = (
        alpha + second * c0,
        second * c1,
        (1.0 - second) * (1.0 - alpha) - second * beta,
        -(1.0 - second) * alpha - second * c0,
        alpha * second,
    )
    for i, value in enumerate(values):
        c_out[i : i + 1, :] = jnp.broadcast_to(value, (1, lanes))


def combine_kernel(block, v, c, increment, residual, held, sems):
    size, lanes = increment.shape
    copies = []
    for n, first in enumerate(range(0, size, block)):
        count = min(block, size - first)
        part = pl.ds(first, count)
        zero, one, two = v[0, part], v[1, part], v[2, part]
        held[0, part] = c[0:1] * zero + c[1:2] * one
        held[1, part] = c[2:3] * zero + c[3:4] * one + c[4:5] * two
        for i, target in enumerate((increment, residual)):
            copy = pltpu.make_async_copy(held.at[i, part], target.at[part], sems.at[i, n])
            copy.start()
            copies.append(copy)
    for copy in copies:
        copy.wait()


def local(
    kappa_east, kappa_north, depth, sigma, obs_precision, obs_tile, obs_col, obs_lat, innovation
):
    rows, lanes = kappa_east.shape
    total = sigma.shape[0]
    tiles, bands = lax.axis_size("lon"), lax.axis_size("lat")
    listed = obs_col.shape[0]
    cap = 2 * listed // tiles
    layouts = layouts_of(total, rows, lanes)
    channels = layouts[-1].first + layouts[-1].blocks * layouts[-1].wide
    width = -(-(-(-total // SUB) * SUB + SUB) // 128) * 128

    deep = rows + 2 * PASSES
    vmem = pl.BlockSpec(memory_space=pltpu.VMEM)
    f32 = jnp.float32
    dma = pltpu.SemaphoreType.DMA
    slots = tiles * cap
    v, c = pl.pallas_call(
        functools.partial(main_kernel, tiles, bands, cap, total),
        out_shape=[
            jax.ShapeDtypeStruct((3, channels * rows, lanes), f32),
            jax.ShapeDtypeStruct((SUB, lanes), f32),
        ],
        in_specs=[pl.BlockSpec(memory_space=pltpu.HBM)] * 9,
        out_specs=[vmem] * 2,
        scratch_shapes=[
            pltpu.VMEM((rows, lanes), jnp.int32),
            pltpu.VMEM((1, total), f32),
            pltpu.VMEM((1, total), f32),
            pltpu.VMEM((3, 1, listed), jnp.int32),
            pltpu.VMEM((total, listed), f32),
            pltpu.VMEM((3, rows, lanes), f32),
            pltpu.VMEM((width, listed), f32),
            pltpu.VMEM((SUB, -(-channels // lanes) * lanes), f32),
            pltpu.VMEM((tiles, cap + SUB, lanes), f32),
            pltpu.VMEM((tiles, cap + SUB, lanes), f32),
            pltpu.VMEM((9, 3, rows, lanes), f32),
            pltpu.VMEM((3, 3, -(-(deep + 1) // SUB) * SUB, lanes), f32),
            pltpu.VMEM((STAGES, SUB, lanes), f32),
            pltpu.VMEM((SUB, lanes), f32),
            pltpu.VMEM((SUB, lanes), f32),
            pltpu.VMEM((tiles * bands // 2 - 1, SUB, lanes), f32),
            dma((tiles - 1,)),
            dma((tiles - 1,)),
            dma((8,)),
            dma((8,)),
            dma,
            dma((9,)),
            dma((2,)),
            dma((2,)),
        ]
        + [shape for lay in layouts for shape in lay.shapes(slots)],
        compiler_params=pltpu.CompilerParams(
            collective_id=1, has_side_effects=True, vmem_limit_bytes=48 * 1024 * 1024
        ),
        name="smooth_all",
    )(
        *[
            pltpu.with_memory_space_constraint(x, pltpu.HBM)
            for x in (
                kappa_east,
                kappa_north,
                depth,
                sigma.reshape(1, total),
                obs_precision.reshape(1, total),
                obs_tile.reshape(1, listed),
                obs_col.reshape(1, listed),
                obs_lat.reshape(1, listed),
                innovation,
            )
        ]
    )

    block = 4 * SUB * rows
    pieces = -(-total * rows // block)
    increment, residual = pl.pallas_call(
        functools.partial(combine_kernel, block),
        out_shape=[jax.ShapeDtypeStruct((total * rows, lanes), f32)] * 2,
        in_specs=[vmem] * 2,
        out_specs=[pl.BlockSpec(memory_space=pl.ANY)] * 2,
        scratch_shapes=[pltpu.VMEM((2, total * rows, lanes), f32), dma((2, pieces))],
        compiler_params=pltpu.CompilerParams(vmem_limit_bytes=10 * 1024 * 1024),
        name="combine",
    )(v, c)
    shape = (total, rows, lanes)
    return increment.reshape(shape), residual.reshape(shape)


def solution(mesh):
    return jax.shard_map(
        local,
        mesh=mesh,
        in_specs=(
            P("lat", "lon"),
            P("lat", "lon"),
            P("lat", "lon"),
            P(),
            P(),
            P(("lon", "lat"), None),
            P(("lon", "lat")),
            P(("lon", "lat")),
            P(None, ("lon", "lat")),
        ),
        out_specs=(P(None, "lat", "lon"), P(None, "lat", "lon")),
        check_vma=False,
    )
```

```python
import functools

import jax
import jax.numpy as jnp
from jax import lax
from jax.experimental import pallas as pl
from jax.experimental.pallas import tpu as pltpu
from jax.sharding import PartitionSpec as P

MESH = pl.DeviceIdType.MESH
SUB = 8
PASSES = 5
STAGES = 5
EDGE = 8


SCRATCH = ("base", "values", "cell", "coef", "f", "fe", "fn", "tmp", "gain")
SCRATCH += ("hs", "hn", "pw", "pe", "pk", "send", "recv")


class Layout:
    def __init__(self, first, blocks, groups, rows, lanes):
        self.first, self.blocks, self.groups = first, blocks, groups
        self.wide = lanes // groups
        self.span = self.wide + 2 * EDGE
        self.regs = self.span // SUB
        self.packs = rows // groups
        self.corner = (PASSES - 1) // groups
        self.rows, self.lanes = rows, lanes

    def bind(self, refs):
        for name, ref in zip(SCRATCH, refs):
            setattr(self, name, ref)

    def shapes(self, slots):
        f32, dma = jnp.float32, pltpu.SemaphoreType.DMA
        rows, lanes, blocks = self.rows, self.lanes, self.blocks
        deep = rows + 2 * PASSES
        faces = pltpu.VMEM((blocks, self.regs, deep, SUB, lanes), f32)
        beside = pltpu.VMEM((2, blocks, PASSES, self.wide, lanes), f32)
        edge = pltpu.VMEM((2, blocks, self.packs + 2 * self.corner, SUB, lanes), f32)
        return [
            pltpu.VMEM((5, deep, self.span, lanes), f32),
            pltpu.VMEM((3, slots, (blocks + 1) * lanes), jnp.bfloat16),
            pltpu.VMEM((rows * self.wide, slots), jnp.bfloat16),
            pltpu.VMEM((blocks, SUB, lanes), f32),
            pltpu.VMEM((blocks, deep, self.span, lanes), f32),
            faces,
            faces,
            pltpu.VMEM((2, self.regs, deep, SUB, lanes), f32),
            pltpu.VMEM((blocks, rows, self.span, lanes), f32),
            beside,
            beside,
            edge,
            edge,
            pltpu.VMEM((blocks, 2, self.packs, SUB, lanes), f32),
            dma((2, blocks, 8)),
            dma((2, blocks, 8)),
        ]


def layouts_of(total, rows, lanes):
    pairs = total // (lanes // 2)
    left = total - pairs * (lanes // 2)
    out = [Layout(0, pairs, 2, rows, lanes)]
    if left:
        out.append(Layout(pairs * (lanes // 2), -(-left // (lanes // 4)), 4, rows, lanes))
    return out


def split3(x):
    high = x.astype(jnp.bfloat16)
    left = x - high.astype(jnp.float32)
    middle = left.astype(jnp.bfloat16)
    low = (left - middle.astype(jnp.float32)).astype(jnp.bfloat16)
    return high, middle, low


def chunks(first, end, most=5):
    count = -(-(end - first) // most)
    cuts = [first + (end - first) * i // count for i in range(count + 1)]
    return list(zip(cuts[:-1], cuts[1:]))


def iota(shape, dim):
    return lax.broadcasted_iota(jnp.int32, shape, dim)


def ones_where(mask):
    return jnp.where(mask, 1.0, 0.0).astype(jnp.bfloat16)


def main_kernel(
    tiles,
    bands,
    cap,
    total,
    ke_in,
    kn_in,
    depth_in,
    sigma_in,
    precision_in,
    tile_in,
    col_in,
    lat_in,
    innovation_in,
    v_out,
    c_out,
    depth_own,
    sigma,
    precision,
    index,
    innovation,
    maps,
    data,
    rates,
    pay,
    rcv,
    near,
    ext,
    mom,
    red,
    red_pair,
    red_all,
    obs_send,
    obs_recv,
    map_send,
    map_recv,
    own_sem,
    load_sem,
    sum_send,
    sum_recv,
    *rest,
):
    lon, lat = lax.axis_index("lon"), lax.axis_index("lat")
    rows, lanes = maps.shape[1], maps.shape[2]
    deep = rows + 2 * PASSES
    last = rows + PASSES
    layouts = layouts_of(total, rows, lanes)
    for n, lay in enumerate(layouts):
        lay.bind(rest[n * len(SCRATCH) : (n + 1) * len(SCRATCH)])
    has_s, has_n = lat > 0, lat < bands - 1

    def at(dl, db):
        return lax.rem(lon + dl + tiles, tiles), lax.rem(lat + db + bands, bands)

    along = [(lax.rem(lon + k, tiles), lat) for k in sorted(range(1, tiles), key=lambda k: abs(2 * k - tiles))]
    ways = [(0, -1), (0, 1), (-1, 0), (1, 0), (-1, -1), (1, -1), (-1, 1), (1, 1)]
    there = {-1: has_s, 0: None, 1: has_n}

    def only(cond, body):
        if cond is None:
            body()
        else:
            pl.when(cond)(body)

    loads = [
        pltpu.make_async_copy(src, dst, load_sem.at[i])
        for i, (src, dst) in enumerate(
            (
                (ke_in, maps.at[0]),
                (kn_in, maps.at[1]),
                (depth_in, depth_own),
                (tile_in, index.at[0]),
                (col_in, index.at[1]),
                (lat_in, index.at[2]),
                (innovation_in, innovation),
                (sigma_in, sigma),
                (precision_in, precision),
            )
        )
    ]
    for load in loads:
        load.start()

    barrier = pltpu.get_barrier_semaphore()

    def greet(peer):
        pl.semaphore_signal(barrier, inc=1, device_id=peer, device_id_type=MESH)

    half = bands // 2
    kin = tiles * half
    me = lon * half + lax.div(lat, 2)

    def kin_of(k):
        peer = lax.rem(me + k, kin)
        return lax.div(peer, half), 2 * lax.rem(peer, half) + lax.rem(lat, 2)

    def greet_kin(k, carry):
        greet(kin_of(k))
        return carry

    lax.fori_loop(1, kin, greet_kin, 0)
    for dl, db in ways:
        if db:
            only(there[db], functools.partial(greet, at(dl, db)))

    def remote(src, dst, send, recv, peer):
        return pltpu.make_async_remote_copy(
            src_ref=src,
            dst_ref=dst,
            send_sem=send,
            recv_sem=recv,
            device_id=peer,
            device_id_type=MESH,
        )

    def slot_of(dl, db):
        return (dl + 1) * 3 + db + 1

    def map_copy(d):
        dl, db = ways[d]
        return remote(
            maps, near.at[slot_of(-dl, -db)], map_send.at[d], map_recv.at[d], at(dl, db)
        )

    for load in loads[:3]:
        load.wait()
    maps[2] = depth_own[...].astype(jnp.float32)
    for load in loads[3:7]:
        load.wait()
    listed = index.shape[2]
    slots = tiles * cap
    width = data.shape[0]
    kinds_at = -(-total // SUB) * SUB
    data[kinds_at - SUB :] = jnp.zeros((width - kinds_at + SUB, listed), jnp.float32)
    data[0:total] = innovation[...]
    data[kinds_at : kinds_at + 1] = jnp.ones((1, listed), jnp.float32)
    data[kinds_at + 1 : kinds_at + 2] = index[1].astype(jnp.float32)
    data[kinds_at + 2 : kinds_at + 3] = index[2].astype(jnp.float32)
    tile_row = jnp.broadcast_to(index[0].astype(jnp.float32), (listed, listed))
    earlier = iota((listed, listed), 0) < iota((listed, listed), 1)
    same = (tile_row == tile_row.T) & earlier
    rank = jnp.sum(jnp.where(same, 1.0, 0.0), 0, keepdims=True)
    slot = index[0] * cap + rank.astype(jnp.int32)
    chosen = ones_where(iota((slots, listed), 0) == slot)
    packed = jnp.zeros((slots, width), jnp.float32)
    for part in split3(data[...]):
        packed = packed + lax.dot_general(
            chosen, part, (((1,), (1,)), ((), ())), preferred_element_type=jnp.float32
        )
    share = lanes * SUB // cap
    packed = packed.reshape(tiles, cap, width)
    pay[:, 0:cap] = packed[:, :, 0:lanes]
    low = iota((SUB, lanes), 1)
    for n in range(tiles):
        out = packed[n, 0:SUB, lanes:]
        for i in range(1, cap // SUB):
            piece = pltpu.roll(packed[n, SUB * i : SUB * i + SUB, lanes:], share * i, 1)
            out = jnp.where(low >= share * i, piece, out)
        pay[n, cap:] = out
    greeted = jnp.where(has_s, 3, 0) + jnp.where(has_n, 3, 0)
    pl.semaphore_wait(barrier, kin - 1 + greeted)
    obs = []
    for k, peer in enumerate(along):
        copy = remote(pay.at[peer[0]], rcv.at[lon], obs_send.at[k], obs_recv.at[k], peer)
        copy.start()
        obs.append(copy)
    for d in (4, 5, 6, 7, 2, 3, 0, 1):
        only(there[ways[d][1]], lambda d=d: map_copy(d).start())
    own = pltpu.make_async_copy(pay.at[lon], rcv.at[lon], own_sem)
    own.start()

    nothing = jnp.zeros(maps.shape, jnp.float32)
    near[slot_of(0, 0)] = maps[...]

    @pl.when(jnp.logical_not(has_s))
    def _():
        for dl in (-1, 0, 1):
            near[slot_of(dl, -1)] = nothing
        for lay in layouts:
            lay.hs[...] = jnp.zeros(lay.hs.shape, jnp.float32)
            for ref in (lay.pw, lay.pe):
                none = jnp.zeros(ref.shape[:2] + (lay.corner,) + ref.shape[3:], jnp.float32)
                ref[:, :, 0 : lay.corner] = none

    @pl.when(jnp.logical_not(has_n))
    def _():
        for dl in (-1, 0, 1):
            near[slot_of(dl, 1)] = nothing
        for lay in layouts:
            lay.hn[...] = jnp.zeros(lay.hn.shape, jnp.float32)
            for ref in (lay.pw, lay.pe):
                none = jnp.zeros(ref.shape[:2] + (lay.corner,) + ref.shape[3:], jnp.float32)
                ref[:, :, lay.packs + lay.corner :] = none

    mom[...] = jnp.zeros(mom.shape, jnp.float32)
    red[...] = jnp.zeros(red.shape, jnp.float32)
    ext[...] = jnp.zeros(ext.shape, jnp.float32)

    for lay in layouts:
        for b in range(lay.blocks):
            for r in (0, deep - 1):
                lay.f[b, r] = jnp.zeros((lay.span, lanes), jnp.float32)
            for c in (0, lay.span - EDGE):
                lay.f[b, :, c : c + EDGE] = jnp.zeros((deep, EDGE, lanes), jnp.float32)
                lay.gain[b, :, c : c + EDGE] = jnp.zeros((rows, EDGE, lanes), jnp.float32)

    for load in loads[7:]:
        load.wait()
    levels = (total - 1) // 2
    rates[...] = jnp.zeros(rates.shape, jnp.float32)
    rates[0:1, 0:total] = sigma[...] * precision[...]
    rates[1:2, 0:total] = sigma[...] * sigma[...] * precision[...]
    coef_lane = iota((SUB, lanes), 1)
    for lay in layouts:
        for b in range(lay.blocks):
            start = lay.first + b * lay.wide
            tile, first = start // lanes, start % lanes
            piece = rates[:, tile * lanes : tile * lanes + lanes]
            out = None
            for g in range(lay.groups):
                move = (lay.wide * g - first) % lanes
                moved = pltpu.roll(piece, move, 1) if move else piece
                out = moved if g == 0 else jnp.where(coef_lane >= lay.wide * g, moved, out)
            lay.coef[b, 1:3] = out[0:2]
            channel = coef_lane[0:1] % lay.wide + start
            level = jnp.where(channel < 2 * levels, channel % levels, 0)
            level = jnp.where(channel < total, level, 2 * levels)
            lay.coef[b, 0:1] = level.astype(jnp.float32)

    own_mask = iota((1, SUB, lanes), 2) % SUB == iota((1, SUB, lanes), 1)
    picked = jnp.where(own_mask, maps[2][:, None, :], 0.0)
    picked = picked.reshape(rows * SUB, lanes).astype(jnp.bfloat16)
    for lay in layouts:
        tiles_of = lay.wide // SUB
        column = iota((lanes, tiles_of * lanes), 0)
        target = iota((lanes, tiles_of * lanes), 1)
        start = target % lanes // lay.wide * lay.wide + target // lanes * SUB
        to_lane = ones_where((column >= start) & (column < start + SUB))
        out = jnp.dot(picked, to_lane, preferred_element_type=jnp.float32)
        for i in range(tiles_of):
            piece = out[:, lanes * i : lanes * i + lanes].reshape(rows, SUB, lanes)
            lay.base[4, PASSES:last, EDGE + SUB * i : EDGE + SUB * i + SUB] = piece

    for lay in layouts:
        flat = (lay.blocks + 1) * lanes
        source, goal = iota((width, flat), 0), iota((width, flat), 1)
        channel = goal // lanes * lay.wide + goal % lay.wide + lay.first
        channel = jnp.where(goal < lay.blocks * lanes, channel, kinds_at)
        lay.to_flat = ones_where(source == channel)

    own.wait()
    for copy in obs:
        copy.wait()
    def cells_of(lay, first, end, count):
        out = None
        for i in range(count):
            part = jnp.dot(
                lay.cell[...],
                lay.values[i, :, first * lanes : end * lanes],
                preferred_element_type=jnp.float32,
            )
            out = part if i == 0 else out + part
        return [
            out[:, n * lanes : (n + 1) * lanes].reshape(rows, lay.wide, lanes)
            for n in range(end - first)
        ]

    first_half = rcv[:, 0:cap].reshape(slots, lanes)
    second = []
    for n in range(tiles):
        for i in range(cap // SUB):
            piece = rcv[n, cap:]
            second.append(pltpu.roll(piece, lanes - share * i, 1) if i else piece)
    arrived = jnp.concatenate([first_half, jnp.concatenate(second, 0)], 1)
    arrived = jnp.where(iota((slots, width), 1) < lanes + share, arrived, 0.0)
    columns = arrived[:, kinds_at + 1 : kinds_at + 2]
    picker = ones_where(iota((SUB, width), 1) == iota((SUB, width), 0) + kinds_at + 1)
    turned = lax.dot_general(
        picker,
        arrived.astype(jnp.bfloat16),
        (((1,), (1,)), ((), ())),
        preferred_element_type=jnp.float32,
    )
    pieces = split3(arrived)
    for lay in layouts:
        wide, blocks = lay.wide, lay.blocks
        flat = (blocks + 1) * lanes
        group = (iota((slots, flat), 1) % lanes // wide * wide).astype(jnp.float32)
        mine = (columns >= group) & (columns < group + wide)
        for i, piece in enumerate(pieces):
            wide_part = jnp.dot(piece, lay.to_flat, preferred_element_type=jnp.float32)
            lay.values[i] = jnp.where(mine, wide_part, 0.0).astype(jnp.bfloat16)
        place = turned[1:2] * wide + turned[0:1] - jnp.floor(turned[0:1] / wide) * wide
        spots = iota((rows * wide, slots), 0).astype(jnp.float32)
        lay.cell[...] = ones_where(spots == place)
        own_cols = slice(EDGE, EDGE + wide)
        depths = lay.base[4, PASSES:last, own_cols]
        for b, cells in enumerate(cells_of(lay, 0, blocks, 3)):
            wet = depths > lay.coef[b, 0:1][None]
            cells = lay.coef[b, 1:2][None] * cells
            lay.f[b, PASSES:last, own_cols] = jnp.where(wet, cells, 0.0)

    lane = iota((SUB, lanes), 1)
    subs = iota((SUB, lanes), 0)

    def halo(lay, par, b, d):
        dl, db = ways[d]
        send, recv = lay.send.at[par, b, d], lay.recv.at[par, b, d]
        if dl == 0:
            first = PASSES if db < 0 else last - PASSES
            src = lay.f.at[b, pl.ds(first, PASSES), pl.ds(EDGE, lay.wide)]
            dst = (lay.hn if db < 0 else lay.hs).at[par, b]
        else:
            pack, to = (0, lay.pe) if dl < 0 else (1, lay.pw)
            packs, corner = lay.packs, lay.corner
            if db == 0:
                src = lay.pk.at[b, pack]
                dst = to.at[par, b, pl.ds(corner, packs)]
            else:
                src = lay.pk.at[b, pack, pl.ds(0 if db < 0 else packs - corner, corner)]
                dst = to.at[par, b, pl.ds(packs + corner if db < 0 else 0, corner)]
        return remote(src, dst, send, recv, at(dl, db))

    def emit(lay, par, b):
        wide, groups = lay.wide, lay.groups
        for a in range(lay.packs):
            for side, first, from_lane in ((0, EDGE, 0), (1, wide, lanes - wide)):
                out = None
                for i in range(groups):
                    piece = lay.f[b, PASSES + groups * a + i, first : first + EDGE]
                    move = (wide * i - from_lane) % lanes
                    piece = pltpu.roll(piece, move, 1) if move else piece
                    out = piece if out is None else jnp.where(lane >= wide * i, piece, out)
                lay.pk[b, side, a] = out
        for d in (2, 3, 4, 5, 6, 7, 0, 1):
            only(there[ways[d][1]], lambda d=d: halo(lay, par, b, d).start())

    for lay in layouts:
        for b in range(lay.blocks):
            emit(lay, 0, b)

    for lay in layouts:
        own_cols = slice(EDGE, EDGE + lay.wide)
        depths = lay.base[4, PASSES:last, own_cols]
        counts = cells_of(lay, lay.blocks, lay.blocks + 1, 1)[0]
        for b in range(lay.blocks):
            wet = depths > lay.coef[b, 0:1][None]
            lay.gain[b, :, own_cols] = jnp.where(wet, lay.coef[b, 2:3][None] * counts, 0.0)

    for d in range(8):
        dl, db = ways[d]
        only(there[-db], lambda d=d: map_copy(d).wait_recv())
    for d in range(8):
        only(there[ways[d][1]], lambda d=d: map_copy(d).wait_send())

    for m in range(3):
        for side in range(3):
            ext[m, side, 0:PASSES] = near[3 * side, m, rows - PASSES : rows]
            ext[m, side, PASSES:last] = near[3 * side + 1, m]
            ext[m, side, last:deep] = near[3 * side + 2, m, 0:PASSES]
    edge = iota((deep, lanes), 1) == lanes - 1
    east, north, depth = [], [], [ext[2, side, 0:deep] for side in range(3)]
    ahead = [pltpu.roll(ext[2, side], lanes - 1, 1)[0:deep] for side in range(3)]
    for side in range(3):
        moved = ahead[side]
        if side < 2:
            moved = jnp.where(edge, ahead[side + 1], moved)
        east.append(jnp.minimum(depth[side], moved))
        north.append(jnp.minimum(depth[side], ext[2, side, 1 : deep + 1]))
    reach = 3 * lanes
    for lay in layouts:
        column = iota((reach, lay.regs * lanes), 0) - lanes + EDGE
        target = iota((reach, lay.regs * lanes), 1)
        start = target % lanes // lay.wide * lay.wide + target // lanes * SUB
        lay.to_lane = ones_where((column >= start) & (column < start + SUB))
    sub_mask = iota((1, SUB, reach), 2) % SUB == iota((1, SUB, reach), 1)
    kinds = (
        [ext[0, side, 0:deep] for side in range(3)],
        east,
        [ext[1, side, 0:deep] for side in range(3)],
        north,
    )
    for m, kind in enumerate(kinds):
        line = jnp.concatenate(kind, 1)
        parts = [line] if m in (1, 3) else [x.astype(jnp.float32) for x in split3(line)]
        picked = [
            jnp.where(sub_mask, part[:, None, :], 0.0)
            .reshape(deep * SUB, reach)
            .astype(jnp.bfloat16)
            for part in parts
        ]
        for lay in layouts:
            out = jnp.zeros((deep * SUB, lay.regs * lanes), jnp.float32)
            for part in picked:
                out = out + jnp.dot(part, lay.to_lane, preferred_element_type=jnp.float32)
            for i in range(lay.regs):
                piece = out[:, lanes * i : lanes * i + lanes].reshape(deep, SUB, lanes)
                lay.base[m, :, SUB * i : SUB * i + SUB] = piece

    def build(lay, b, carry):
        level = lay.coef[b, 0:1]
        base, regs = lay.base, lay.regs
        for j in range(regs):
            pick = pl.ds(j, SUB, stride=regs)
            for r in range(deep):
                east_wet = base[1, r, pick, :] > level
                north_wet = base[3, r, pick, :] > level
                lay.fe[b, j, r] = jnp.where(east_wet, base[0, r, pick, :], 0.0)
                lay.fn[b, j, r] = jnp.where(north_wet, base[2, r, pick, :], 0.0)
        return carry

    for lay in layouts:
        lax.fori_loop(0, lay.blocks, functools.partial(build, lay), 0)

    def pair_copy():
        partner = lat + 1 - 2 * lax.rem(lat, 2)
        return remote(red, red_pair, sum_send.at[0], sum_recv.at[0], (lon, partner))

    def sum_copy(k):
        return remote(red, red_all.at[k - 1], sum_send.at[1], sum_recv.at[1], kin_of(k))

    def one_pass(lay, b, t, finish):
        f, fe, fn, tmp, regs = lay.f, lay.fe, lay.fn, lay.tmp, lay.regs

        def old(j, lo, hi):
            if t == 0:
                return jnp.stack(
                    [f[b, r, pl.ds(j, SUB, stride=regs), :] for r in range(lo, hi)]
                )
            return tmp[(t + 1) % 2, j, lo:hi]

        for lo, hi in chunks(t + 1, deep - 1 - t):
            v = old(0, lo - 1, hi + 1)
            wrap = pltpu.roll(v[1:-1], SUB - 1, 1)
            end = old(regs - 1, lo, hi)
            end = fe[b, regs - 1, lo:hi] * (wrap - end)
            west = pltpu.roll(end, 1, 1)
            for j in range(regs):
                centre = v[1:-1]
                if j < regs - 1:
                    following = old(j + 1, lo - 1, hi + 1)
                    flux = fe[b, j, lo:hi] * (following[1:-1] - centre)
                else:
                    following, flux = None, end
                up = fn[b, j, lo - 1 : hi] * (v[1:] - v[:-1])
                new = centre + ((flux - west) + (up[1:] - up[:-1]))
                if finish is None:
                    tmp[t % 2, j, lo:hi] = new
                else:
                    finish(j, lo, new)
                v, west = following, flux

    def step(lay, e, b):
        par = lax.rem(e, 2)
        odd = par == 1
        f, wide, span, groups = lay.f, lay.wide, lay.span, lay.groups
        own_cols = slice(EDGE, EDGE + wide)
        for d in range(8):
            only(there[-ways[d][1]], lambda d=d: halo(lay, par, b, d).wait_recv())
        f[b, 0:PASSES, own_cols] = lay.hs[par, b]
        f[b, last:deep, own_cols] = lay.hn[par, b]
        for r in range(1, deep - 1):
            a, i = (r - 1) // groups, (r - 1) % groups
            west = pltpu.roll(f[b, r, wide : wide + EDGE], wide, 1)
            far = lay.pw[par, b, a]
            far = pltpu.roll(far, lanes - wide * i, 1) if i else far
            f[b, r, 0:EDGE] = jnp.where(lane < wide, far, west)
            east = pltpu.roll(f[b, r, EDGE : 2 * EDGE], lanes - wide, 1)
            far = lay.pe[par, b, a]
            move = (lanes - wide - wide * i) % lanes
            far = pltpu.roll(far, move, 1) if move else far
            f[b, r, wide + EDGE : span] = jnp.where(lane >= lanes - wide, far, east)
        for t in range(PASSES - 1):
            one_pass(lay, b, t, None)
        for d in range(8):
            only(there[ways[d][1]], lambda d=d: halo(lay, par, b, d).wait_send())

        def finish(j, lo, new):
            pick = pl.ds(j, SUB, stride=lay.regs)
            at_col = subs * lay.regs + j
            own_here = jnp.where((at_col >= EDGE) & (at_col < EDGE + wide), 1.0, 0.0)
            sums = None
            for i in range(new.shape[0]):
                r = lo + i
                weight = jnp.where(odd, lay.gain[b, r - PASSES, pick, :], own_here)
                weighed = new[i] * weight
                square = new[i] * weighed
                sums = square if sums is None else sums + square
                f[b, r, pick, :] = weighed
            mom[e] = mom[e] + sums

        one_pass(lay, b, PASSES - 1, finish)

        @pl.when(e < STAGES - 1)
        def _():
            emit(lay, 1 - par, b)

        @pl.when(jnp.logical_not(odd))
        def _():
            lane_all = iota((wide, lanes), 1)
            for a in range(lay.packs):
                first = PASSES + groups * a
                square = f[b, first : first + groups, own_cols].reshape(lanes, lanes).T
                pieces = [square[wide * g : wide * g + wide] for g in range(groups)]
                half = groups // 2
                while half:
                    move = half * wide
                    low = lane_all // move % 2 == 0
                    for g in range(groups):
                        if g // half % 2 == 0:
                            one, two = pieces[g], pieces[g + half]
                            pieces[g] = jnp.where(low, one, pltpu.roll(two, move, 1))
                            pieces[g + half] = jnp.where(
                                low, pltpu.roll(one, lanes - move, 1), two
                            )
                    half //= 2
                for i in range(groups):
                    begin = (lay.first + b * wide) * rows + groups * a + i
                    v_out[lax.div(e, 2), pl.ds(begin, wide, stride=rows), :] = pieces[i]

    def send_sum(k, carry):
        sum_copy(k).start()
        return carry

    def stage(e, carry):
        for lay in layouts:

            def block(b, carry, lay=lay):
                step(lay, e, b)
                if lay is layouts[0]:

                    @pl.when((e == STAGES - 1) & (b == 0))
                    def _():
                        pair_copy().wait()
                        red[...] = red[...] + red_pair[...]
                        lax.fori_loop(1, kin, send_sum, 0)

                return carry

            lax.fori_loop(0, lay.blocks, block, 0)
        @pl.when(e == STAGES - 2)
        def _():
            for i in range(4):
                red[i : i + 1, :] = jnp.sum(mom[i], 0, keepdims=True)
            pair_copy().start()

        return carry

    lax.fori_loop(0, STAGES, stage, 0)

    total_copy = remote(red_all, red_all, sum_send.at[1], sum_recv.at[1], at(1, 0))
    total_copy.wait_recv()
    total_copy.wait_send()
    sums = jnp.sum(red[...] + jnp.sum(red_all[...], 0), 1, keepdims=True)
    m0 = sums[0:1]
    x, y, z = sums[1:2] / m0, sums[2:3] / m0, sums[3:4] / m0
    alpha = 1.0 / (1.0 + x)
    beta = (y - x * x) * alpha * alpha
    c0, c1 = 1.0 - alpha + beta, -alpha
    curve = c0 * c0 * (1.0 + x) + 2.0 * c0 * c1 * (x + y) + c1 * c1 * (y + z)
    second = beta / curve
    values = (
        alpha + second * c0,
        second * c1,
        (1.0 - second) * (1.0 - alpha) - second * beta,
        -(1.0 - second) * alpha - second * c0,
        alpha * second,
    )
    for i, value in enumerate(values):
        c_out[i : i + 1, :] = jnp.broadcast_to(value, (1, lanes))


def combine_kernel(block, v, c, increment, residual, held, sems):
    size, lanes = increment.shape
    copies = []
    for n, first in enumerate(range(0, size, block)):
        count = min(block, size - first)
        part = pl.ds(first, count)
        zero, one, two = v[0, part], v[1, part], v[2, part]
        held[0, part] = c[0:1] * zero + c[1:2] * one
        held[1, part] = c[2:3] * zero + c[3:4] * one + c[4:5] * two
        for i, target in enumerate((increment, residual)):
            copy = pltpu.make_async_copy(held.at[i, part], target.at[part], sems.at[i, n])
            copy.start()
            copies.append(copy)
    for copy in copies:
        copy.wait()


def local(
    kappa_east, kappa_north, depth, sigma, obs_precision, obs_tile, obs_col, obs_lat, innovation
):
    rows, lanes = kappa_east.shape
    total = sigma.shape[0]
    tiles, bands = lax.axis_size("lon"), lax.axis_size("lat")
    listed = obs_col.shape[0]
    cap = 2 * listed // tiles
    layouts = layouts_of(total, rows, lanes)
    channels = layouts[-1].first + layouts[-1].blocks * layouts[-1].wide
    width = -(-(-(-total // SUB) * SUB + SUB) // 128) * 128

    deep = rows + 2 * PASSES
    vmem = pl.BlockSpec(memory_space=pltpu.VMEM)
    f32 = jnp.float32
    dma = pltpu.SemaphoreType.DMA
    slots = tiles * cap
    v, c = pl.pallas_call(
        functools.partial(main_kernel, tiles, bands, cap, total),
        out_shape=[
            jax.ShapeDtypeStruct((3, channels * rows, lanes), f32),
            jax.ShapeDtypeStruct((SUB, lanes), f32),
        ],
        in_specs=[pl.BlockSpec(memory_space=pltpu.HBM)] * 9,
        out_specs=[vmem] * 2,
        scratch_shapes=[
            pltpu.VMEM((rows, lanes), jnp.int32),
            pltpu.VMEM((1, total), f32),
            pltpu.VMEM((1, total), f32),
            pltpu.VMEM((3, 1, listed), jnp.int32),
            pltpu.VMEM((total, listed), f32),
            pltpu.VMEM((3, rows, lanes), f32),
            pltpu.VMEM((width, listed), f32),
            pltpu.VMEM((SUB, -(-channels // lanes) * lanes), f32),
            pltpu.VMEM((tiles, cap + SUB, lanes), f32),
            pltpu.VMEM((tiles, cap + SUB, lanes), f32),
            pltpu.VMEM((9, 3, rows, lanes), f32),
            pltpu.VMEM((3, 3, -(-(deep + 1) // SUB) * SUB, lanes), f32),
            pltpu.VMEM((STAGES, SUB, lanes), f32),
            pltpu.VMEM((SUB, lanes), f32),
            pltpu.VMEM((SUB, lanes), f32),
            pltpu.VMEM((tiles * bands // 2 - 1, SUB, lanes), f32),
            dma((tiles - 1,)),
            dma((tiles - 1,)),
            dma((8,)),
            dma((8,)),
            dma,
            dma((9,)),
            dma((2,)),
            dma((2,)),
        ]
        + [shape for lay in layouts for shape in lay.shapes(slots)],
        compiler_params=pltpu.CompilerParams(
            collective_id=1, has_side_effects=True, vmem_limit_bytes=48 * 1024 * 1024
        ),
        name="smooth_all",
    )(
        *[
            pltpu.with_memory_space_constraint(x, pltpu.HBM)
            for x in (
                kappa_east,
                kappa_north,
                depth,
                sigma.reshape(1, total),
                obs_precision.reshape(1, total),
                obs_tile.reshape(1, listed),
                obs_col.reshape(1, listed),
                obs_lat.reshape(1, listed),
                innovation,
            )
        ]
    )

    block = 4 * SUB * rows
    pieces = -(-total * rows // block)
    increment, residual = pl.pallas_call(
        functools.partial(combine_kernel, block),
        out_shape=[jax.ShapeDtypeStruct((total * rows, lanes), f32)] * 2,
        in_specs=[vmem] * 2,
        out_specs=[pl.BlockSpec(memory_space=pl.ANY)] * 2,
        scratch_shapes=[pltpu.VMEM((2, total * rows, lanes), f32), dma((2, pieces))],
        compiler_params=pltpu.CompilerParams(vmem_limit_bytes=10 * 1024 * 1024),
        name="combine",
    )(v, c)
    shape = (total, rows, lanes)
    return increment.reshape(shape), residual.reshape(shape)


def solution(mesh):
    return jax.shard_map(
        local,
        mesh=mesh,
        in_specs=(
            P("lat", "lon"),
            P("lat", "lon"),
            P("lat", "lon"),
            P(),
            P(),
            P(("lon", "lat"), None),
            P(("lon", "lat")),
            P(("lon", "lat")),
            P(None, ("lon", "lat")),
        ),
        out_specs=(P(None, "lat", "lon"), P(None, "lat", "lon")),
        check_vma=False,
    )
```

```python
import functools

import jax
import jax.numpy as jnp
from jax import lax
from jax.experimental import pallas as pl
from jax.experimental.pallas import tpu as pltpu
from jax.sharding import PartitionSpec as P

MESH = pl.DeviceIdType.MESH
SUB = 8
PASSES = 5
STAGES = 5
EDGE = 8


SCRATCH = ("base", "values", "cell", "coef", "f", "fe", "fn", "tmp", "gain")
SCRATCH += ("hs", "hn", "pw", "pe", "pk", "send", "recv")


class Layout:
    def __init__(self, first, blocks, groups, rows, lanes):
        self.first, self.blocks, self.groups = first, blocks, groups
        self.wide = lanes // groups
        self.span = self.wide + 2 * EDGE
        self.regs = self.span // SUB
        self.packs = rows // groups
        self.corner = (PASSES - 1) // groups
        self.rows, self.lanes = rows, lanes

    def bind(self, refs):
        for name, ref in zip(SCRATCH, refs):
            setattr(self, name, ref)

    def shapes(self, slots):
        f32, dma = jnp.float32, pltpu.SemaphoreType.DMA
        rows, lanes, blocks = self.rows, self.lanes, self.blocks
        deep = rows + 2 * PASSES
        faces = pltpu.VMEM((blocks, self.regs, deep, SUB, lanes), f32)
        beside = pltpu.VMEM((2, blocks, PASSES, self.wide, lanes), f32)
        edge = pltpu.VMEM((2, blocks, self.packs + 2 * self.corner, SUB, lanes), f32)
        return [
            pltpu.VMEM((5, deep, self.span, lanes), f32),
            pltpu.VMEM((3, slots, (blocks + 1) * lanes), jnp.bfloat16),
            pltpu.VMEM((rows * self.wide, slots), jnp.bfloat16),
            pltpu.VMEM((blocks, SUB, lanes), f32),
            pltpu.VMEM((blocks, deep, self.span, lanes), f32),
            faces,
            faces,
            pltpu.VMEM((2, self.regs, deep, SUB, lanes), f32),
            pltpu.VMEM((blocks, rows, self.span, lanes), f32),
            beside,
            beside,
            edge,
            edge,
            pltpu.VMEM((blocks, 2, self.packs, SUB, lanes), f32),
            dma((2, blocks, 8)),
            dma((2, blocks, 8)),
        ]


def layouts_of(total, rows, lanes):
    pairs = total // (lanes // 2)
    left = total - pairs * (lanes // 2)
    out = [Layout(0, pairs, 2, rows, lanes)]
    if left:
        out.append(Layout(pairs * (lanes // 2), -(-left // (lanes // 4)), 4, rows, lanes))
    return out


def split3(x):
    high = x.astype(jnp.bfloat16)
    left = x - high.astype(jnp.float32)
    middle = left.astype(jnp.bfloat16)
    low = (left - middle.astype(jnp.float32)).astype(jnp.bfloat16)
    return high, middle, low


def chunks(first, end, most=5):
    count = -(-(end - first) // most)
    cuts = [first + (end - first) * i // count for i in range(count + 1)]
    return list(zip(cuts[:-1], cuts[1:]))


def iota(shape, dim):
    return lax.broadcasted_iota(jnp.int32, shape, dim)


def ones_where(mask):
    return jnp.where(mask, 1.0, 0.0).astype(jnp.bfloat16)


def main_kernel(
    tiles,
    bands,
    cap,
    total,
    ke_in,
    kn_in,
    depth_in,
    sigma_in,
    precision_in,
    tile_in,
    col_in,
    lat_in,
    innovation_in,
    v_out,
    c_out,
    depth_own,
    sigma,
    precision,
    index,
    innovation,
    maps,
    data,
    rates,
    pay,
    rcv,
    near,
    ext,
    mom,
    red,
    red_pair,
    red_all,
    obs_send,
    obs_recv,
    map_send,
    map_recv,
    own_sem,
    load_sem,
    sum_send,
    sum_recv,
    *rest,
):
    lon, lat = lax.axis_index("lon"), lax.axis_index("lat")
    rows, lanes = maps.shape[1], maps.shape[2]
    deep = rows + 2 * PASSES
    last = rows + PASSES
    layouts = layouts_of(total, rows, lanes)
    for n, lay in enumerate(layouts):
        lay.bind(rest[n * len(SCRATCH) : (n + 1) * len(SCRATCH)])
    has_s, has_n = lat > 0, lat < bands - 1

    def at(dl, db):
        return lax.rem(lon + dl + tiles, tiles), lax.rem(lat + db + bands, bands)

    along = [(lax.rem(lon + k, tiles), lat) for k in sorted(range(1, tiles), key=lambda k: abs(2 * k - tiles))]
    ways = [(0, -1), (0, 1), (-1, 0), (1, 0), (-1, -1), (1, -1), (-1, 1), (1, 1)]
    there = {-1: has_s, 0: None, 1: has_n}

    def only(cond, body):
        if cond is None:
            body()
        else:
            pl.when(cond)(body)

    loads = [
        pltpu.make_async_copy(src, dst, load_sem.at[i])
        for i, (src, dst) in enumerate(
            (
                (ke_in, maps.at[0]),
                (kn_in, maps.at[1]),
                (depth_in, depth_own),
                (tile_in, index.at[0]),
                (col_in, index.at[1]),
                (lat_in, index.at[2]),
                (innovation_in, innovation),
                (sigma_in, sigma),
                (precision_in, precision),
            )
        )
    ]
    for load in loads:
        load.start()

    barrier = pltpu.get_barrier_semaphore()

    def greet(peer):
        pl.semaphore_signal(barrier, inc=1, device_id=peer, device_id_type=MESH)

    half = bands // 2
    kin = tiles * half
    me = lon * half + lax.div(lat, 2)

    def kin_of(k):
        peer = lax.rem(me + k, kin)
        return lax.div(peer, half), 2 * lax.rem(peer, half) + lax.rem(lat, 2)

    def greet_kin(k, carry):
        greet(kin_of(k))
        return carry

    lax.fori_loop(1, kin, greet_kin, 0)
    for dl, db in ways:
        if db:
            only(there[db], functools.partial(greet, at(dl, db)))

    def remote(src, dst, send, recv, peer):
        return pltpu.make_async_remote_copy(
            src_ref=src,
            dst_ref=dst,
            send_sem=send,
            recv_sem=recv,
            device_id=peer,
            device_id_type=MESH,
        )

    def slot_of(dl, db):
        return (dl + 1) * 3 + db + 1

    def map_copy(d):
        dl, db = ways[d]
        return remote(
            maps, near.at[slot_of(-dl, -db)], map_send.at[d], map_recv.at[d], at(dl, db)
        )

    for load in loads[:3]:
        load.wait()
    maps[2] = depth_own[...].astype(jnp.float32)
    for load in loads[3:7]:
        load.wait()
    listed = index.shape[2]
    slots = tiles * cap
    width = data.shape[0]
    kinds_at = -(-total // SUB) * SUB
    data[kinds_at - SUB :] = jnp.zeros((width - kinds_at + SUB, listed), jnp.float32)
    data[0:total] = innovation[...]
    data[kinds_at : kinds_at + 1] = jnp.ones((1, listed), jnp.float32)
    data[kinds_at + 1 : kinds_at + 2] = index[1].astype(jnp.float32)
    data[kinds_at + 2 : kinds_at + 3] = index[2].astype(jnp.float32)
    tile_row = jnp.broadcast_to(index[0].astype(jnp.float32), (listed, listed))
    earlier = iota((listed, listed), 0) < iota((listed, listed), 1)
    same = (tile_row == tile_row.T) & earlier
    rank = jnp.sum(jnp.where(same, 1.0, 0.0), 0, keepdims=True)
    slot = index[0] * cap + rank.astype(jnp.int32)
    chosen = ones_where(iota((slots, listed), 0) == slot)
    packed = jnp.zeros((slots, width), jnp.float32)
    for part in split3(data[...]):
        packed = packed + lax.dot_general(
            chosen, part, (((1,), (1,)), ((), ())), preferred_element_type=jnp.float32
        )
    share = lanes * SUB // cap
    packed = packed.reshape(tiles, cap, width)
    pay[:, 0:cap] = packed[:, :, 0:lanes]
    low = iota((SUB, lanes), 1)
    for n in range(tiles):
        out = packed[n, 0:SUB, lanes:]
        for i in range(1, cap // SUB):
            piece = pltpu.roll(packed[n, SUB * i : SUB * i + SUB, lanes:], share * i, 1)
            out = jnp.where(low >= share * i, piece, out)
        pay[n, cap:] = out
    greeted = jnp.where(has_s, 3, 0) + jnp.where(has_n, 3, 0)
    pl.semaphore_wait(barrier, kin - 1 + greeted)
    obs = []
    for k, peer in enumerate(along):
        copy = remote(pay.at[peer[0]], rcv.at[lon], obs_send.at[k], obs_recv.at[k], peer)
        copy.start()
        obs.append(copy)
    for d in (4, 5, 6, 7, 2, 3, 0, 1):
        only(there[ways[d][1]], lambda d=d: map_copy(d).start())
    own = pltpu.make_async_copy(pay.at[lon], rcv.at[lon], own_sem)
    own.start()

    nothing = jnp.zeros(maps.shape, jnp.float32)
    near[slot_of(0, 0)] = maps[...]

    @pl.when(jnp.logical_not(has_s))
    def _():
        for dl in (-1, 0, 1):
            near[slot_of(dl, -1)] = nothing
        for lay in layouts:
            lay.hs[...] = jnp.zeros(lay.hs.shape, jnp.float32)
            for ref in (lay.pw, lay.pe):
                none = jnp.zeros(ref.shape[:2] + (lay.corner,) + ref.shape[3:], jnp.float32)
                ref[:, :, 0 : lay.corner] = none

    @pl.when(jnp.logical_not(has_n))
    def _():
        for dl in (-1, 0, 1):
            near[slot_of(dl, 1)] = nothing
        for lay in layouts:
            lay.hn[...] = jnp.zeros(lay.hn.shape, jnp.float32)
            for ref in (lay.pw, lay.pe):
                none = jnp.zeros(ref.shape[:2] + (lay.corner,) + ref.shape[3:], jnp.float32)
                ref[:, :, lay.packs + lay.corner :] = none

    mom[...] = jnp.zeros(mom.shape, jnp.float32)
    red[...] = jnp.zeros(red.shape, jnp.float32)
    ext[...] = jnp.zeros(ext.shape, jnp.float32)

    for lay in layouts:
        for b in range(lay.blocks):
            for r in (0, deep - 1):
                lay.f[b, r] = jnp.zeros((lay.span, lanes), jnp.float32)
            for c in (0, lay.span - EDGE):
                lay.f[b, :, c : c + EDGE] = jnp.zeros((deep, EDGE, lanes), jnp.float32)
                lay.gain[b, :, c : c + EDGE] = jnp.zeros((rows, EDGE, lanes), jnp.float32)

    for load in loads[7:]:
        load.wait()
    levels = (total - 1) // 2
    rates[...] = jnp.zeros(rates.shape, jnp.float32)
    rates[0:1, 0:total] = sigma[...] * precision[...]
    rates[1:2, 0:total] = sigma[...] * sigma[...] * precision[...]
    coef_lane = iota((SUB, lanes), 1)
    for lay in layouts:
        for b in range(lay.blocks):
            start = lay.first + b * lay.wide
            tile, first = start // lanes, start % lanes
            piece = rates[:, tile * lanes : tile * lanes + lanes]
            out = None
            for g in range(lay.groups):
                move = (lay.wide * g - first) % lanes
                moved = pltpu.roll(piece, move, 1) if move else piece
                out = moved if g == 0 else jnp.where(coef_lane >= lay.wide * g, moved, out)
            lay.coef[b, 1:3] = out[0:2]
            channel = coef_lane[0:1] % lay.wide + start
            level = jnp.where(channel < 2 * levels, channel % levels, 0)
            level = jnp.where(channel < total, level, 2 * levels)
            lay.coef[b, 0:1] = level.astype(jnp.float32)

    own_mask = iota((1, SUB, lanes), 2) % SUB == iota((1, SUB, lanes), 1)
    picked = jnp.where(own_mask, maps[2][:, None, :], 0.0)
    picked = picked.reshape(rows * SUB, lanes).astype(jnp.bfloat16)
    for lay in layouts:
        tiles_of = lay.wide // SUB
        column = iota((lanes, tiles_of * lanes), 0)
        target = iota((lanes, tiles_of * lanes), 1)
        start = target % lanes // lay.wide * lay.wide + target // lanes * SUB
        to_lane = ones_where((column >= start) & (column < start + SUB))
        out = jnp.dot(picked, to_lane, preferred_element_type=jnp.float32)
        for i in range(tiles_of):
            piece = out[:, lanes * i : lanes * i + lanes].reshape(rows, SUB, lanes)
            lay.base[4, PASSES:last, EDGE + SUB * i : EDGE + SUB * i + SUB] = piece

    for lay in layouts:
        flat = (lay.blocks + 1) * lanes
        source, goal = iota((width, flat), 0), iota((width, flat), 1)
        channel = goal // lanes * lay.wide + goal % lay.wide + lay.first
        channel = jnp.where(goal < lay.blocks * lanes, channel, kinds_at)
        lay.to_flat = ones_where(source == channel)

    own.wait()
    for copy in obs:
        copy.wait()
    def cells_of(lay, first, end, count):
        out = None
        for i in range(count):
            part = jnp.dot(
                lay.cell[...],
                lay.values[i, :, first * lanes : end * lanes],
                preferred_element_type=jnp.float32,
            )
            out = part if i == 0 else out + part
        return [
            out[:, n * lanes : (n + 1) * lanes].reshape(rows, lay.wide, lanes)
            for n in range(end - first)
        ]

    first_half = rcv[:, 0:cap].reshape(slots, lanes)
    second = []
    for n in range(tiles):
        for i in range(cap // SUB):
            piece = rcv[n, cap:]
            second.append(pltpu.roll(piece, lanes - share * i, 1) if i else piece)
    arrived = jnp.concatenate([first_half, jnp.concatenate(second, 0)], 1)
    arrived = jnp.where(iota((slots, width), 1) < lanes + share, arrived, 0.0)
    columns = arrived[:, kinds_at + 1 : kinds_at + 2]
    picker = ones_where(iota((SUB, width), 1) == iota((SUB, width), 0) + kinds_at + 1)
    turned = lax.dot_general(
        picker,
        arrived.astype(jnp.bfloat16),
        (((1,), (1,)), ((), ())),
        preferred_element_type=jnp.float32,
    )
    pieces = split3(arrived)
    for lay in layouts:
        wide, blocks = lay.wide, lay.blocks
        flat = (blocks + 1) * lanes
        group = (iota((slots, flat), 1) % lanes // wide * wide).astype(jnp.float32)
        mine = (columns >= group) & (columns < group + wide)
        for i, piece in enumerate(pieces):
            wide_part = jnp.dot(piece, lay.to_flat, preferred_element_type=jnp.float32)
            lay.values[i] = jnp.where(mine, wide_part, 0.0).astype(jnp.bfloat16)
        place = turned[1:2] * wide + turned[0:1] - jnp.floor(turned[0:1] / wide) * wide
        spots = iota((rows * wide, slots), 0).astype(jnp.float32)
        lay.cell[...] = ones_where(spots == place)
        own_cols = slice(EDGE, EDGE + wide)
        depths = lay.base[4, PASSES:last, own_cols]
        for b, cells in enumerate(cells_of(lay, 0, blocks, 3)):
            wet = depths > lay.coef[b, 0:1][None]
            cells = lay.coef[b, 1:2][None] * cells
            lay.f[b, PASSES:last, own_cols] = jnp.where(wet, cells, 0.0)

    lane = iota((SUB, lanes), 1)
    subs = iota((SUB, lanes), 0)

    def halo(lay, par, b, d):
        dl, db = ways[d]
        send, recv = lay.send.at[par, b, d], lay.recv.at[par, b, d]
        if dl == 0:
            first = PASSES if db < 0 else last - PASSES
            src = lay.f.at[b, pl.ds(first, PASSES), pl.ds(EDGE, lay.wide)]
            dst = (lay.hn if db < 0 else lay.hs).at[par, b]
        else:
            pack, to = (0, lay.pe) if dl < 0 else (1, lay.pw)
            packs, corner = lay.packs, lay.corner
            if db == 0:
                src = lay.pk.at[b, pack]
                dst = to.at[par, b, pl.ds(corner, packs)]
            else:
                src = lay.pk.at[b, pack, pl.ds(0 if db < 0 else packs - corner, corner)]
                dst = to.at[par, b, pl.ds(packs + corner if db < 0 else 0, corner)]
        return remote(src, dst, send, recv, at(dl, db))

    def emit(lay, par, b):
        wide, groups = lay.wide, lay.groups
        for a in range(lay.packs):
            for side, first, from_lane in ((0, EDGE, 0), (1, wide, lanes - wide)):
                out = None
                for i in range(groups):
                    piece = lay.f[b, PASSES + groups * a + i, first : first + EDGE]
                    move = (wide * i - from_lane) % lanes
                    piece = pltpu.roll(piece, move, 1) if move else piece
                    out = piece if out is None else jnp.where(lane >= wide * i, piece, out)
                lay.pk[b, side, a] = out
        for d in (2, 3, 4, 5, 6, 7, 0, 1):
            only(there[ways[d][1]], lambda d=d: halo(lay, par, b, d).start())

    for lay in layouts:
        for b in range(lay.blocks):
            emit(lay, 0, b)

    for lay in layouts:
        own_cols = slice(EDGE, EDGE + lay.wide)
        depths = lay.base[4, PASSES:last, own_cols]
        counts = cells_of(lay, lay.blocks, lay.blocks + 1, 1)[0]
        for b in range(lay.blocks):
            wet = depths > lay.coef[b, 0:1][None]
            lay.gain[b, :, own_cols] = jnp.where(wet, lay.coef[b, 2:3][None] * counts, 0.0)

    for d in range(8):
        dl, db = ways[d]
        only(there[-db], lambda d=d: map_copy(d).wait_recv())
    for d in range(8):
        only(there[ways[d][1]], lambda d=d: map_copy(d).wait_send())

    for m in range(3):
        for side in range(3):
            ext[m, side, 0:PASSES] = near[3 * side, m, rows - PASSES : rows]
            ext[m, side, PASSES:last] = near[3 * side + 1, m]
            ext[m, side, last:deep] = near[3 * side + 2, m, 0:PASSES]
    edge = iota((deep, lanes), 1) == lanes - 1
    east, north, depth = [], [], [ext[2, side, 0:deep] for side in range(3)]
    ahead = [pltpu.roll(ext[2, side], lanes - 1, 1)[0:deep] for side in range(3)]
    for side in range(3):
        moved = ahead[side]
        if side < 2:
            moved = jnp.where(edge, ahead[side + 1], moved)
        east.append(jnp.minimum(depth[side], moved))
        north.append(jnp.minimum(depth[side], ext[2, side, 1 : deep + 1]))
    reach = 3 * lanes
    for lay in layouts:
        column = iota((reach, lay.regs * lanes), 0) - lanes + EDGE
        target = iota((reach, lay.regs * lanes), 1)
        start = target % lanes // lay.wide * lay.wide + target // lanes * SUB
        lay.to_lane = ones_where((column >= start) & (column < start + SUB))
    sub_mask = iota((1, SUB, reach), 2) % SUB == iota((1, SUB, reach), 1)
    kinds = (
        [ext[0, side, 0:deep] for side in range(3)],
        east,
        [ext[1, side, 0:deep] for side in range(3)],
        north,
    )
    for m, kind in enumerate(kinds):
        line = jnp.concatenate(kind, 1)
        parts = [line] if m in (1, 3) else [x.astype(jnp.float32) for x in split3(line)]
        picked = [
            jnp.where(sub_mask, part[:, None, :], 0.0)
            .reshape(deep * SUB, reach)
            .astype(jnp.bfloat16)
            for part in parts
        ]
        for lay in layouts:
            out = jnp.zeros((deep * SUB, lay.regs * lanes), jnp.float32)
            for part in picked:
                out = out + jnp.dot(part, lay.to_lane, preferred_element_type=jnp.float32)
            for i in range(lay.regs):
                piece = out[:, lanes * i : lanes * i + lanes].reshape(deep, SUB, lanes)
                lay.base[m, :, SUB * i : SUB * i + SUB] = piece

    def build(lay, b, carry):
        level = lay.coef[b, 0:1]
        base, regs = lay.base, lay.regs
        for j in range(regs):
            pick = pl.ds(j, SUB, stride=regs)
            for r in range(deep):
                east_wet = base[1, r, pick, :] > level
                north_wet = base[3, r, pick, :] > level
                lay.fe[b, j, r] = jnp.where(east_wet, base[0, r, pick, :], 0.0)
                lay.fn[b, j, r] = jnp.where(north_wet, base[2, r, pick, :], 0.0)
        return carry

    for lay in layouts:
        lax.fori_loop(0, lay.blocks, functools.partial(build, lay), 0)

    def pair_copy():
        partner = lat + 1 - 2 * lax.rem(lat, 2)
        return remote(red, red_pair, sum_send.at[0], sum_recv.at[0], (lon, partner))

    def sum_copy(k):
        return remote(red, red_all.at[k - 1], sum_send.at[1], sum_recv.at[1], kin_of(k))

    def one_pass(lay, b, t, finish):
        f, fe, fn, tmp, regs = lay.f, lay.fe, lay.fn, lay.tmp, lay.regs

        def old(j, lo, hi):
            if t == 0:
                return jnp.stack(
                    [f[b, r, pl.ds(j, SUB, stride=regs), :] for r in range(lo, hi)]
                )
            return tmp[(t + 1) % 2, j, lo:hi]

        for lo, hi in chunks(t + 1, deep - 1 - t):
            v = old(0, lo - 1, hi + 1)
            wrap = pltpu.roll(v[1:-1], SUB - 1, 1)
            end = old(regs - 1, lo, hi)
            end = fe[b, regs - 1, lo:hi] * (wrap - end)
            west = pltpu.roll(end, 1, 1)
            for j in range(regs):
                centre = v[1:-1]
                if j < regs - 1:
                    following = old(j + 1, lo - 1, hi + 1)
                    flux = fe[b, j, lo:hi] * (following[1:-1] - centre)
                else:
                    following, flux = None, end
                up = fn[b, j, lo - 1 : hi] * (v[1:] - v[:-1])
                new = centre + ((flux - west) + (up[1:] - up[:-1]))
                if finish is None:
                    tmp[t % 2, j, lo:hi] = new
                else:
                    finish(j, lo, new)
                v, west = following, flux

    def step(lay, e, b):
        par = lax.rem(e, 2)
        odd = par == 1
        f, wide, span, groups = lay.f, lay.wide, lay.span, lay.groups
        own_cols = slice(EDGE, EDGE + wide)
        for d in (0, 1):
            only(there[-ways[d][1]], lambda d=d: halo(lay, par, b, d).wait_recv())
        f[b, 0:PASSES, own_cols] = lay.hs[par, b]
        f[b, last:deep, own_cols] = lay.hn[par, b]
        for r in range(1, deep - 1):
            f[b, r, 0:EDGE] = pltpu.roll(f[b, r, wide : wide + EDGE], wide, 1)
            f[b, r, wide + EDGE : span] = pltpu.roll(f[b, r, EDGE : 2 * EDGE], lanes - wide, 1)
        for d in range(2, 8):
            only(there[-ways[d][1]], lambda d=d: halo(lay, par, b, d).wait_recv())
        for r in range(1, deep - 1):
            a, i = (r - 1) // groups, (r - 1) % groups
            west = f[b, r, 0:EDGE]
            far = lay.pw[par, b, a]
            far = pltpu.roll(far, lanes - wide * i, 1) if i else far
            f[b, r, 0:EDGE] = jnp.where(lane < wide, far, west)
            east = f[b, r, wide + EDGE : span]
            far = lay.pe[par, b, a]
            move = (lanes - wide - wide * i) % lanes
            far = pltpu.roll(far, move, 1) if move else far
            f[b, r, wide + EDGE : span] = jnp.where(lane >= lanes - wide, far, east)
        for t in range(PASSES - 1):
            one_pass(lay, b, t, None)
        for d in range(8):
            only(there[ways[d][1]], lambda d=d: halo(lay, par, b, d).wait_send())

        def finish(j, lo, new):
            pick = pl.ds(j, SUB, stride=lay.regs)
            at_col = subs * lay.regs + j
            own_here = jnp.where((at_col >= EDGE) & (at_col < EDGE + wide), 1.0, 0.0)
            sums = None
            for i in range(new.shape[0]):
                r = lo + i
                weight = jnp.where(odd, lay.gain[b, r - PASSES, pick, :], own_here)
                weighed = new[i] * weight
                square = new[i] * weighed
                sums = square if sums is None else sums + square
                f[b, r, pick, :] = weighed
            mom[e] = mom[e] + sums

        one_pass(lay, b, PASSES - 1, finish)

        @pl.when(e < STAGES - 1)
        def _():
            emit(lay, 1 - par, b)

        @pl.when(jnp.logical_not(odd))
        def _():
            lane_all = iota((wide, lanes), 1)
            for a in range(lay.packs):
                first = PASSES + groups * a
                square = f[b, first : first + groups, own_cols].reshape(lanes, lanes).T
                pieces = [square[wide * g : wide * g + wide] for g in range(groups)]
                half = groups // 2
                while half:
                    move = half * wide
                    low = lane_all // move % 2 == 0
                    for g in range(groups):
                        if g // half % 2 == 0:
                            one, two = pieces[g], pieces[g + half]
                            pieces[g] = jnp.where(low, one, pltpu.roll(two, move, 1))
                            pieces[g + half] = jnp.where(
                                low, pltpu.roll(one, lanes - move, 1), two
                            )
                    half //= 2
                for i in range(groups):
                    begin = (lay.first + b * wide) * rows + groups * a + i
                    v_out[lax.div(e, 2), pl.ds(begin, wide, stride=rows), :] = pieces[i]

    def send_sum(k, carry):
        sum_copy(k).start()
        return carry

    def stage(e, carry):
        for lay in layouts:

            def block(b, carry, lay=lay):
                step(lay, e, b)
                if lay is layouts[0]:

                    @pl.when((e == STAGES - 1) & (b == 0))
                    def _():
                        pair_copy().wait()
                        red[...] = red[...] + red_pair[...]
                        lax.fori_loop(1, kin, send_sum, 0)

                return carry

            lax.fori_loop(0, lay.blocks, block, 0)
        @pl.when(e == STAGES - 2)
        def _():
            for i in range(4):
                red[i : i + 1, :] = jnp.sum(mom[i], 0, keepdims=True)
            pair_copy().start()

        return carry

    lax.fori_loop(0, STAGES, stage, 0)

    total_copy = remote(red_all, red_all, sum_send.at[1], sum_recv.at[1], at(1, 0))
    total_copy.wait_recv()
    total_copy.wait_send()
    sums = jnp.sum(red[...] + jnp.sum(red_all[...], 0), 1, keepdims=True)
    m0 = sums[0:1]
    x, y, z = sums[1:2] / m0, sums[2:3] / m0, sums[3:4] / m0
    alpha = 1.0 / (1.0 + x)
    beta = (y - x * x) * alpha * alpha
    c0, c1 = 1.0 - alpha + beta, -alpha
    curve = c0 * c0 * (1.0 + x) + 2.0 * c0 * c1 * (x + y) + c1 * c1 * (y + z)
    second = beta / curve
    values = (
        alpha + second * c0,
        second * c1,
        (1.0 - second) * (1.0 - alpha) - second * beta,
        -(1.0 - second) * alpha - second * c0,
        alpha * second,
    )
    for i, value in enumerate(values):
        c_out[i : i + 1, :] = jnp.broadcast_to(value, (1, lanes))


def combine_kernel(block, v, c, increment, residual, held, sems):
    size, lanes = increment.shape
    copies = []
    for n, first in enumerate(range(0, size, block)):
        count = min(block, size - first)
        part = pl.ds(first, count)
        zero, one, two = v[0, part], v[1, part], v[2, part]
        held[0, part] = c[0:1] * zero + c[1:2] * one
        held[1, part] = c[2:3] * zero + c[3:4] * one + c[4:5] * two
        for i, target in enumerate((increment, residual)):
            copy = pltpu.make_async_copy(held.at[i, part], target.at[part], sems.at[i, n])
            copy.start()
            copies.append(copy)
    for copy in copies:
        copy.wait()


def local(
    kappa_east, kappa_north, depth, sigma, obs_precision, obs_tile, obs_col, obs_lat, innovation
):
    rows, lanes = kappa_east.shape
    total = sigma.shape[0]
    tiles, bands = lax.axis_size("lon"), lax.axis_size("lat")
    listed = obs_col.shape[0]
    cap = 2 * listed // tiles
    layouts = layouts_of(total, rows, lanes)
    channels = layouts[-1].first + layouts[-1].blocks * layouts[-1].wide
    width = -(-(-(-total // SUB) * SUB + SUB) // 128) * 128

    deep = rows + 2 * PASSES
    vmem = pl.BlockSpec(memory_space=pltpu.VMEM)
    f32 = jnp.float32
    dma = pltpu.SemaphoreType.DMA
    slots = tiles * cap
    v, c = pl.pallas_call(
        functools.partial(main_kernel, tiles, bands, cap, total),
        out_shape=[
            jax.ShapeDtypeStruct((3, channels * rows, lanes), f32),
            jax.ShapeDtypeStruct((SUB, lanes), f32),
        ],
        in_specs=[pl.BlockSpec(memory_space=pltpu.HBM)] * 9,
        out_specs=[vmem] * 2,
        scratch_shapes=[
            pltpu.VMEM((rows, lanes), jnp.int32),
            pltpu.VMEM((1, total), f32),
            pltpu.VMEM((1, total), f32),
            pltpu.VMEM((3, 1, listed), jnp.int32),
            pltpu.VMEM((total, listed), f32),
            pltpu.VMEM((3, rows, lanes), f32),
            pltpu.VMEM((width, listed), f32),
            pltpu.VMEM((SUB, -(-channels // lanes) * lanes), f32),
            pltpu.VMEM((tiles, cap + SUB, lanes), f32),
            pltpu.VMEM((tiles, cap + SUB, lanes), f32),
            pltpu.VMEM((9, 3, rows, lanes), f32),
            pltpu.VMEM((3, 3, -(-(deep + 1) // SUB) * SUB, lanes), f32),
            pltpu.VMEM((STAGES, SUB, lanes), f32),
            pltpu.VMEM((SUB, lanes), f32),
            pltpu.VMEM((SUB, lanes), f32),
            pltpu.VMEM((tiles * bands // 2 - 1, SUB, lanes), f32),
            dma((tiles - 1,)),
            dma((tiles - 1,)),
            dma((8,)),
            dma((8,)),
            dma,
            dma((9,)),
            dma((2,)),
            dma((2,)),
        ]
        + [shape for lay in layouts for shape in lay.shapes(slots)],
        compiler_params=pltpu.CompilerParams(
            collective_id=1, has_side_effects=True, vmem_limit_bytes=48 * 1024 * 1024
        ),
        name="smooth_all",
    )(
        *[
            pltpu.with_memory_space_constraint(x, pltpu.HBM)
            for x in (
                kappa_east,
                kappa_north,
                depth,
                sigma.reshape(1, total),
                obs_precision.reshape(1, total),
                obs_tile.reshape(1, listed),
                obs_col.reshape(1, listed),
                obs_lat.reshape(1, listed),
                innovation,
            )
        ]
    )

    block = 2 * SUB * rows
    pieces = -(-total * rows // block)
    increment, residual = pl.pallas_call(
        functools.partial(combine_kernel, block),
        out_shape=[jax.ShapeDtypeStruct((total * rows, lanes), f32)] * 2,
        in_specs=[vmem] * 2,
        out_specs=[pl.BlockSpec(memory_space=pl.ANY)] * 2,
        scratch_shapes=[pltpu.VMEM((2, total * rows, lanes), f32), dma((2, pieces))],
        compiler_params=pltpu.CompilerParams(vmem_limit_bytes=10 * 1024 * 1024),
        name="combine",
    )(v, c)
    shape = (total, rows, lanes)
    return increment.reshape(shape), residual.reshape(shape)


def solution(mesh):
    return jax.shard_map(
        local,
        mesh=mesh,
        in_specs=(
            P("lat", "lon"),
            P("lat", "lon"),
            P("lat", "lon"),
            P(),
            P(),
            P(("lon", "lat"), None),
            P(("lon", "lat")),
            P(("lon", "lat")),
            P(None, ("lon", "lat")),
        ),
        out_specs=(P(None, "lat", "lon"), P(None, "lat", "lon")),
        check_vma=False,
    )
```
